32 devices in a mesh: clips: 2 (over y), frames: 4 (over z), heads: 4 (over x, core).
Axes of the slice: x: 2, y: 2, z: 4, core: 2. Of those that a mesh axis runs over, the one named last changes fastest.
Arguments:
- queries: bfloat16 [3072, 3072], P(('clips', 'frames'), 'heads'), parts along dimension 0, may hold values from -25 to 25
- keys: bfloat16 [3072, 3072], P(('clips', 'frames'), 'heads'), parts along dimension 0, may hold values from -6 to 6
- values: bfloat16 [3072, 3072], P(('clips', 'frames'), 'heads'), parts along dimension 0, may hold values from -6 to 6
- grad_out: bfloat16 [3072, 3072], P(('clips', 'frames'), 'heads'), parts along dimension 0, may hold values from -6 to 6
- offsets: int32 [16, 3], P('clips'), parts along dimension 0, may hold values from -2 to 2, as said below
- spatial: int32 [16, 3, 4, 4], P('clips'), parts along dimension 0, may hold values from 0 to 1, as said below
Outputs:
- grad_queries: bfloat16 [3072, 3072], P(('clips', 'frames'), 'heads'), parts along dimension 0
- grad_keys: bfloat16 [3072, 3072], P(('clips', 'frames'), 'heads'), parts along dimension 0
- grad_values: bfloat16 [3072, 3072], P(('clips', 'frames'), 'heads'), parts along dimension 0
The draws below stay inside these ranges and needn't reach their ends.
There are 2 independent parts, one for each index of `clips`. The reference program is written for one: setup_inputs(seed, part) draws one part's arguments, and reference() takes and returns one part's arrays. A program takes and returns all parts, laid end to end along the dimension named above; each array names one. Nothing has to cross between parts.
Inputs may be any that keep to these rules, and one draw needn't show every extreme that they name: Slot 0 of every frame is offset 0; the other slots hold two different nonzero offsets. Slots whose key frame lies outside the clip see nothing. `spatial`: slot 0's diagonal blocks are always 1.
All inputs are finite; a program needn't handle non-finite values.
Results may differ from the reference program's by a relative error of at most 0.0099.
Values may be sent and summed in bfloat16 or wider, within the bound.
No kernel may reach another device: no remote copies, remote signals or barrier semaphores. Data moves between devices by JAX's collectives and lax.ppermute only.
A program may use at most 64 MiB of HBM per device.

```python
import jax
import jax.numpy as jnp
from jax import lax

HEADS = 24
HD = 128
TOK_FRAME = 192
R = 2
NSEL = 3
SB = 4
FRAMES = 8
TOKENS = 1536


def joint_draw(key):
    query_key = jax.random.fold_in(key, 101)
    key_key = jax.random.fold_in(key, 102)
    width = HEADS * HD
    query_vals = jnp.clip(jax.random.normal(query_key, (TOKENS, width), jnp.float32), -6.0, 6.0)
    key_vals = jnp.clip(jax.random.normal(key_key, (TOKENS, width), jnp.float32), -6.0, 6.0)
    return (query_vals, key_vals)


def draw_queries(key, part):
    return joint_draw(key)[0].astype(jnp.bfloat16)


def draw_keys(key, part):
    return joint_draw(key)[1].astype(jnp.bfloat16)


def draw_offsets(key, part):
    frame_keys = jax.random.split(jax.random.fold_in(key, 201), FRAMES)
    perms = jax.vmap(lambda one_key: jax.random.permutation(one_key, 2 * R))(frame_keys)[:, :NSEL - 1]
    others = jnp.where(perms < R, perms - R, perms - R + 1).astype(jnp.int32)
    table = jnp.concatenate([jnp.zeros((FRAMES, 1), jnp.int32), others], 1)
    table = table.at[0, 1].set(R).at[0, 2].set(-R)
    return table


def draw_spatial(key, part):
    level = jax.random.randint(jax.random.fold_in(key, 301), (FRAMES, 1, 1, 1), 1, SB + 1)
    picks = jax.random.randint(jax.random.fold_in(key, 302), (FRAMES, NSEL, SB, SB), 0, SB)
    blocks = (picks < level).astype(jnp.int32)
    identity = jnp.eye(SB, dtype=jnp.int32)
    return blocks.at[:, 0].set(jnp.maximum(blocks[:, 0], identity))


def steps_of(rng, dims, cuts, low, largest):
    loudness, own = 1.0, jax.random.fold_in(rng, 6)
    for dim, shards_of in cuts:
        heights = jnp.exp(jax.random.uniform(jax.random.fold_in(own, dim), (shards_of,), jnp.float32, low / len(cuts), largest / len(cuts)))
        loudness = loudness * jnp.repeat(heights, dims[dim] // shards_of).reshape([-1 if axis == dim else 1 for axis in range(len(dims))])
    return loudness


def scatter_about(rng, shape, spread, bound, pieces=(), held_as=jnp.bfloat16):
    loudness = steps_of(rng, shape, pieces, -0.22, 0.18) if pieces else 1.0
    array = jax.random.normal(rng, shape, jnp.float32) * spread * loudness
    return jnp.minimum(jnp.maximum(array, -bound), bound).astype(held_as)


def setup_inputs(seed: int = 0, part: int = 0) -> dict:
    streams_of = jax.random.split(jax.random.key(seed), 7)
    own_keys = jax.random.split(jax.random.fold_in(streams_of[6], part), 7)
    return {
        "queries": draw_queries(jax.random.fold_in(jax.random.fold_in(streams_of[6], part), 71), part),
        "keys": draw_keys(jax.random.fold_in(jax.random.fold_in(streams_of[6], part), 71), part),
        "values": scatter_about(own_keys[2], (TOKENS, HEADS * HD), 1.0, 6.0, ((0, 4), (1, 4))),
        "grad_out": scatter_about(own_keys[3], (TOKENS, HEADS * HD), 1.0, 6.0, ((0, 4), (1, 4))),
        "offsets": draw_offsets(jax.random.fold_in(jax.random.fold_in(streams_of[6], part), 71), part),
        "spatial": draw_spatial(jax.random.fold_in(jax.random.fold_in(streams_of[6], part), 71), part),
    }


def span_mask(block_mask, inside, block_rows):
    masked = block_mask * inside[:, None, None]
    tokens = jnp.repeat(jnp.repeat(masked, block_rows, axis=1), block_rows, axis=2)
    return jnp.transpose(tokens, (1, 0, 2)).reshape(tokens.shape[1], -1) > 0


def add_frame(accum, piece, where_at):
    current = lax.dynamic_index_in_dim(accum, where_at, 0, False)
    return lax.dynamic_update_index_in_dim(accum, current + piece, where_at, 0)


def reference(queries, keys, values, grad_out, offsets, spatial):
    scaling = HD ** -0.5
    block_rows = TOK_FRAME // SB
    shape_four = (FRAMES, TOK_FRAME, HEADS, HD)
    query_all = queries.reshape(shape_four)
    grad_all = grad_out.reshape(shape_four)
    padding = ((R, R), (0, 0), (0, 0), (0, 0))
    key_all = jnp.pad(keys.reshape(shape_four), padding)
    value_all = jnp.pad(values.reshape(shape_four), padding)
    zeros_acc = jnp.zeros((FRAMES + 2 * R, TOK_FRAME, HEADS, HD), jnp.float32)

    def per_frame(carry, frame):
        key_acc, value_acc = carry
        shifts = lax.dynamic_index_in_dim(offsets, frame, 0, False)
        spots = (frame + R + shifts).astype(jnp.int32)
        key_rows = jnp.concatenate([lax.dynamic_index_in_dim(key_all, spots[slot], 0, False) for slot in range(NSEL)], 0).astype(jnp.float32)
        value_rows = jnp.concatenate([lax.dynamic_index_in_dim(value_all, spots[slot], 0, False) for slot in range(NSEL)], 0).astype(jnp.float32)
        query_rows = lax.dynamic_index_in_dim(query_all, frame, 0, False).astype(jnp.float32)
        grad_rows = lax.dynamic_index_in_dim(grad_all, frame, 0, False).astype(jnp.float32)
        inside = ((frame + shifts >= 0) & (frame + shifts < FRAMES)).astype(jnp.int32)
        allowed = span_mask(lax.dynamic_index_in_dim(spatial, frame, 0, False), inside, block_rows)
        scores = jnp.einsum("qhd,khd->hqk", query_rows, key_rows) * scaling
        masked = jnp.where(allowed[None], scores, -1e30)
        highest = jnp.max(masked, -1, keepdims=True)
        log_total = highest + jnp.log(jnp.sum(jnp.exp(masked - highest), -1, keepdims=True))
        attn_prob = jnp.exp(masked - log_total)
        prob_low = lax.optimization_barrier(attn_prob.astype(jnp.bfloat16)).astype(jnp.float32)
        attended = jnp.einsum("hqk,khd->qhd", prob_low, value_rows)
        row_delta = jnp.transpose(jnp.sum(grad_rows * attended, -1))
        grad_prob = jnp.einsum("qhd,khd->hqk", grad_rows, value_rows)
        grad_score = attn_prob * (grad_prob - row_delta[..., None])
        score_low = lax.optimization_barrier(grad_score.astype(jnp.bfloat16)).astype(jnp.float32)
        grad_query = jnp.einsum("hqk,khd->qhd", score_low, key_rows) * scaling
        key_part = (jnp.einsum("hqk,qhd->khd", score_low, query_rows) * scaling).reshape(NSEL, TOK_FRAME, HEADS, HD)
        value_part = jnp.einsum("hqk,qhd->khd", prob_low, grad_rows).reshape(NSEL, TOK_FRAME, HEADS, HD)
        for slot in range(NSEL):
            key_acc = add_frame(key_acc, key_part[slot], spots[slot])
            value_acc = add_frame(value_acc, value_part[slot], spots[slot])
        return (key_acc, value_acc), grad_query.astype(jnp.bfloat16)

    (key_acc, value_acc), grad_query = lax.scan(per_frame, (zeros_acc, zeros_acc), jnp.arange(FRAMES, dtype=jnp.int32))
    width = HEADS * HD
    grad_queries = grad_query.reshape(TOKENS, width)
    grad_keys = key_acc[R:R + FRAMES].reshape(TOKENS, width).astype(jnp.bfloat16)
    grad_values = value_acc[R:R + FRAMES].reshape(TOKENS, width).astype(jnp.bfloat16)
    return grad_queries, grad_keys, grad_values
```

```python
import functools
import math

import jax
import jax.numpy as jnp
from jax import lax
from jax.experimental import pallas as pl
from jax.experimental.pallas import tpu as pltpu
from jax.sharding import PartitionSpec as P

HD = 128
TOK_FRAME = 192
FR_DEV = 2
NSEL = 3
SB = 4
ROWS = FR_DEV * TOK_FRAME
BLOCK = TOK_FRAME // SB
SCALE = HD ** (-0.5)
SCALE2 = SCALE * math.log2(math.e)
NEG = -1e30
NT = (((1,), (1,)), ((), ()))
NN = (((1,), (0,)), ((), ()))
TN = (((0,), (0,)), ((), ()))


def dot(lhs, rhs, dims):
    return lax.dot_general(lhs, rhs, dims, preferred_element_type=jnp.float32)


def fill_bias(table, bias):
    q_block = lax.broadcasted_iota(jnp.int32, (BLOCK, TOK_FRAME), 1) // BLOCK
    for frame in range(FR_DEV):
        for slot in range(NSEL):
            for k_block in range(SB):
                value = jnp.zeros((BLOCK, TOK_FRAME), jnp.float32)
                for block in range(SB):
                    at = FR_DEV * NSEL + ((frame * NSEL + slot) * SB + block) * SB + k_block
                    drop = jnp.where(table[at] > 0, 0.0, NEG)
                    value = jnp.where(q_block == block, drop, value)
                bias[frame, pl.ds(slot * TOK_FRAME + k_block * BLOCK, BLOCK), :] = value


def fill_window(window, one, own, two):
    window[0:ROWS] = one[...]
    window[ROWS : 2 * ROWS] = own[...]
    window[2 * ROWS : 3 * ROWS] = two[...]


def span(table, frame, slot):
    return pl.ds(pl.multiple_of(table[frame * NSEL + slot] * TOK_FRAME, TOK_FRAME), TOK_FRAME)


def values_kernel(
    table, queries, grad_out, k_one, k_own, k_two, log_out, own_out, one_out, two_out,
    bias, window, accum,
):
    @pl.when(pl.program_id(0) == 0)
    def _():
        fill_bias(table, bias)

    fill_window(window, k_one, k_own, k_two)
    accum[...] = jnp.zeros_like(accum)
    for frame in range(FR_DEV):
        rows = pl.ds(frame * TOK_FRAME, TOK_FRAME)
        query = queries[rows, :]
        grad = grad_out[rows, :]
        masked = []
        for slot in range(NSEL):
            scores = dot(window[span(table, frame, slot), :], query, NT)
            masked.append(
                scores * SCALE2 + bias[frame, pl.ds(slot * TOK_FRAME, TOK_FRAME), :]
            )
        highest = functools.reduce(
            jnp.maximum, [jnp.max(each, 0, keepdims=True) for each in masked]
        )
        raised = [jnp.exp2(each - highest) for each in masked]
        total = functools.reduce(jnp.add, [jnp.sum(each, 0, keepdims=True) for each in raised])
        log_out[0, frame : frame + 1, :] = highest + jnp.log2(total)
        inverse = 1.0 / total
        for slot in range(NSEL):
            prob_low = (raised[slot] * inverse).astype(jnp.bfloat16)
            accum[span(table, frame, slot), :] += dot(prob_low, grad, NN)
    one_out[...] = accum[0:ROWS].astype(one_out.dtype)
    own_out[...] = accum[ROWS : 2 * ROWS].astype(own_out.dtype)
    two_out[...] = accum[2 * ROWS : 3 * ROWS].astype(two_out.dtype)


def keys_kernel(
    table, queries, grad_out, k_one, k_own, k_two, v_one, v_own, v_two, log_in,
    query_out, own_out, one_out, two_out,
    bias, window, v_window, accum,
):
    @pl.when(pl.program_id(0) == 0)
    def _():
        fill_bias(table, bias)

    fill_window(window, k_one, k_own, k_two)
    fill_window(v_window, v_one, v_own, v_two)
    accum[...] = jnp.zeros_like(accum)
    for frame in range(FR_DEV):
        rows = pl.ds(frame * TOK_FRAME, TOK_FRAME)
        query = queries[rows, :]
        grad = grad_out[rows, :]
        log_total = log_in[0, frame : frame + 1, :]
        probs = []
        grads = []
        delta = jnp.zeros((1, TOK_FRAME), jnp.float32)
        for slot in range(NSEL):
            where_at = span(table, frame, slot)
            scores = dot(window[where_at, :], query, NT)
            prob = jnp.exp2(
                scores * SCALE2
                + bias[frame, pl.ds(slot * TOK_FRAME, TOK_FRAME), :]
                - log_total
            )
            grad_prob = dot(v_window[where_at, :], grad, NT)
            low = prob.astype(jnp.bfloat16).astype(jnp.float32)
            delta += jnp.sum(low * grad_prob, 0, keepdims=True)
            probs.append(prob)
            grads.append(grad_prob)
        grad_query = jnp.zeros((TOK_FRAME, HD), jnp.float32)
        for slot in range(NSEL):
            where_at = span(table, frame, slot)
            score_low = (probs[slot] * (grads[slot] - delta)).astype(jnp.bfloat16)
            accum[where_at, :] += dot(score_low, query, NN)
            grad_query += dot(score_low, window[where_at, :], TN)
        query_out[rows, :] = (grad_query * SCALE).astype(query_out.dtype)
    one_out[...] = (accum[0:ROWS] * SCALE).astype(one_out.dtype)
    own_out[...] = (accum[ROWS : 2 * ROWS] * SCALE).astype(own_out.dtype)
    two_out[...] = (accum[2 * ROWS : 3 * ROWS] * SCALE).astype(two_out.dtype)


def exchanges(count):
    first = [(i, i + 1) for i in range(0, count - 1, 2)]
    second = [(i, i + 1) for i in range(1, count - 1, 2)]
    return tuple([pair for i, j in part for pair in ((i, j), (j, i))] for part in (first, second))


def swap(one, two):
    first, second = exchanges(lax.axis_size("frames"))
    return lax.ppermute(one, "frames", first), lax.ppermute(two, "frames", second)


def lookup(offsets, spatial):
    me = lax.axis_index("frames")
    first_frame = me * FR_DEV
    shifts = lax.dynamic_slice_in_dim(offsets, first_frame, FR_DEV, 0)
    blocks = lax.dynamic_slice_in_dim(spatial, first_frame, FR_DEV, 0)
    place = jnp.arange(FR_DEV, dtype=jnp.int32)[:, None] + shifts
    target = first_frame + place
    inside = ((target >= 0) & (target < offsets.shape[0])).astype(jnp.int32)
    side = (place >= 0).astype(jnp.int32) + (place >= FR_DEV).astype(jnp.int32)
    side = jnp.where(me % 2 == 1, side, 2 - side)
    spot = side * FR_DEV + (place % FR_DEV)
    blocks = blocks * inside[:, :, None, None]
    return jnp.concatenate([spot.reshape(-1), blocks.reshape(-1)]).astype(jnp.int32)


def local(queries, keys, values, grad_out, offsets, spatial):
    heads = queries.shape[1] // HD
    k_one, k_two = swap(keys, keys)
    v_one, v_two = swap(values, values)
    table = lookup(offsets, spatial)
    column = pl.BlockSpec((ROWS, HD), lambda head, _: (0, head))
    stat = pl.BlockSpec((1, FR_DEV, TOK_FRAME), lambda head, _: (head, 0, 0))
    low = jax.ShapeDtypeStruct(queries.shape, jnp.bfloat16)
    full = jax.ShapeDtypeStruct(queries.shape, jnp.float32)
    logs = jax.ShapeDtypeStruct((heads, FR_DEV, TOK_FRAME), jnp.float32)
    bias = pltpu.VMEM((FR_DEV, NSEL * TOK_FRAME, TOK_FRAME), jnp.float32)
    window = pltpu.VMEM((3 * ROWS, HD), jnp.bfloat16)
    accum = pltpu.VMEM((3 * ROWS, HD), jnp.float32)
    flops = 2 * heads * FR_DEV * NSEL * TOK_FRAME * TOK_FRAME * HD
    size = queries.size * 2
    log_total, gv_own, gv_one, gv_two = pl.pallas_call(
        values_kernel,
        out_shape=(logs, full, low, low),
        grid_spec=pltpu.PrefetchScalarGridSpec(
            num_scalar_prefetch=1,
            grid=(heads,),
            in_specs=[column] * 5,
            out_specs=(stat, column, column, column),
            scratch_shapes=[bias, window, accum],
        ),
        compiler_params=pltpu.CompilerParams(vmem_limit_bytes=24 << 20),
        cost_estimate=pl.CostEstimate(
            flops=2 * flops, bytes_accessed=9 * size, transcendentals=0
        ),
        name="values_part",
    )(table, queries, grad_out, k_one, keys, k_two)
    rv_one, rv_two = swap(gv_one, gv_two)
    grad_queries, gk_own, gk_one, gk_two = pl.pallas_call(
        keys_kernel,
        out_shape=(low, full, low, low),
        grid_spec=pltpu.PrefetchScalarGridSpec(
            num_scalar_prefetch=1,
            grid=(heads,),
            in_specs=[column] * 8 + [stat],
            out_specs=(column, column, column, column),
            scratch_shapes=[bias, window, window, accum],
        ),
        compiler_params=pltpu.CompilerParams(vmem_limit_bytes=24 << 20),
        cost_estimate=pl.CostEstimate(
            flops=4 * flops, bytes_accessed=13 * size, transcendentals=0
        ),
        name="keys_part",
    )(table, queries, grad_out, k_one, keys, k_two, v_one, values, v_two, log_total)
    rk_one, rk_two = swap(gk_one, gk_two)

    def joined(own, one, two):
        return (own + one.astype(jnp.float32) + two.astype(jnp.float32)).astype(jnp.bfloat16)

    return (grad_queries, joined(gk_own, rk_one, rk_two), joined(gv_own, rv_one, rv_two))


def solution(mesh):
    rows = P(("clips", "frames"), "heads")
    return jax.shard_map(
        local,
        mesh=mesh,
        in_specs=(rows, rows, rows, rows, P("clips", None), P("clips", None, None, None)),
        out_specs=(rows, rows, rows),
        check_vma=False,
    )
```

```python
import math

import jax
import jax.numpy as jnp
from jax import lax
from jax.experimental import pallas as pl
from jax.experimental.pallas import tpu as pltpu
from jax.sharding import PartitionSpec as P

HD = 128
TOK_FRAME = 192
FR_DEV = 2
NSEL = 3
SB = 4
GROUP = 3
ROWS = FR_DEV * TOK_FRAME
BLOCK = TOK_FRAME // SB
SCALE = HD ** (-0.5)
SCALE2 = SCALE * math.log2(math.e)
NEG = -1e30
NT = (((1,), (1,)), ((), ()))
NN = (((1,), (0,)), ((), ()))
TN = (((0,), (0,)), ((), ()))


def dot(lhs, rhs, dims):
    return lax.dot_general(lhs, rhs, dims, preferred_element_type=jnp.float32)


def fill_bias(table, bias):
    q_block = lax.broadcasted_iota(jnp.int32, (BLOCK, TOK_FRAME), 1) // BLOCK
    for frame in range(FR_DEV):
        for slot in range(NSEL):
            for k_block in range(SB):
                value = jnp.zeros((BLOCK, TOK_FRAME), jnp.float32)
                for block in range(SB):
                    at = FR_DEV * NSEL + ((frame * NSEL + slot) * SB + block) * SB + k_block
                    drop = jnp.where(table[at] > 0, 0.0, NEG)
                    value = jnp.where(q_block == block, drop, value)
                bias[frame, pl.ds(slot * TOK_FRAME + k_block * BLOCK, BLOCK), :] = value


def fill_window(window, one, own, two, column):
    window[0:ROWS] = one[:, column]
    window[ROWS : 2 * ROWS] = own[:, column]
    window[2 * ROWS : 3 * ROWS] = two[:, column]


def span(table, frame, slot):
    return pl.ds(pl.multiple_of(table[frame * NSEL + slot] * TOK_FRAME, TOK_FRAME), TOK_FRAME)


def pick(table, frame, window, chosen):
    for slot in range(NSEL):
        chosen[slot * TOK_FRAME : (slot + 1) * TOK_FRAME] = window[span(table, frame, slot), :]


def spread(table, frame, accum, parts):
    for slot in range(NSEL):
        accum[span(table, frame, slot), :] += parts[slot * TOK_FRAME : (slot + 1) * TOK_FRAME]


def values_kernel(
    table, queries, grad_out, k_one, k_own, k_two, prob_out, own_out, one_out, two_out,
    bias, windows, choices, accums,
):
    @pl.when(pl.program_id(0) == 0)
    def _():
        fill_bias(table, bias)

    for head in range(GROUP):
        column = slice(head * HD, (head + 1) * HD)
        window = windows.at[head]
        accum = accums.at[head]
        fill_window(window, k_one, k_own, k_two, column)
        accum[...] = jnp.zeros_like(accum)
        for frame in range(FR_DEV):
            rows = slice(frame * TOK_FRAME, (frame + 1) * TOK_FRAME)
            chosen = choices.at[head, frame]
            pick(table, frame, window, chosen)
            scores = dot(chosen[...], queries[rows, column], NT)
            masked = scores * SCALE2 + bias[frame]
            raised = jnp.exp2(masked - jnp.max(masked, 0, keepdims=True))
            inverse = 1.0 / jnp.sum(raised, 0, keepdims=True)
            prob_low = (raised * inverse).astype(jnp.bfloat16)
            prob_out[head, frame] = prob_low
            spread(table, frame, accum, dot(prob_low, grad_out[rows, column], NN))
        one_out[:, column] = accum[0:ROWS].astype(one_out.dtype)
        own_out[:, column] = accum[ROWS : 2 * ROWS].astype(own_out.dtype)
        two_out[:, column] = accum[2 * ROWS : 3 * ROWS].astype(two_out.dtype)


def keys_kernel(
    table, queries, grad_out, k_one, k_own, k_two, v_one, v_own, v_two, prob_in,
    query_out, own_out, one_out, two_out,
    windows, v_windows, choices, v_choices, accums,
):
    for head in range(GROUP):
        column = slice(head * HD, (head + 1) * HD)
        window = windows.at[head]
        v_window = v_windows.at[head]
        accum = accums.at[head]
        fill_window(window, k_one, k_own, k_two, column)
        fill_window(v_window, v_one, v_own, v_two, column)
        accum[...] = jnp.zeros_like(accum)
        for frame in range(FR_DEV):
            rows = slice(frame * TOK_FRAME, (frame + 1) * TOK_FRAME)
            chosen = choices.at[head, frame]
            v_chosen = v_choices.at[head, frame]
            pick(table, frame, window, chosen)
            pick(table, frame, v_window, v_chosen)
            grad_prob = dot(v_chosen[...], grad_out[rows, column], NT)
            prob = prob_in[head, frame].astype(jnp.float32)
            delta = jnp.sum(prob * grad_prob, 0, keepdims=True)
            score_low = (prob * (grad_prob - delta)).astype(jnp.bfloat16)
            spread(table, frame, accum, dot(score_low, queries[rows, column], NN))
            grad_query = dot(score_low, chosen[...], TN)
            query_out[rows, column] = (grad_query * SCALE).astype(query_out.dtype)
        one_out[:, column] = (accum[0:ROWS] * SCALE).astype(one_out.dtype)
        own_out[:, column] = (accum[ROWS : 2 * ROWS] * SCALE).astype(own_out.dtype)
        two_out[:, column] = (accum[2 * ROWS : 3 * ROWS] * SCALE).astype(two_out.dtype)


def exchanges(count):
    first = [(i, i + 1) for i in range(0, count - 1, 2)]
    second = [(i, i + 1) for i in range(1, count - 1, 2)]
    return tuple([pair for i, j in part for pair in ((i, j), (j, i))] for part in (first, second))


def swap(one, two):
    first, second = exchanges(lax.axis_size("frames"))
    return lax.ppermute(one, "frames", first), lax.ppermute(two, "frames", second)


def lookup(offsets, spatial):
    me = lax.axis_index("frames")
    first_frame = me * FR_DEV
    shifts = lax.dynamic_slice_in_dim(offsets, first_frame, FR_DEV, 0)
    blocks = lax.dynamic_slice_in_dim(spatial, first_frame, FR_DEV, 0)
    place = jnp.arange(FR_DEV, dtype=jnp.int32)[:, None] + shifts
    target = first_frame + place
    inside = ((target >= 0) & (target < offsets.shape[0])).astype(jnp.int32)
    side = (place >= 0).astype(jnp.int32) + (place >= FR_DEV).astype(jnp.int32)
    side = jnp.where(me % 2 == 1, side, 2 - side)
    spot = side * FR_DEV + (place % FR_DEV)
    blocks = blocks * inside[:, :, None, None]
    return jnp.concatenate([spot.reshape(-1), blocks.reshape(-1)]).astype(jnp.int32)


def local(queries, keys, values, grad_out, offsets, spatial):
    heads = queries.shape[1] // HD
    k_one, k_two = swap(keys, keys)
    v_one, v_two = swap(values, values)
    table = lookup(offsets, spatial)
    column = pl.BlockSpec((ROWS, GROUP * HD), lambda step, _: (0, step))
    slots = NSEL * TOK_FRAME
    chance = pl.BlockSpec(
        (GROUP, FR_DEV, slots, TOK_FRAME), lambda step, _: (step, 0, 0, 0)
    )
    low = jax.ShapeDtypeStruct(queries.shape, jnp.bfloat16)
    full = jax.ShapeDtypeStruct(queries.shape, jnp.float32)
    chances = jax.ShapeDtypeStruct((heads, FR_DEV, slots, TOK_FRAME), jnp.bfloat16)
    bias = pltpu.VMEM((FR_DEV, slots, TOK_FRAME), jnp.float32)
    window = pltpu.VMEM((GROUP, 3 * ROWS, HD), jnp.bfloat16)
    choice = pltpu.VMEM((GROUP, FR_DEV, slots, HD), jnp.bfloat16)
    accum = pltpu.VMEM((GROUP, 3 * ROWS, HD), jnp.float32)
    params = pltpu.CompilerParams(vmem_limit_bytes=56 << 20)
    flops = 2 * heads * FR_DEV * NSEL * TOK_FRAME * TOK_FRAME * HD
    size = queries.size * 2
    prob_low, gv_own, gv_one, gv_two = pl.pallas_call(
        values_kernel,
        out_shape=(chances, full, low, low),
        grid_spec=pltpu.PrefetchScalarGridSpec(
            num_scalar_prefetch=1,
            grid=(heads // GROUP,),
            in_specs=[column] * 5,
            out_specs=(chance, column, column, column),
            scratch_shapes=[bias, window, choice, accum],
        ),
        compiler_params=params,
        cost_estimate=pl.CostEstimate(
            flops=2 * flops, bytes_accessed=14 * size, transcendentals=0
        ),
        name="values_part",
    )(table, queries, grad_out, k_one, keys, k_two)
    rv_one, rv_two = swap(gv_one, gv_two)
    grad_queries, gk_own, gk_one, gk_two = pl.pallas_call(
        keys_kernel,
        out_shape=(low, full, low, low),
        grid_spec=pltpu.PrefetchScalarGridSpec(
            num_scalar_prefetch=1,
            grid=(heads // GROUP,),
            in_specs=[column] * 8 + [chance],
            out_specs=(column, column, column, column),
            scratch_shapes=[window, window, choice, choice, accum],
        ),
        compiler_params=params,
        cost_estimate=pl.CostEstimate(
            flops=3 * flops, bytes_accessed=18 * size, transcendentals=0
        ),
        name="keys_part",
    )(table, queries, grad_out, k_one, keys, k_two, v_one, values, v_two, prob_low)
    rk_one, rk_two = swap(gk_one, gk_two)

    def joined(own, one, two):
        return (own + one.astype(jnp.float32) + two.astype(jnp.float32)).astype(jnp.bfloat16)

    return (grad_queries, joined(gk_own, rk_one, rk_two), joined(gv_own, rv_one, rv_two))


def solution(mesh):
    rows = P(("clips", "frames"), "heads")
    return jax.shard_map(
        local,
        mesh=mesh,
        in_specs=(rows, rows, rows, rows, P("clips", None), P("clips", None, None, None)),
        out_specs=(rows, rows, rows),
        check_vma=False,
    )
```

```python
import math

import jax
import jax.numpy as jnp
from jax import lax
from jax.experimental import pallas as pl
from jax.experimental.pallas import tpu as pltpu
from jax.sharding import PartitionSpec as P

HD = 128
TOK_FRAME = 192
FR_DEV = 2
NSEL = 3
SB = 4
DEPTH = 3
ROWS = FR_DEV * TOK_FRAME
BLOCK = TOK_FRAME // SB
SCALE = HD ** (-0.5)
SCALE2 = SCALE * math.log2(math.e)
NEG = -1e30
NT = (((1,), (1,)), ((), ()))
NN = (((1,), (0,)), ((), ()))
TN = (((0,), (0,)), ((), ()))


def dot(lhs, rhs, dims):
    return lax.dot_general(lhs, rhs, dims, preferred_element_type=jnp.float32)


def column_of(head):
    return slice(head * HD, (head + 1) * HD)


def rows_of(frame):
    return slice(frame * TOK_FRAME, (frame + 1) * TOK_FRAME)


def span(table, frame, slot):
    return pl.ds(pl.multiple_of(table[frame * NSEL + slot] * TOK_FRAME, TOK_FRAME), TOK_FRAME)


def fill_bias(table, bias):
    q_block = lax.broadcasted_iota(jnp.int32, (8, TOK_FRAME), 1) // BLOCK
    for frame in range(FR_DEV):
        for slot in range(NSEL):
            for k_block in range(SB):
                value = jnp.zeros((8, TOK_FRAME), jnp.float32)
                for block in range(SB):
                    at = FR_DEV * NSEL + ((frame * NSEL + slot) * SB + block) * SB + k_block
                    drop = jnp.where(table[at] > 0, 0.0, NEG)
                    value = jnp.where(q_block == block, drop, value)
                for step in range(0, BLOCK, 8):
                    bias[frame, pl.ds(slot * TOK_FRAME + k_block * BLOCK + step, 8), :] = value


def fill_window(window, one, own, two, column):
    window[0:ROWS] = one[:, column]
    window[ROWS : 2 * ROWS] = own[:, column]
    window[2 * ROWS : 3 * ROWS] = two[:, column]


def pick(table, frame, window, chosen):
    for slot in range(NSEL):
        chosen[rows_of(slot)] = window[span(table, frame, slot), :]


def spread(table, frame, accum, parts):
    for slot in range(1, NSEL):
        accum[span(table, frame, slot), :] += parts[rows_of(slot - 1)]


def stage_kernel(table, *refs):
    arrays, copies, bias, sems = refs[:4], refs[4:8], refs[8], refs[9]
    moves = [
        pltpu.make_async_copy(array, copy, sems.at[i])
        for i, (array, copy) in enumerate(zip(arrays, copies))
    ]
    for move in moves:
        move.start()
    fill_bias(table, bias)
    for move in moves:
        move.wait()


def values_kernel(
    table, queries, grad_out, k_own, bias, k_one, k_two,
    chosen_out, prob_out, own_out, one_out, two_out,
    windows, accums,
):
    for head in range(queries.shape[1] // HD):
        column = column_of(head)
        window = windows.at[head % DEPTH]
        accum = accums.at[head % DEPTH]
        fill_window(window, k_one, k_own, k_two, column)
        accum[...] = jnp.zeros_like(accum)
        for frame in range(FR_DEV):
            chosen = chosen_out.at[head, frame]
            pick(table, frame, window, chosen)
            scores = dot(chosen[...], queries[rows_of(frame), column], NT)
            masked = scores * SCALE2 + bias[frame]
            raised = jnp.exp2(masked - jnp.max(masked, 0, keepdims=True))
            inverse = 1.0 / jnp.sum(raised, 0, keepdims=True)
            prob_low = (raised * inverse).astype(jnp.bfloat16)
            prob_out[head, frame] = prob_low
            far = dot(prob_low[TOK_FRAME:], grad_out[rows_of(frame), column], NN)
            spread(table, frame, accum, far)
        one_out[:, column] = accum[0:ROWS].astype(one_out.dtype)
        own_out[:, column] = accum[ROWS : 2 * ROWS]
        two_out[:, column] = accum[2 * ROWS : 3 * ROWS].astype(two_out.dtype)


def keys_kernel(
    table, queries, grad_out, v_own, prob_in, v_one, v_two,
    score_out, own_out, one_out, two_out,
    windows, choices, accums,
):
    for head in range(queries.shape[1] // HD):
        column = column_of(head)
        window = windows.at[head % DEPTH]
        accum = accums.at[head % DEPTH]
        fill_window(window, v_one, v_own, v_two, column)
        accum[...] = jnp.zeros_like(accum)
        for frame in range(FR_DEV):
            chosen = choices.at[head % DEPTH, frame]
            pick(table, frame, window, chosen)
            grad_prob = dot(chosen[...], grad_out[rows_of(frame), column], NT)
            prob = prob_in[head, frame].astype(jnp.float32)
            delta = jnp.sum(prob * grad_prob, 0, keepdims=True)
            score_low = (prob * (grad_prob - delta)).astype(jnp.bfloat16)
            score_out[head, frame] = score_low
            far = dot(score_low[TOK_FRAME:], queries[rows_of(frame), column], NN)
            spread(table, frame, accum, far)
        one_out[:, column] = (accum[0:ROWS] * SCALE).astype(one_out.dtype)
        own_out[:, column] = accum[ROWS : 2 * ROWS]
        two_out[:, column] = (accum[2 * ROWS : 3 * ROWS] * SCALE).astype(two_out.dtype)


def rest_kernel(
    queries, grad_out, chosen_in, prob_in, score_in, gv_own, gk_own, rv_one, rv_two,
    query_out, value_out, key_out,
):
    for head in range(queries.shape[1] // HD):
        column = column_of(head)
        for frame in range(FR_DEV):
            rows = rows_of(frame)
            score_low = score_in[head, frame]
            grad_query = dot(score_low, chosen_in[head, frame], TN)
            query_out[rows, column] = (grad_query * SCALE).astype(query_out.dtype)
            near = dot(score_low[:TOK_FRAME], queries[rows, column], NN)
            key_out[rows, column] = (gk_own[rows, column] + near) * SCALE
            near = dot(prob_in[head, frame, :TOK_FRAME], grad_out[rows, column], NN)
            total = gv_own[rows, column] + near
            total += rv_one[rows, column].astype(jnp.float32)
            total += rv_two[rows, column].astype(jnp.float32)
            value_out[rows, column] = total.astype(value_out.dtype)


def exchanges(count):
    first = [(i, i + 1) for i in range(0, count - 1, 2)]
    second = [(i, i + 1) for i in range(1, count - 1, 2)]
    return tuple([pair for i, j in part for pair in ((i, j), (j, i))] for part in (first, second))


def swap(one, two):
    first, second = exchanges(lax.axis_size("frames"))
    return lax.ppermute(one, "frames", first), lax.ppermute(two, "frames", second)


def lookup(offsets, spatial):
    me = lax.axis_index("frames")
    first_frame = me * FR_DEV
    shifts = lax.dynamic_slice_in_dim(offsets, first_frame, FR_DEV, 0)
    blocks = lax.dynamic_slice_in_dim(spatial, first_frame, FR_DEV, 0)
    place = jnp.arange(FR_DEV, dtype=jnp.int32)[:, None] + shifts
    target = first_frame + place
    inside = ((target >= 0) & (target < offsets.shape[0])).astype(jnp.int32)
    side = (place >= 0).astype(jnp.int32) + (place >= FR_DEV).astype(jnp.int32)
    side = jnp.where(me % 2 == 1, side, 2 - side)
    spot = side * FR_DEV + (place % FR_DEV)
    blocks = blocks * inside[:, :, None, None]
    return jnp.concatenate([spot.reshape(-1), blocks.reshape(-1)]).astype(jnp.int32)


def call(kernel, name, scalars, arrays, outs, scratch, flops, space=pltpu.VMEM):
    if space is pltpu.VMEM:
        arrays = [pltpu.with_memory_space_constraint(array, space) for array in arrays]
    return pl.pallas_call(
        kernel,
        out_shape=outs,
        in_specs=[pl.BlockSpec(memory_space=pltpu.SMEM)] * len(scalars)
        + [pl.BlockSpec(memory_space=space)] * len(arrays),
        out_specs=tuple(pl.BlockSpec(memory_space=pltpu.VMEM) for _ in outs),
        scratch_shapes=scratch,
        compiler_params=pltpu.CompilerParams(vmem_limit_bytes=16 << 20),
        cost_estimate=pl.CostEstimate(flops=flops, bytes_accessed=0, transcendentals=0),
        name=name,
    )(*scalars, *arrays)


def local(queries, keys, values, grad_out, offsets, spatial):
    heads = queries.shape[1] // HD
    k_one, k_two = swap(keys, keys)
    v_one, v_two = swap(values, values)
    table = lookup(offsets, spatial)
    shape = queries.shape
    slots = NSEL * TOK_FRAME
    low = pltpu.VMEM(shape, jnp.bfloat16)
    full = pltpu.VMEM(shape, jnp.float32)
    pairs = pltpu.VMEM((heads, FR_DEV, slots, TOK_FRAME), jnp.bfloat16)
    choices = pltpu.VMEM((heads, FR_DEV, slots, HD), jnp.bfloat16)
    biases = pltpu.VMEM((FR_DEV, slots, TOK_FRAME), jnp.float32)
    windows = pltpu.VMEM((DEPTH, 3 * ROWS, HD), jnp.bfloat16)
    accums = pltpu.VMEM((DEPTH, 3 * ROWS, HD), jnp.float32)
    flops = 2 * heads * FR_DEV * NSEL * TOK_FRAME * TOK_FRAME * HD
    staged = call(
        stage_kernel, "stage", (table,), (queries, grad_out, keys, values),
        (low, low, low, low, biases), [pltpu.SemaphoreType.DMA((4,))], flops // 2, pl.ANY,
    )
    query, grad, key, value, bias = staged
    chosen, prob_low, gv_own, gv_one, gv_two = call(
        values_kernel, "values_part", (table,), (query, grad, key, bias, k_one, k_two),
        (choices, pairs, full, low, low), [windows, accums], 2 * flops,
    )
    rv_one, rv_two = swap(gv_one, gv_two)
    score_low, gk_own, gk_one, gk_two = call(
        keys_kernel, "keys_part", (table,), (query, grad, value, prob_low, v_one, v_two),
        (pairs, full, low, low),
        [windows, pltpu.VMEM((DEPTH, FR_DEV, slots, HD), jnp.bfloat16), accums], 2 * flops,
    )
    rk_one, rk_two = swap(gk_one, gk_two)
    grad_queries, grad_values, gk_own = call(
        rest_kernel, "rest", (),
        (query, grad, chosen, prob_low, score_low, gv_own, gk_own, rv_one, rv_two),
        (low, low, full), [], 2 * flops,
    )
    grad_keys = gk_own + rk_one.astype(jnp.float32) + rk_two.astype(jnp.float32)
    return (grad_queries, grad_keys.astype(jnp.bfloat16), grad_values)


def solution(mesh):
    rows = P(("clips", "frames"), "heads")
    return jax.shard_map(
        local,
        mesh=mesh,
        in_specs=(rows, rows, rows, rows, P("clips", None), P("clips", None, None, None)),
        out_specs=(rows, rows, rows),
        check_vma=False,
    )
```

```python
import math

import jax
import jax.numpy as jnp
from jax import lax
from jax.experimental import pallas as pl
from jax.experimental.pallas import tpu as pltpu
from jax.sharding import PartitionSpec as P

HD = 128
TOK_FRAME = 192
FR_DEV = 2
REACH = 2
NSEL = 3
SB = 4
DEPTH = 3
MOVED = 2
SPLIT = MOVED * HD
ROWS = FR_DEV * TOK_FRAME
WINDOW = FR_DEV + 2 * REACH
SLOTS = NSEL * TOK_FRAME
BLOCK = TOK_FRAME // SB
SCALE = HD ** (-0.5)
SCALE2 = SCALE * math.log2(math.e)
NEG = -1e30
NT = (((1,), (1,)), ((), ()))
NN = (((1,), (0,)), ((), ()))
TN = (((0,), (0,)), ((), ()))
MASKS = WINDOW * NSEL
FIRST = MASKS + WINDOW * NSEL * SB * SB
RANK = FIRST + 1
COUNT = FIRST + 2


def dot(lhs, rhs, dims):
    return lax.dot_general(lhs, rhs, dims, preferred_element_type=jnp.float32)


def column_of(head):
    return slice(head * HD, (head + 1) * HD)


def rows_of(frame):
    return slice(frame * TOK_FRAME, (frame + 1) * TOK_FRAME)


def side_of(table, side):
    return jnp.where(table[RANK] % 2 == 1, side, 2 - side)


def inside(table, place):
    target = table[FIRST] + place
    return (target >= 0) & (target < table[COUNT])


def spot_of(table, frame, slot):
    place = frame + table[(REACH + frame) * NSEL + slot]
    side = (place >= 0).astype(jnp.int32) + (place >= FR_DEV).astype(jnp.int32)
    return side_of(table, side) * FR_DEV + (place + FR_DEV) % FR_DEV


def span(table, frame, slot):
    spot = spot_of(table, frame, slot)
    return pl.ds(pl.multiple_of(spot * TOK_FRAME, TOK_FRAME), TOK_FRAME)


def pair_of(table, query, key):
    index = side_of(table, query // FR_DEV) * FR_DEV + query % FR_DEV
    place = index - REACH
    active = jnp.zeros((), jnp.int32)
    slot = jnp.zeros((), jnp.int32)
    for each in range(NSEL):
        hit = (table[index * NSEL + each] + place == key).astype(jnp.int32)
        active += hit
        slot += hit * each
    active = (active > 0) & inside(table, place)
    return active, MASKS + (index * NSEL + slot) * SB * SB


def write_bias(table, start, seen, bias, row):
    q_block = lax.broadcasted_iota(jnp.int32, (8, TOK_FRAME), 1) // BLOCK
    for k_block in range(SB):
        value = jnp.zeros((8, TOK_FRAME), jnp.float32)
        for block in range(SB):
            keep = (table[start + block * SB + k_block] > 0) & seen
            value = jnp.where(q_block == block, jnp.where(keep, 0.0, NEG), value)
        for step in range(0, BLOCK, 8):
            bias[pl.ds(row + k_block * BLOCK + step, 8), :] = value


def copy_all(pairs, sems):
    moves = [pltpu.make_async_copy(a, b, sems.at[i]) for i, (a, b) in enumerate(pairs)]
    for move in moves:
        move.start()
    return moves


def pack_kernel(queries, grad_out, keys, values, both, k_send, v_send, sems):
    moves = copy_all(
        [
            (queries.at[:, :SPLIT], both.at[0]),
            (grad_out.at[:, :SPLIT], both.at[1]),
            (keys.at[:, SPLIT:], k_send),
            (values.at[:, SPLIT:], v_send),
        ],
        sems,
    )
    for move in moves:
        move.wait()


def stage_kernel(table, *refs):
    arrays, copies, bias, moved_bias, sems = refs[:4], refs[4:8], refs[8], refs[9], refs[10]
    moves = copy_all(list(zip(arrays, copies)), sems)
    for frame in range(FR_DEV):
        for slot in range(NSEL):
            at = (REACH + frame) * NSEL + slot
            seen = inside(table, frame + table[at])
            write_bias(table, MASKS + at * SB * SB, seen, bias.at[frame], slot * TOK_FRAME)
    for query in range(WINDOW):
        for key in range(FR_DEV):
            active, start = pair_of(table, query, key)

            @pl.when(active)
            def _():
                write_bias(table, start, active, moved_bias.at[query, key], 0)

    for move in moves:
        move.wait()


def fill_window(window, one, own, two, column, far_column):
    window[0:ROWS] = one[:, far_column]
    window[ROWS : 2 * ROWS] = own[:, column]
    window[2 * ROWS : 3 * ROWS] = two[:, far_column]


def pick(table, frame, window, chosen):
    for slot in range(NSEL):
        chosen[rows_of(slot)] = window[span(table, frame, slot), :]


def spread(table, frame, accum, parts):
    for slot in range(1, NSEL):
        accum[span(table, frame, slot), :] += parts[rows_of(slot - 1)]


def values_kernel(
    table, queries, grad_out, k_own, bias, k_one, k_two,
    chosen_out, prob_out, own_out, one_out, two_out,
    windows, accums,
):
    for head in range(one_out.shape[1] // HD):
        column = column_of(MOVED + head)
        far_column = column_of(head)
        window = windows.at[head % DEPTH]
        accum = accums.at[head % DEPTH]
        fill_window(window, k_one, k_own, k_two, column, far_column)
        accum[...] = jnp.zeros_like(accum)
        for frame in range(FR_DEV):
            chosen = chosen_out.at[head, frame]
            pick(table, frame, window, chosen)
            scores = dot(chosen[...], queries[rows_of(frame), column], NT)
            masked = scores * SCALE2 + bias[frame]
            raised = jnp.exp2(masked - jnp.max(masked, 0, keepdims=True))
            inverse = 1.0 / jnp.sum(raised, 0, keepdims=True)
            prob_low = (raised * inverse).astype(jnp.bfloat16)
            prob_out[head, frame] = prob_low
            far = dot(prob_low[TOK_FRAME:], grad_out[rows_of(frame), column], NN)
            spread(table, frame, accum, far)
        one_out[:, far_column] = accum[0:ROWS].astype(one_out.dtype)
        own_out[:, far_column] = accum[ROWS : 2 * ROWS]
        two_out[:, far_column] = accum[2 * ROWS : 3 * ROWS].astype(two_out.dtype)


def keys_kernel(
    table, queries, grad_out, v_own, prob_in, v_one, v_two,
    score_out, own_out, one_out, two_out,
    windows, choices, accums,
):
    for head in range(one_out.shape[1] // HD):
        column = column_of(MOVED + head)
        far_column = column_of(head)
        window = windows.at[head % DEPTH]
        accum = accums.at[head % DEPTH]
        fill_window(window, v_one, v_own, v_two, column, far_column)
        accum[...] = jnp.zeros_like(accum)
        for frame in range(FR_DEV):
            chosen = choices.at[head % DEPTH, frame]
            pick(table, frame, window, chosen)
            grad_prob = dot(chosen[...], grad_out[rows_of(frame), column], NT)
            prob = prob_in[head, frame].astype(jnp.float32)
            delta = jnp.sum(prob * grad_prob, 0, keepdims=True)
            score_low = (prob * (grad_prob - delta)).astype(jnp.bfloat16)
            score_out[head, frame] = score_low
            far = dot(score_low[TOK_FRAME:], queries[rows_of(frame), column], NN)
            spread(table, frame, accum, far)
        one_out[:, far_column] = (accum[0:ROWS] * SCALE).astype(one_out.dtype)
        own_out[:, far_column] = accum[ROWS : 2 * ROWS]
        two_out[:, far_column] = (accum[2 * ROWS : 3 * ROWS] * SCALE).astype(two_out.dtype)


def rest_kernel(
    queries, grad_out, chosen_in, prob_in, score_in, gv_own, gk_own, rv_one, rv_two,
    query_out, value_out, key_out,
):
    for head in range(query_out.shape[1] // HD):
        column = column_of(MOVED + head)
        far_column = column_of(head)
        for frame in range(FR_DEV):
            rows = rows_of(frame)
            score_low = score_in[head, frame]
            grad_query = dot(score_low, chosen_in[head, frame], TN)
            query_out[rows, far_column] = (grad_query * SCALE).astype(query_out.dtype)
            near = dot(score_low[:TOK_FRAME], queries[rows, column], NN)
            key_out[rows, far_column] = (gk_own[rows, far_column] + near) * SCALE
            near = dot(prob_in[head, frame, :TOK_FRAME], grad_out[rows, column], NN)
            total = gv_own[rows, far_column] + near
            total += rv_one[rows, far_column].astype(jnp.float32)
            total += rv_two[rows, far_column].astype(jnp.float32)
            value_out[rows, far_column] = total.astype(value_out.dtype)


def view_of(query, own, one, two, part, head):
    rows = rows_of(query % FR_DEV)
    column = column_of(head)
    if query // FR_DEV == 1:
        return own[rows, column]
    return (one if query < FR_DEV else two)[part, rows, column]


def stats_kernel(
    table, queries, grad_out, keys, values, bias, f_one, f_two,
    masked_out, grad_prob_out, mine_out, one_out, two_out, far_out, other_out,
    parts,
):
    for query in range(WINDOW):
        for key in range(FR_DEV):
            active, _ = pair_of(table, query, key)

            @pl.when(active)
            def _():
                for head in range(MOVED):
                    column = column_of(head)
                    row = slice(query * MOVED + head, query * MOVED + head + 1)
                    rows = rows_of(key)
                    scores = dot(
                        keys[rows, column], view_of(query, queries, f_one, f_two, 0, head), NT
                    )
                    masked = scores * SCALE2 + bias[query, key]
                    highest = jnp.max(masked, 0, keepdims=True)
                    raised = jnp.exp2(masked - highest)
                    grad_prob = dot(
                        values[rows, column], view_of(query, grad_out, f_one, f_two, 1, head), NT
                    )
                    masked_out[query, key, head] = masked
                    grad_prob_out[query, key, head] = grad_prob
                    parts[key, 0, row] = highest
                    parts[key, 1, row] = jnp.sum(raised, 0, keepdims=True)
                    parts[key, 2, row] = jnp.sum(raised * grad_prob, 0, keepdims=True)

            @pl.when(jnp.logical_not(active))
            def _():
                rows = slice(query * MOVED, (query + 1) * MOVED)
                parts[key, 0, rows] = jnp.full((MOVED, TOK_FRAME), NEG, jnp.float32)
                parts[key, 1, rows] = jnp.zeros((MOVED, TOK_FRAME), jnp.float32)
                parts[key, 2, rows] = jnp.zeros((MOVED, TOK_FRAME), jnp.float32)

    highest, total, moment = joined_stats([parts[key] for key in range(FR_DEV)])
    mine_out[0] = highest
    mine_out[1] = total
    mine_out[2] = moment
    side = FR_DEV * MOVED
    rank = table[RANK] % 4
    swapped = (rank == 1) | (rank == 2)
    for index in range(3):
        whole = mine_out[index]
        one_out[index] = whole[0 : 2 * side]
        two_out[index] = whole[side : 3 * side]
        far_out[index] = jnp.where(swapped, whole[2 * side :], whole[:side])
        other_out[index] = jnp.where(swapped, whole[:side], whole[2 * side :])


def joined_stats(sources):
    tops = [jnp.where(each[1] > 0, each[0], NEG) for each in sources]
    highest = tops[0]
    for top in tops[1:]:
        highest = jnp.maximum(highest, top)
    weights = [jnp.exp2(top - highest) for top in tops]
    total = sum(weight * each[1] for weight, each in zip(weights, sources))
    moment = sum(weight * each[2] for weight, each in zip(weights, sources))
    return highest, total, moment


def finish_pair(query, key, head, masked, grad_probs, logs, deltas):
    row = slice(query * MOVED + head, query * MOVED + head + 1)
    prob = jnp.exp2(masked[query, key, head] - logs[row])
    score_low = (prob * (grad_probs[query, key, head] - deltas[row])).astype(jnp.bfloat16)
    return prob.astype(jnp.bfloat16), score_low


def back_kernel(
    table, keys, masked, grad_probs, mine, s_one, s_two, s_far, s_other,
    prob_out, score_out, logs, deltas, one_out, two_out,
    accums,
):
    side = FR_DEV * MOVED
    rank = table[RANK] % 4
    swapped = (rank == 1) | (rank == 2)
    far = [jnp.where(swapped, s_other[i], s_far[i]) for i in range(3)]
    other = [jnp.where(swapped, s_far[i], s_other[i]) for i in range(3)]

    def part(ref, start):
        return [ref[i, start : start + side] for i in range(3)]

    groups = (
        (part(mine, 0), part(s_one, side), far),
        (part(mine, side), part(s_one, 0), part(s_two, side)),
        (part(mine, 2 * side), part(s_two, 0), other),
    )
    for index, sources in enumerate(groups):
        highest, total, moment = joined_stats(sources)
        rows = slice(index * side, (index + 1) * side)
        total = jnp.where(total > 0, total, 1.0)
        logs[rows] = highest + jnp.log2(total)
        deltas[rows] = moment / total
    accums[...] = jnp.zeros_like(accums)
    for query in (0, 1, 4, 5):
        for key in range(FR_DEV):
            active, _ = pair_of(table, query, key)

            @pl.when(active)
            def _():
                for head in range(MOVED):
                    prob_low, score_low = finish_pair(
                        query, key, head, masked, grad_probs, logs, deltas
                    )
                    prob_out[query, key, head] = prob_low
                    score_out[query, key, head] = score_low
                    accums[query // 4, rows_of(query % FR_DEV), column_of(head)] += dot(
                        score_low, keys[rows_of(key), column_of(head)], TN
                    )

    one_out[...] = (accums[0] * SCALE).astype(one_out.dtype)
    two_out[...] = (accums[1] * SCALE).astype(two_out.dtype)


def home_kernel(
    table, queries, grad_out, keys, f_one, f_two, masked, grad_probs, prob_in, score_in,
    logs, deltas,
    query_out, key_out, value_out,
    key_accum, value_accum,
):
    query_out[...] = jnp.zeros_like(query_out)
    key_accum[...] = jnp.zeros_like(key_accum)
    value_accum[...] = jnp.zeros_like(value_accum)
    for query in range(WINDOW):
        for key in range(FR_DEV):
            active, _ = pair_of(table, query, key)

            @pl.when(active)
            def _():
                for head in range(MOVED):
                    column = column_of(head)
                    rows = rows_of(key)
                    if query // FR_DEV == 1:
                        prob_low, score_low = finish_pair(
                            query, key, head, masked, grad_probs, logs, deltas
                        )
                        query_out[rows_of(query % FR_DEV), column] += dot(
                            score_low, keys[rows, column], TN
                        )
                    else:
                        prob_low = prob_in[query, key, head]
                        score_low = score_in[query, key, head]
                    key_accum[rows, column] += dot(
                        score_low, view_of(query, queries, f_one, f_two, 0, head), NN
                    )
                    value_accum[rows, column] += dot(
                        prob_low, view_of(query, grad_out, f_one, f_two, 1, head), NN
                    )

    query_out[...] = query_out[...] * SCALE
    key_out[...] = (key_accum[...] * SCALE).astype(key_out.dtype)
    value_out[...] = value_accum[...].astype(value_out.dtype)


def both_ways(pairs):
    return [pair for i, j in pairs for pair in ((i, j), (j, i))]


def swap(one, two):
    count = lax.axis_size("frames")
    first = [(i, i + 1) for i in range(0, count - 1, 2)]
    second = [(i, i + 1) for i in range(1, count - 1, 2)]
    return (
        lax.ppermute(one, "frames", both_ways(first)),
        lax.ppermute(two, "frames", both_ways(second)),
    )


def swap_far(far, other):
    count = lax.axis_size("frames")
    near = [(i, i + 2) for i in range(count - 2) if i % 4 < 2]
    over = [(i, i + 2) for i in range(count - 2) if i % 4 >= 2]
    far = lax.ppermute(far, "frames", both_ways(near))
    other = lax.ppermute(other, "frames", both_ways(over)) if over else jnp.zeros_like(other)
    return far, other


def lookup(offsets, spatial):
    rank = lax.axis_index("frames")
    first = rank * FR_DEV
    frames = offsets.shape[0]
    around = ((REACH, REACH), (0, 0))
    shifts = lax.dynamic_slice_in_dim(jnp.pad(offsets, around), first, WINDOW, 0)
    blocks = lax.dynamic_slice_in_dim(
        jnp.pad(spatial, around + ((0, 0), (0, 0))), first, WINDOW, 0
    )
    ends = jnp.stack([first, rank, jnp.full_like(rank, frames)]).astype(jnp.int32)
    return jnp.concatenate([shifts.reshape(-1), blocks.reshape(-1), ends])


def call(kernel, name, scalars, arrays, outs, scratch, flops, space=pltpu.VMEM):
    arrays = [pltpu.with_memory_space_constraint(array, space) for array in arrays]
    return pl.pallas_call(
        kernel,
        out_shape=outs,
        in_specs=[pl.BlockSpec(memory_space=pltpu.SMEM)] * len(scalars)
        + [pl.BlockSpec(memory_space=space)] * len(arrays),
        out_specs=tuple(pl.BlockSpec(memory_space=pltpu.VMEM) for _ in outs),
        scratch_shapes=scratch,
        compiler_params=pltpu.CompilerParams(vmem_limit_bytes=16 << 20),
        cost_estimate=pl.CostEstimate(flops=flops, bytes_accessed=0, transcendentals=0),
        name=name,
    )(*scalars, *arrays)


def local(queries, keys, values, grad_out, offsets, spatial):
    width = queries.shape[1]
    heads = width // HD - MOVED

    def low(*shape):
        return pltpu.VMEM(shape, jnp.bfloat16)

    def full(*shape):
        return pltpu.VMEM(shape, jnp.float32)

    unit = 2 * FR_DEV * NSEL * TOK_FRAME * TOK_FRAME * HD
    rest = width - SPLIT
    y_send, k_send, v_send = call(
        pack_kernel, "pack", (), (queries, grad_out, keys, values),
        (low(2, ROWS, SPLIT), low(ROWS, rest), low(ROWS, rest)),
        [pltpu.SemaphoreType.DMA((4,))], unit, pltpu.HBM,
    )
    f_one, f_two = swap(y_send, y_send)
    k_one, k_two = swap(k_send, k_send)
    v_one, v_two = swap(v_send, v_send)
    table = lookup(offsets, spatial)
    query, grad, key, value, bias, moved_bias = call(
        stage_kernel, "stage", (table,), (queries, grad_out, keys, values),
        (low(ROWS, width),) * 4
        + (full(FR_DEV, SLOTS, TOK_FRAME), full(WINDOW, FR_DEV, TOK_FRAME, TOK_FRAME)),
        [pltpu.SemaphoreType.DMA((4,))], unit, pltpu.HBM,
    )
    grid = (WINDOW, FR_DEV, MOVED, TOK_FRAME, TOK_FRAME)
    side = FR_DEV * MOVED
    masked, grad_probs, mine, s_one, s_two, s_far, s_other = call(
        stats_kernel, "stats", (table,), (query, grad, key, value, moved_bias, f_one, f_two),
        (full(*grid), full(*grid), full(3, 3 * side, TOK_FRAME))
        + (full(3, 2 * side, TOK_FRAME),) * 2 + (full(3, side, TOK_FRAME),) * 2,
        [full(FR_DEV, 3, 3 * side, TOK_FRAME)], 2 * MOVED * unit,
    )
    s_one, s_two = swap(s_one, s_two)
    s_far, s_other = swap_far(s_far, s_other)
    k_one, k_two, mine = lax.optimization_barrier((k_one, k_two, mine))
    windows = low(DEPTH, 3 * ROWS, HD)
    accums = full(DEPTH, 3 * ROWS, HD)
    pairs = low(heads, FR_DEV, SLOTS, TOK_FRAME)
    chosen, prob_low, gv_own, gv_one, gv_two = call(
        values_kernel, "values_part", (table,), (query, grad, key, bias, k_one, k_two),
        (low(heads, FR_DEV, SLOTS, HD), pairs, full(ROWS, rest), low(ROWS, rest), low(ROWS, rest)),
        [windows, accums], 2 * heads * unit,
    )
    rv_one, rv_two = swap(gv_one, gv_two)
    score_low, gk_own, gk_one, gk_two = call(
        keys_kernel, "keys_part", (table,), (query, grad, value, prob_low, v_one, v_two),
        (pairs, full(ROWS, rest), low(ROWS, rest), low(ROWS, rest)),
        [windows, low(DEPTH, FR_DEV, SLOTS, HD), accums], 2 * heads * unit,
    )
    rk_one, rk_two = swap(gk_one, gk_two)
    gk_own, masked = lax.optimization_barrier((gk_own, masked))
    y_prob, y_score, logs, deltas, gq_one, gq_two = call(
        back_kernel, "back", (table,),
        (key, masked, grad_probs, mine, s_one, s_two, s_far, s_other),
        (low(*grid), low(*grid), full(3 * side, TOK_FRAME), full(3 * side, TOK_FRAME))
        + (low(ROWS, SPLIT),) * 2,
        [full(2, ROWS, SPLIT)], MOVED * unit,
    )
    rq_one, rq_two = swap(gq_one, gq_two)
    gq_near, gk_near, gv_near = call(
        home_kernel, "home", (table,),
        (query, grad, key, f_one, f_two, masked, grad_probs, y_prob, y_score, logs, deltas),
        (full(ROWS, SPLIT), low(ROWS, SPLIT), low(ROWS, SPLIT)),
        [full(ROWS, SPLIT), full(ROWS, SPLIT)], 3 * MOVED * unit,
    )
    gq_rest, gv_rest, gk_own = call(
        rest_kernel, "rest", (),
        (query, grad, chosen, prob_low, score_low, gv_own, gk_own, rv_one, rv_two),
        (low(ROWS, rest), low(ROWS, rest), full(ROWS, rest)), [], 2 * heads * unit,
    )

    def joined(own, one, two):
        total = own + one.astype(jnp.float32) + two.astype(jnp.float32)
        return total.astype(jnp.bfloat16)

    grad_queries = jnp.concatenate([joined(gq_near, rq_one, rq_two), gq_rest], 1)
    grad_keys = jnp.concatenate([gk_near, joined(gk_own, rk_one, rk_two)], 1)
    grad_values = jnp.concatenate([gv_near, gv_rest], 1)
    return grad_queries, grad_keys, grad_values


def solution(mesh):
    rows = P(("clips", "frames"), "heads")
    return jax.shard_map(
        local,
        mesh=mesh,
        in_specs=(rows, rows, rows, rows, P("clips", None), P("clips", None, None, None)),
        out_specs=(rows, rows, rows),
        check_vma=False,
    )
```

```python
import math

import jax
import jax.numpy as jnp
from jax import lax
from jax.experimental import pallas as pl
from jax.experimental.pallas import tpu as pltpu
from jax.sharding import PartitionSpec as P

HD = 128
TOK_FRAME = 192
FR_DEV = 2
REACH = 2
NSEL = 3
SB = 4
DEPTH = 3
MOVED = 3
SPLIT = MOVED * HD
ROWS = FR_DEV * TOK_FRAME
WINDOW = FR_DEV + 2 * REACH
SLOTS = NSEL * TOK_FRAME
BLOCK = TOK_FRAME // SB
SCALE = HD ** (-0.5)
SCALE2 = SCALE * math.log2(math.e)
NEG = -(2.0**100)
NT = (((1,), (1,)), ((), ()))
NN = (((1,), (0,)), ((), ()))
TN = (((0,), (0,)), ((), ()))
MASKS = WINDOW * NSEL
FIRST = MASKS + WINDOW * NSEL * SB * SB
RANK = FIRST + 1
COUNT = FIRST + 2
NOTES = 32
SIDE = FR_DEV * MOVED


def dot(lhs, rhs, dims):
    return lax.dot_general(lhs, rhs, dims, preferred_element_type=jnp.float32)


def column_of(head):
    return slice(head * HD, (head + 1) * HD)


def rows_of(frame):
    return slice(frame * TOK_FRAME, (frame + 1) * TOK_FRAME)


def side_of(table, side):
    return jnp.where(table[RANK] % 2 == 1, side, 2 - side)


def inside(table, place):
    target = table[FIRST] + place
    return (target >= 0) & (target < table[COUNT])


def spot_of(table, frame, slot):
    place = frame + table[(REACH + frame) * NSEL + slot]
    side = (place >= 0).astype(jnp.int32) + (place >= FR_DEV).astype(jnp.int32)
    return side_of(table, side) * FR_DEV + (place + FR_DEV) % FR_DEV


def span(table, frame, slot):
    spot = spot_of(table, frame, slot)
    return pl.ds(pl.multiple_of(spot * TOK_FRAME, TOK_FRAME), TOK_FRAME)


def pair_of(table, query, key):
    index = side_of(table, query // FR_DEV) * FR_DEV + query % FR_DEV
    place = index - REACH
    active = jnp.zeros((), jnp.int32)
    slot = jnp.zeros((), jnp.int32)
    for each in range(NSEL):
        hit = (table[index * NSEL + each] + place == key).astype(jnp.int32)
        active += hit
        slot += hit * each
    active = (active > 0) & inside(table, place)
    return active, MASKS + (index * NSEL + slot) * SB * SB


def write_bias(table, start, seen, bias, row):
    q_block = lax.broadcasted_iota(jnp.int32, (8, TOK_FRAME), 1) // BLOCK
    for k_block in range(SB):
        value = jnp.zeros((8, TOK_FRAME), jnp.float32)
        for block in range(SB):
            keep = (table[start + block * SB + k_block] > 0) & seen
            value = jnp.where(q_block == block, jnp.where(keep, 0.0, NEG), value)
        for step in range(0, BLOCK, 8):
            bias[pl.ds(row + k_block * BLOCK + step, 8), :] = value


def copy_all(pairs, sems):
    moves = [pltpu.make_async_copy(a, b, sems.at[i]) for i, (a, b) in enumerate(pairs)]
    for move in moves:
        move.start()
    return moves


def pack_kernel(queries, grad_out, keys, values, both, k_send, v_send, sems):
    moves = copy_all(
        [
            (queries.at[:, :SPLIT], both.at[0]),
            (grad_out.at[:, :SPLIT], both.at[1]),
            (keys.at[:, SPLIT:], k_send),
            (values.at[:, SPLIT:], v_send),
        ],
        sems,
    )
    for move in moves:
        move.wait()


def stage_kernel(table, *refs):
    arrays, copies, bias, moved_bias, sems = refs[:4], refs[4:8], refs[8], refs[9], refs[10]
    moves = copy_all(list(zip(arrays, copies)), sems)
    for frame in range(FR_DEV):
        for slot in range(NSEL):
            at = (REACH + frame) * NSEL + slot
            seen = inside(table, frame + table[at])
            write_bias(table, MASKS + at * SB * SB, seen, bias.at[frame], slot * TOK_FRAME)
    for query in range(WINDOW):
        for key in range(FR_DEV):
            active, start = pair_of(table, query, key)

            @pl.when(active)
            def _():
                write_bias(table, start, active, moved_bias.at[query, key], 0)

    for move in moves:
        move.wait()


def fill_window(window, one, own, two, column, far_column):
    window[0:ROWS] = one[:, far_column]
    window[ROWS : 2 * ROWS] = own[:, column]
    window[2 * ROWS : 3 * ROWS] = two[:, far_column]


def pick(table, frame, window, chosen):
    for slot in range(NSEL):
        chosen[rows_of(slot)] = window[span(table, frame, slot), :]


def spread(table, frame, accum, parts):
    for slot in range(1, NSEL):
        accum[span(table, frame, slot), :] += parts[rows_of(slot - 1)]


def values_kernel(
    table, queries, grad_out, k_own, bias, k_one, k_two, n_one, n_two,
    chosen_out, prob_out, own_out, one_out, two_out,
    windows, accums,
):
    for head in range(one_out.shape[1] // HD):
        column = column_of(MOVED + head)
        far_column = column_of(head)
        window = windows.at[head % DEPTH]
        accum = accums.at[head % DEPTH]
        fill_window(window, k_one, k_own, k_two, column, far_column)
        accum[...] = jnp.zeros_like(accum)
        for frame in range(FR_DEV):
            chosen = chosen_out.at[head, frame]
            pick(table, frame, window, chosen)
            scores = dot(chosen[...], queries[rows_of(frame), column], NT)
            masked = scores * SCALE2 + bias[frame]
            raised = jnp.exp2(masked - jnp.max(masked, 0, keepdims=True))
            inverse = 1.0 / jnp.sum(raised, 0, keepdims=True)
            prob_low = (raised * inverse).astype(jnp.bfloat16)
            prob_out[head, frame] = prob_low
            far = dot(prob_low[TOK_FRAME:], grad_out[rows_of(frame), column], NN)
            spread(table, frame, accum, far)
        one_out[:ROWS, far_column] = accum[0:ROWS].astype(one_out.dtype)
        own_out[:, far_column] = accum[ROWS : 2 * ROWS]
        two_out[:ROWS, far_column] = accum[2 * ROWS : 3 * ROWS].astype(two_out.dtype)
    write_notes(n_one, one_out)
    write_notes(n_two, two_out)


def keys_kernel(
    table, queries, grad_out, v_own, prob_in, v_one, v_two,
    score_out, own_out, one_out, two_out,
    windows, choices, accums,
):
    for head in range(one_out.shape[1] // HD):
        column = column_of(MOVED + head)
        far_column = column_of(head)
        window = windows.at[head % DEPTH]
        accum = accums.at[head % DEPTH]
        fill_window(window, v_one, v_own, v_two, column, far_column)
        accum[...] = jnp.zeros_like(accum)
        for frame in range(FR_DEV):
            chosen = choices.at[head % DEPTH, frame]
            pick(table, frame, window, chosen)
            grad_prob = dot(chosen[...], grad_out[rows_of(frame), column], NT)
            prob = prob_in[head, frame].astype(jnp.float32)
            delta = jnp.sum(prob * grad_prob, 0, keepdims=True)
            score_low = (prob * (grad_prob - delta)).astype(jnp.bfloat16)
            score_out[head, frame] = score_low
            far = dot(score_low[TOK_FRAME:], queries[rows_of(frame), column], NN)
            spread(table, frame, accum, far)
        one_out[:, far_column] = (accum[0:ROWS] * SCALE).astype(one_out.dtype)
        own_out[:, far_column] = accum[ROWS : 2 * ROWS]
        two_out[:, far_column] = (accum[2 * ROWS : 3 * ROWS] * SCALE).astype(two_out.dtype)


def rest_kernel(
    queries, grad_out, chosen_in, prob_in, score_in, gv_own, gk_own, rv_one, rv_two,
    query_out, value_out, key_out,
):
    for head in range(query_out.shape[1] // HD):
        column = column_of(MOVED + head)
        far_column = column_of(head)
        for frame in range(FR_DEV):
            rows = rows_of(frame)
            score_low = score_in[head, frame]
            grad_query = dot(score_low, chosen_in[head, frame], TN)
            query_out[rows, far_column] = (grad_query * SCALE).astype(query_out.dtype)
            near = dot(score_low[:TOK_FRAME], queries[rows, column], NN)
            key_out[rows, far_column] = (gk_own[rows, far_column] + near) * SCALE
            near = dot(prob_in[head, frame, :TOK_FRAME], grad_out[rows, column], NN)
            total = gv_own[rows, far_column] + near
            total += rv_one[rows, far_column].astype(jnp.float32)
            total += rv_two[rows, far_column].astype(jnp.float32)
            value_out[rows, far_column] = total.astype(value_out.dtype)


def view_of(query, own, one, two, part, head):
    rows = rows_of(query % FR_DEV)
    column = column_of(head)
    if query // FR_DEV == 1:
        return own[rows, column]
    return (one if query < FR_DEV else two)[part, rows, column]


def stats_kernel(
    table, queries, grad_out, keys, values, bias, f_one, f_two,
    masked_out, grad_prob_out, mine_out, one_out, two_out, far_out, other_out,
    parts,
):
    for query in range(WINDOW):
        for key in range(FR_DEV):
            active, _ = pair_of(table, query, key)

            @pl.when(active)
            def _():
                for head in range(MOVED):
                    column = column_of(head)
                    row = slice(query * MOVED + head, query * MOVED + head + 1)
                    rows = rows_of(key)
                    scores = dot(
                        keys[rows, column], view_of(query, queries, f_one, f_two, 0, head), NT
                    )
                    masked = scores * SCALE2 + bias[query, key]
                    highest = rounded(jnp.max(masked, 0, keepdims=True))
                    raised = jnp.exp2(masked - highest)
                    grad_prob = dot(
                        values[rows, column], view_of(query, grad_out, f_one, f_two, 1, head), NT
                    )
                    masked_out[query, key, head] = masked
                    grad_prob_out[query, key, head] = grad_prob
                    parts[key, 0, row] = highest
                    parts[key, 1, row] = jnp.sum(raised, 0, keepdims=True)
                    parts[key, 2, row] = jnp.sum(raised * grad_prob, 0, keepdims=True)

            @pl.when(jnp.logical_not(active))
            def _():
                rows = slice(query * MOVED, (query + 1) * MOVED)
                parts[key, 0, rows] = jnp.full((MOVED, TOK_FRAME), NEG, jnp.float32)
                parts[key, 1, rows] = jnp.zeros((MOVED, TOK_FRAME), jnp.float32)
                parts[key, 2, rows] = jnp.zeros((MOVED, TOK_FRAME), jnp.float32)

    highest, total, moment = joined_stats([parts[key] for key in range(FR_DEV)])
    mine_out[0] = highest
    mine_out[1] = total
    mine_out[2] = moment
    side = SIDE
    rank = table[RANK] % 4
    swapped = (rank == 1) | (rank == 2)
    for out, start in ((one_out, 0), (two_out, side)):
        rows = slice(start, start + 2 * side)
        out[...] = jnp.zeros_like(out)
        notes = (highest[rows], *halves(total[rows]), *halves(moment[rows]))
        for index, note in enumerate(notes):
            out[index * 2 * side : (index + 1) * 2 * side] = note
    for index in range(3):
        whole = mine_out[index]
        far_out[index] = jnp.where(swapped, whole[2 * side :], whole[:side])
        other_out[index] = jnp.where(swapped, whole[:side], whole[2 * side :])


def rounded(array):
    return array.astype(jnp.bfloat16).astype(jnp.float32)


def halves(array):
    high = rounded(array)
    return high, array - high


def write_notes(notes, message):
    for half in range(2):
        message[ROWS:, half * TOK_FRAME : (half + 1) * TOK_FRAME] = notes[
            half * NOTES : (half + 1) * NOTES
        ].astype(message.dtype)


def read_notes(message, notes):
    for half in range(2):
        notes[half * NOTES : (half + 1) * NOTES] = message[
            ROWS:, half * TOK_FRAME : (half + 1) * TOK_FRAME
        ].astype(notes.dtype)
    parts = [notes[i * 2 * SIDE : (i + 1) * 2 * SIDE] for i in range(5)]
    return parts[0], parts[1] + parts[2], parts[3] + parts[4]


def joined_stats(sources):
    tops = [jnp.where(each[1] > 0, each[0], NEG) for each in sources]
    highest = tops[0]
    for top in tops[1:]:
        highest = jnp.maximum(highest, top)
    weights = [jnp.exp2(top - highest) for top in tops]
    total = sum(weight * each[1] for weight, each in zip(weights, sources))
    moment = sum(weight * each[2] for weight, each in zip(weights, sources))
    return highest, total, moment


def finish_pair(query, key, head, masked, grad_probs, logs, deltas):
    row = slice(query * MOVED + head, query * MOVED + head + 1)
    prob = jnp.exp2(masked[query, key, head] - logs[row])
    score_low = (prob * (grad_probs[query, key, head] - deltas[row])).astype(jnp.bfloat16)
    return prob.astype(jnp.bfloat16), score_low


def back_kernel(
    table, keys, masked, grad_probs, mine, r_one, r_two, s_far, s_other,
    prob_out, score_out, logs, deltas, one_out, two_out,
    accums, notes,
):
    side = SIDE
    rank = table[RANK] % 4
    swapped = (rank == 1) | (rank == 2)
    far = [jnp.where(swapped, s_other[i], s_far[i]) for i in range(3)]
    other = [jnp.where(swapped, s_far[i], s_other[i]) for i in range(3)]
    s_one = read_notes(r_one, notes.at[0])
    s_two = read_notes(r_two, notes.at[1])
    s_mine = [mine[i] for i in range(3)]

    def part(stats, start):
        return [each[start : start + side] for each in stats]

    groups = (
        (part(s_mine, 0), part(s_one, side), far),
        (part(s_mine, side), part(s_one, 0), part(s_two, side)),
        (part(s_mine, 2 * side), part(s_two, 0), other),
    )
    for index, sources in enumerate(groups):
        highest, total, moment = joined_stats(sources)
        rows = slice(index * side, (index + 1) * side)
        total = jnp.where(total > 0, total, 1.0)
        logs[rows] = highest + jnp.log2(total)
        deltas[rows] = moment / total
    accums[...] = jnp.zeros_like(accums)
    for query in (0, 1, 4, 5):
        for key in range(FR_DEV):
            active, _ = pair_of(table, query, key)

            @pl.when(active)
            def _():
                for head in range(MOVED):
                    prob_low, score_low = finish_pair(
                        query, key, head, masked, grad_probs, logs, deltas
                    )
                    prob_out[query, key, head] = prob_low
                    score_out[query, key, head] = score_low
                    accums[query // 4, rows_of(query % FR_DEV), column_of(head)] += dot(
                        score_low, keys[rows_of(key), column_of(head)], TN
                    )

    one_out[...] = (accums[0] * SCALE).astype(one_out.dtype)
    two_out[...] = (accums[1] * SCALE).astype(two_out.dtype)


def home_kernel(
    table, queries, grad_out, keys, f_one, f_two, masked, grad_probs, prob_in, score_in,
    logs, deltas,
    query_out, key_out, value_out,
    key_accum, value_accum,
):
    query_out[...] = jnp.zeros_like(query_out)
    key_accum[...] = jnp.zeros_like(key_accum)
    value_accum[...] = jnp.zeros_like(value_accum)
    for query in range(WINDOW):
        for key in range(FR_DEV):
            active, _ = pair_of(table, query, key)

            @pl.when(active)
            def _():
                for head in range(MOVED):
                    column = column_of(head)
                    rows = rows_of(key)
                    if query // FR_DEV == 1:
                        prob_low, score_low = finish_pair(
                            query, key, head, masked, grad_probs, logs, deltas
                        )
                        query_out[rows_of(query % FR_DEV), column] += dot(
                            score_low, keys[rows, column], TN
                        )
                    else:
                        prob_low = prob_in[query, key, head]
                        score_low = score_in[query, key, head]
                    key_accum[rows, column] += dot(
                        score_low, view_of(query, queries, f_one, f_two, 0, head), NN
                    )
                    value_accum[rows, column] += dot(
                        prob_low, view_of(query, grad_out, f_one, f_two, 1, head), NN
                    )

    query_out[...] = query_out[...] * SCALE
    key_out[...] = (key_accum[...] * SCALE).astype(key_out.dtype)
    value_out[...] = value_accum[...].astype(value_out.dtype)


def both_ways(pairs):
    return [pair for i, j in pairs for pair in ((i, j), (j, i))]


def swap(one, two):
    count = lax.axis_size("frames")
    first = [(i, i + 1) for i in range(0, count - 1, 2)]
    second = [(i, i + 1) for i in range(1, count - 1, 2)]
    return (
        lax.ppermute(one, "frames", both_ways(first)),
        lax.ppermute(two, "frames", both_ways(second)),
    )


def swap_far(far, other):
    count = lax.axis_size("frames")
    near = [(i, i + 2) for i in range(count - 2) if i % 4 < 2]
    over = [(i, i + 2) for i in range(count - 2) if i % 4 >= 2]
    far = lax.ppermute(far, "frames", both_ways(near))
    other = lax.ppermute(other, "frames", both_ways(over)) if over else jnp.zeros_like(other)
    return far, other


def lookup(offsets, spatial):
    rank = lax.axis_index("frames")
    first = rank * FR_DEV
    frames = offsets.shape[0]
    around = ((REACH, REACH), (0, 0))
    shifts = lax.dynamic_slice_in_dim(jnp.pad(offsets, around), first, WINDOW, 0)
    blocks = lax.dynamic_slice_in_dim(
        jnp.pad(spatial, around + ((0, 0), (0, 0))), first, WINDOW, 0
    )
    ends = jnp.stack([first, rank, jnp.full_like(rank, frames)]).astype(jnp.int32)
    return jnp.concatenate([shifts.reshape(-1), blocks.reshape(-1), ends])


def call(kernel, name, scalars, arrays, outs, scratch, flops, space=pltpu.VMEM):
    arrays = [pltpu.with_memory_space_constraint(array, space) for array in arrays]
    return pl.pallas_call(
        kernel,
        out_shape=outs,
        in_specs=[pl.BlockSpec(memory_space=pltpu.SMEM)] * len(scalars)
        + [pl.BlockSpec(memory_space=space)] * len(arrays),
        out_specs=tuple(pl.BlockSpec(memory_space=pltpu.VMEM) for _ in outs),
        scratch_shapes=scratch,
        compiler_params=pltpu.CompilerParams(vmem_limit_bytes=16 << 20),
        cost_estimate=pl.CostEstimate(flops=flops // 1000, bytes_accessed=0, transcendentals=0),
        name=name,
    )(*scalars, *arrays)


def local(queries, keys, values, grad_out, offsets, spatial):
    width = queries.shape[1]
    heads = width // HD - MOVED

    def low(*shape):
        return pltpu.VMEM(shape, jnp.bfloat16)

    def full(*shape):
        return pltpu.VMEM(shape, jnp.float32)

    unit = 2 * FR_DEV * NSEL * TOK_FRAME * TOK_FRAME * HD
    rest = width - SPLIT
    y_send, k_send, v_send = call(
        pack_kernel, "pack", (), (queries, grad_out, keys, values),
        (low(2, ROWS, SPLIT), low(ROWS, rest), low(ROWS, rest)),
        [pltpu.SemaphoreType.DMA((4,))], unit, pltpu.HBM,
    )
    f_one, f_two = swap(y_send, y_send)
    k_one, k_two = swap(k_send, k_send)
    v_one, v_two = swap(v_send, v_send)
    table = lookup(offsets, spatial)
    query, grad, key, value, bias, moved_bias = call(
        stage_kernel, "stage", (table,), (queries, grad_out, keys, values),
        (low(ROWS, width),) * 4
        + (full(FR_DEV, SLOTS, TOK_FRAME), full(WINDOW, FR_DEV, TOK_FRAME, TOK_FRAME)),
        [pltpu.SemaphoreType.DMA((4,))], unit, pltpu.HBM,
    )
    grid = (WINDOW, FR_DEV, MOVED, TOK_FRAME, TOK_FRAME)
    side = SIDE
    note = full(2 * NOTES, TOK_FRAME)
    masked, grad_probs, mine, n_one, n_two, s_far, s_other = call(
        stats_kernel, "stats", (table,), (query, grad, key, value, moved_bias, f_one, f_two),
        (full(*grid), full(*grid), full(3, 3 * side, TOK_FRAME))
        + (note, note) + (full(3, side, TOK_FRAME),) * 2,
        [full(FR_DEV, 3, 3 * side, TOK_FRAME)], 2 * MOVED * unit,
    )
    s_far, s_other = swap_far(s_far, s_other)
    windows = low(DEPTH, 3 * ROWS, HD)
    accums = full(DEPTH, 3 * ROWS, HD)
    pairs = low(heads, FR_DEV, SLOTS, TOK_FRAME)
    chosen, prob_low, gv_own, gv_one, gv_two = call(
        values_kernel, "values_part", (table,),
        (query, grad, key, bias, k_one, k_two, n_one, n_two),
        (low(heads, FR_DEV, SLOTS, HD), pairs, full(ROWS, rest))
        + (low(ROWS + NOTES, rest),) * 2,
        [windows, accums], 2 * heads * unit,
    )
    rv_one, rv_two = swap(gv_one, gv_two)
    v_one, s_far = lax.optimization_barrier((v_one, s_far))
    score_low, gk_own, gk_one, gk_two = call(
        keys_kernel, "keys_part", (table,), (query, grad, value, prob_low, v_one, v_two),
        (pairs, full(ROWS, rest), low(ROWS, rest), low(ROWS, rest)),
        [windows, low(DEPTH, FR_DEV, SLOTS, HD), accums], 2 * heads * unit,
    )
    rk_one, rk_two = swap(gk_one, gk_two)
    gk_own, masked = lax.optimization_barrier((gk_own, masked))
    y_prob, y_score, logs, deltas, gq_one, gq_two = call(
        back_kernel, "back", (table,),
        (key, masked, grad_probs, mine, rv_one, rv_two, s_far, s_other),
        (low(*grid), low(*grid), full(3 * side, TOK_FRAME), full(3 * side, TOK_FRAME))
        + (low(ROWS, SPLIT),) * 2,
        [full(2, ROWS, SPLIT), full(2, 2 * NOTES, TOK_FRAME)], MOVED * unit,
    )
    rq_one, rq_two = swap(gq_one, gq_two)
    gq_near, gk_near, gv_near = call(
        home_kernel, "home", (table,),
        (query, grad, key, f_one, f_two, masked, grad_probs, y_prob, y_score, logs, deltas),
        (full(ROWS, SPLIT), low(ROWS, SPLIT), low(ROWS, SPLIT)),
        [full(ROWS, SPLIT), full(ROWS, SPLIT)], 3 * MOVED * unit,
    )
    gq_rest, gv_rest, gk_own = call(
        rest_kernel, "rest", (),
        (query, grad, chosen, prob_low, score_low, gv_own, gk_own, rv_one, rv_two),
        (low(ROWS, rest), low(ROWS, rest), full(ROWS, rest)), [], 2 * heads * unit,
    )

    def joined(own, one, two):
        total = own + one.astype(jnp.float32) + two.astype(jnp.float32)
        return total.astype(jnp.bfloat16)

    grad_queries = jnp.concatenate([joined(gq_near, rq_one, rq_two), gq_rest], 1)
    grad_keys = jnp.concatenate([gk_near, joined(gk_own, rk_one, rk_two)], 1)
    grad_values = jnp.concatenate([gv_near, gv_rest], 1)
    return grad_queries, grad_keys, grad_values


def solution(mesh):
    rows = P(("clips", "frames"), "heads")
    return jax.shard_map(
        local,
        mesh=mesh,
        in_specs=(rows, rows, rows, rows, P("clips", None), P("clips", None, None, None)),
        out_specs=(rows, rows, rows),
        check_vma=False,
    )
```

```python
import math

import jax
import jax.numpy as jnp
from jax import lax
from jax.experimental import pallas as pl
from jax.experimental.pallas import tpu as pltpu
from jax.sharding import PartitionSpec as P

HD = 128
TOK_FRAME = 192
FR_DEV = 2
REACH = 2
NSEL = 3
SB = 4
DEPTH = 3
MOVED = 2
SPLIT = MOVED * HD
ROWS = FR_DEV * TOK_FRAME
WINDOW = FR_DEV + 2 * REACH
SLOTS = NSEL * TOK_FRAME
BLOCK = TOK_FRAME // SB
SCALE = HD ** (-0.5)
SCALE2 = SCALE * math.log2(math.e)
NEG = -(2.0**100)
NT = (((1,), (1,)), ((), ()))
NN = (((1,), (0,)), ((), ()))
TN = (((0,), (0,)), ((), ()))
MASKS = WINDOW * NSEL
FIRST = MASKS + WINDOW * NSEL * SB * SB
RANK = FIRST + 1
COUNT = FIRST + 2
NOTES = 32
SIDE = FR_DEV * MOVED


def dot(lhs, rhs, dims):
    return lax.dot_general(lhs, rhs, dims, preferred_element_type=jnp.float32)


def column_of(head):
    return slice(head * HD, (head + 1) * HD)


def rows_of(frame):
    return slice(frame * TOK_FRAME, (frame + 1) * TOK_FRAME)


def side_of(table, side):
    return jnp.where(table[RANK] % 2 == 1, side, 2 - side)


def inside(table, place):
    target = table[FIRST] + place
    return (target >= 0) & (target < table[COUNT])


def spot_of(table, frame, slot):
    place = frame + table[(REACH + frame) * NSEL + slot]
    side = (place >= 0).astype(jnp.int32) + (place >= FR_DEV).astype(jnp.int32)
    return side_of(table, side) * FR_DEV + (place + FR_DEV) % FR_DEV


def span(table, frame, slot):
    spot = spot_of(table, frame, slot)
    return pl.ds(pl.multiple_of(spot * TOK_FRAME, TOK_FRAME), TOK_FRAME)


def pair_of(table, query, key):
    index = side_of(table, query // FR_DEV) * FR_DEV + query % FR_DEV
    place = index - REACH
    active = jnp.zeros((), jnp.int32)
    slot = jnp.zeros((), jnp.int32)
    for each in range(NSEL):
        hit = (table[index * NSEL + each] + place == key).astype(jnp.int32)
        active += hit
        slot += hit * each
    active = (active > 0) & inside(table, place)
    return active, MASKS + (index * NSEL + slot) * SB * SB


def write_bias(table, start, seen, bias, row):
    q_block = lax.broadcasted_iota(jnp.int32, (8, TOK_FRAME), 1) // BLOCK
    for k_block in range(SB):
        value = jnp.zeros((8, TOK_FRAME), jnp.float32)
        for block in range(SB):
            keep = (table[start + block * SB + k_block] > 0) & seen
            value = jnp.where(q_block == block, jnp.where(keep, 0.0, NEG), value)
        for step in range(0, BLOCK, 8):
            bias[pl.ds(row + k_block * BLOCK + step, 8), :] = value


def copy_all(pairs, sems):
    moves = [pltpu.make_async_copy(a, b, sems.at[i]) for i, (a, b) in enumerate(pairs)]
    for move in moves:
        move.start()
    return moves


def pack_kernel(queries, grad_out, keys, values, both, k_send, v_send, sems):
    moves = copy_all(
        [
            (queries.at[:, :SPLIT], both.at[0]),
            (grad_out.at[:, :SPLIT], both.at[1]),
            (keys.at[:, SPLIT:], k_send),
            (values.at[:, SPLIT:], v_send),
        ],
        sems,
    )
    for move in moves:
        move.wait()


def stage_kernel(table, *refs):
    arrays, copies, bias, moved_bias, sems = refs[:4], refs[4:8], refs[8], refs[9], refs[10]
    moves = copy_all(list(zip(arrays, copies)), sems)
    for frame in range(FR_DEV):
        for slot in range(NSEL):
            at = (REACH + frame) * NSEL + slot
            seen = inside(table, frame + table[at])
            write_bias(table, MASKS + at * SB * SB, seen, bias.at[frame], slot * TOK_FRAME)
    for query in range(WINDOW):
        for key in range(FR_DEV):
            active, start = pair_of(table, query, key)

            @pl.when(active)
            def _():
                write_bias(table, start, active, moved_bias.at[query, key], 0)

    for move in moves:
        move.wait()


def fill_window(window, one, own, two, column, far_column):
    window[0:ROWS] = one[:, far_column]
    window[ROWS : 2 * ROWS] = own[:, column]
    window[2 * ROWS : 3 * ROWS] = two[:, far_column]


def pick(table, frame, window, chosen):
    for slot in range(NSEL):
        chosen[rows_of(slot)] = window[span(table, frame, slot), :]


def spread(table, frame, accum, parts):
    for slot in range(1, NSEL):
        accum[span(table, frame, slot), :] += parts[rows_of(slot - 1)]


def values_kernel(
    table, queries, grad_out, k_own, bias, k_one, k_two, n_one, n_two,
    chosen_out, prob_out, own_out, one_out, two_out,
    windows, accums,
):
    for head in range(one_out.shape[1] // HD):
        column = column_of(MOVED + head)
        far_column = column_of(head)
        window = windows.at[head % DEPTH]
        accum = accums.at[head % DEPTH]
        fill_window(window, k_one, k_own, k_two, column, far_column)
        accum[...] = jnp.zeros_like(accum)
        for frame in range(FR_DEV):
            chosen = chosen_out.at[head, frame]
            pick(table, frame, window, chosen)
            scores = dot(chosen[...], queries[rows_of(frame), column], NT)
            masked = scores * SCALE2 + bias[frame]
            raised = jnp.exp2(masked - jnp.max(masked, 0, keepdims=True))
            inverse = 1.0 / jnp.sum(raised, 0, keepdims=True)
            prob_low = (raised * inverse).astype(jnp.bfloat16)
            prob_out[head, frame] = prob_low
            far = dot(prob_low[TOK_FRAME:], grad_out[rows_of(frame), column], NN)
            spread(table, frame, accum, far)
        one_out[:ROWS, far_column] = accum[0:ROWS].astype(one_out.dtype)
        own_out[:, far_column] = accum[ROWS : 2 * ROWS]
        two_out[:ROWS, far_column] = accum[2 * ROWS : 3 * ROWS].astype(two_out.dtype)
    write_notes(n_one, one_out)
    write_notes(n_two, two_out)


def keys_kernel(
    table, queries, grad_out, v_own, prob_in, v_one, v_two,
    score_out, own_out, one_out, two_out,
    windows, choices, accums,
):
    for head in range(one_out.shape[1] // HD):
        column = column_of(MOVED + head)
        far_column = column_of(head)
        window = windows.at[head % DEPTH]
        accum = accums.at[head % DEPTH]
        fill_window(window, v_one, v_own, v_two, column, far_column)
        accum[...] = jnp.zeros_like(accum)
        for frame in range(FR_DEV):
            chosen = choices.at[head % DEPTH, frame]
            pick(table, frame, window, chosen)
            grad_prob = dot(chosen[...], grad_out[rows_of(frame), column], NT)
            prob = prob_in[head, frame].astype(jnp.float32)
            delta = jnp.sum(prob * grad_prob, 0, keepdims=True)
            score_low = (prob * (grad_prob - delta)).astype(jnp.bfloat16)
            score_out[head, frame] = score_low
            far = dot(score_low[TOK_FRAME:], queries[rows_of(frame), column], NN)
            spread(table, frame, accum, far)
        one_out[:, far_column] = (accum[0:ROWS] * SCALE).astype(one_out.dtype)
        own_out[:, far_column] = accum[ROWS : 2 * ROWS]
        two_out[:, far_column] = (accum[2 * ROWS : 3 * ROWS] * SCALE).astype(two_out.dtype)


def rest_kernel(
    queries, grad_out, chosen_in, prob_in, score_in, gv_own, gk_own, rv_one, rv_two,
    query_out, value_out, key_out,
):
    for head in range(query_out.shape[1] // HD):
        column = column_of(MOVED + head)
        far_column = column_of(head)
        for frame in range(FR_DEV):
            rows = rows_of(frame)
            score_low = score_in[head, frame]
            grad_query = dot(score_low, chosen_in[head, frame], TN)
            query_out[rows, far_column] = (grad_query * SCALE).astype(query_out.dtype)
            near = dot(score_low[:TOK_FRAME], queries[rows, column], NN)
            key_out[rows, far_column] = (gk_own[rows, far_column] + near) * SCALE
            near = dot(prob_in[head, frame, :TOK_FRAME], grad_out[rows, column], NN)
            total = gv_own[rows, far_column] + near
            total += rv_one[rows, far_column].astype(jnp.float32)
            total += rv_two[rows, far_column].astype(jnp.float32)
            value_out[rows, far_column] = total.astype(value_out.dtype)


def view_of(query, own, one, two, part, head):
    rows = rows_of(query % FR_DEV)
    column = column_of(head)
    if query // FR_DEV == 1:
        return own[rows, column]
    return (one if query < FR_DEV else two)[part, rows, column]


def stats_kernel(
    table, queries, grad_out, keys, values, bias, f_one, f_two,
    masked_out, grad_prob_out, mine_out, one_out, two_out, far_out, other_out,
    parts,
):
    for query in range(WINDOW):
        for key in range(FR_DEV):
            active, _ = pair_of(table, query, key)

            @pl.when(active)
            def _():
                for head in range(MOVED):
                    column = column_of(head)
                    row = slice(query * MOVED + head, query * MOVED + head + 1)
                    rows = rows_of(key)
                    scores = dot(
                        keys[rows, column], view_of(query, queries, f_one, f_two, 0, head), NT
                    )
                    masked = scores * SCALE2 + bias[query, key]
                    highest = rounded(jnp.max(masked, 0, keepdims=True))
                    raised = jnp.exp2(masked - highest)
                    grad_prob = dot(
                        values[rows, column], view_of(query, grad_out, f_one, f_two, 1, head), NT
                    )
                    masked_out[query, key, head] = masked
                    grad_prob_out[query, key, head] = grad_prob
                    parts[key, 0, row] = highest
                    parts[key, 1, row] = jnp.sum(raised, 0, keepdims=True)
                    parts[key, 2, row] = jnp.sum(raised * grad_prob, 0, keepdims=True)

            @pl.when(jnp.logical_not(active))
            def _():
                rows = slice(query * MOVED, (query + 1) * MOVED)
                parts[key, 0, rows] = jnp.full((MOVED, TOK_FRAME), NEG, jnp.float32)
                parts[key, 1, rows] = jnp.zeros((MOVED, TOK_FRAME), jnp.float32)
                parts[key, 2, rows] = jnp.zeros((MOVED, TOK_FRAME), jnp.float32)

    highest, total, moment = joined_stats([parts[key] for key in range(FR_DEV)])
    mine_out[0] = highest
    mine_out[1] = total
    mine_out[2] = moment
    side = SIDE
    rank = table[RANK] % 4
    swapped = (rank == 1) | (rank == 2)
    for out, start in ((one_out, 0), (two_out, side)):
        rows = slice(start, start + 2 * side)
        out[...] = jnp.zeros_like(out)
        notes = (highest[rows], *halves(total[rows]), *halves(moment[rows]))
        for index, note in enumerate(notes):
            out[index * 2 * side : (index + 1) * 2 * side] = note
    for index in range(3):
        whole = mine_out[index]
        far_out[index] = jnp.where(swapped, whole[2 * side :], whole[:side])
        other_out[index] = jnp.where(swapped, whole[:side], whole[2 * side :])


def rounded(array):
    return array.astype(jnp.bfloat16).astype(jnp.float32)


def halves(array):
    high = rounded(array)
    return high, array - high


def write_notes(notes, message):
    for half in range(2):
        message[ROWS:, half * TOK_FRAME : (half + 1) * TOK_FRAME] = notes[
            half * NOTES : (half + 1) * NOTES
        ].astype(message.dtype)


def read_notes(message, notes):
    for half in range(2):
        notes[half * NOTES : (half + 1) * NOTES] = message[
            ROWS:, half * TOK_FRAME : (half + 1) * TOK_FRAME
        ].astype(notes.dtype)
    parts = [notes[i * 2 * SIDE : (i + 1) * 2 * SIDE] for i in range(5)]
    return parts[0], parts[1] + parts[2], parts[3] + parts[4]


def joined_stats(sources):
    tops = [jnp.where(each[1] > 0, each[0], NEG) for each in sources]
    highest = tops[0]
    for top in tops[1:]:
        highest = jnp.maximum(highest, top)
    weights = [jnp.exp2(top - highest) for top in tops]
    total = sum(weight * each[1] for weight, each in zip(weights, sources))
    moment = sum(weight * each[2] for weight, each in zip(weights, sources))
    return highest, total, moment


def finish_pair(query, key, head, masked, grad_probs, logs, deltas):
    row = slice(query * MOVED + head, query * MOVED + head + 1)
    prob = jnp.exp2(masked[query, key, head] - logs[row])
    score_low = (prob * (grad_probs[query, key, head] - deltas[row])).astype(jnp.bfloat16)
    return prob.astype(jnp.bfloat16), score_low


def back_kernel(
    table, keys, masked, grad_probs, mine, r_one, r_two, s_far, s_other,
    prob_out, score_out, logs, deltas, one_out, two_out,
    accums, notes,
):
    side = SIDE
    rank = table[RANK] % 4
    swapped = (rank == 1) | (rank == 2)
    far = [jnp.where(swapped, s_other[i], s_far[i]) for i in range(3)]
    other = [jnp.where(swapped, s_far[i], s_other[i]) for i in range(3)]
    s_one = read_notes(r_one, notes.at[0])
    s_two = read_notes(r_two, notes.at[1])
    s_mine = [mine[i] for i in range(3)]

    def part(stats, start):
        return [each[start : start + side] for each in stats]

    groups = (
        (part(s_mine, 0), part(s_one, side), far),
        (part(s_mine, side), part(s_one, 0), part(s_two, side)),
        (part(s_mine, 2 * side), part(s_two, 0), other),
    )
    for index, sources in enumerate(groups):
        highest, total, moment = joined_stats(sources)
        rows = slice(index * side, (index + 1) * side)
        total = jnp.where(total > 0, total, 1.0)
        logs[rows] = highest + jnp.log2(total)
        deltas[rows] = moment / total
    accums[...] = jnp.zeros_like(accums)
    for query in (0, 1, 4, 5):
        for key in range(FR_DEV):
            active, _ = pair_of(table, query, key)

            @pl.when(active)
            def _():
                for head in range(MOVED):
                    prob_low, score_low = finish_pair(
                        query, key, head, masked, grad_probs, logs, deltas
                    )
                    prob_out[query, key, head] = prob_low
                    score_out[query, key, head] = score_low
                    accums[query // 4, rows_of(query % FR_DEV), column_of(head)] += dot(
                        score_low, keys[rows_of(key), column_of(head)], TN
                    )

    one_out[...] = (accums[0] * SCALE).astype(one_out.dtype)
    two_out[...] = (accums[1] * SCALE).astype(two_out.dtype)


def home_kernel(
    table, queries, grad_out, keys, f_one, f_two, masked, grad_probs, prob_in, score_in,
    logs, deltas,
    query_out, key_out, value_out,
    key_accum, value_accum,
):
    query_out[...] = jnp.zeros_like(query_out)
    key_accum[...] = jnp.zeros_like(key_accum)
    value_accum[...] = jnp.zeros_like(value_accum)
    for query in range(WINDOW):
        for key in range(FR_DEV):
            active, _ = pair_of(table, query, key)

            @pl.when(active)
            def _():
                for head in range(MOVED):
                    column = column_of(head)
                    rows = rows_of(key)
                    if query // FR_DEV == 1:
                        prob_low, score_low = finish_pair(
                            query, key, head, masked, grad_probs, logs, deltas
                        )
                        query_out[rows_of(query % FR_DEV), column] += dot(
                            score_low, keys[rows, column], TN
                        )
                    else:
                        prob_low = prob_in[query, key, head]
                        score_low = score_in[query, key, head]
                    key_accum[rows, column] += dot(
                        score_low, view_of(query, queries, f_one, f_two, 0, head), NN
                    )
                    value_accum[rows, column] += dot(
                        prob_low, view_of(query, grad_out, f_one, f_two, 1, head), NN
                    )

    query_out[...] = query_out[...] * SCALE
    key_out[...] = (key_accum[...] * SCALE).astype(key_out.dtype)
    value_out[...] = value_accum[...].astype(value_out.dtype)


def both_ways(pairs):
    return [pair for i, j in pairs for pair in ((i, j), (j, i))]


def swap(one, two):
    count = lax.axis_size("frames")
    first = [(i, i + 1) for i in range(0, count - 1, 2)]
    second = [(i, i + 1) for i in range(1, count - 1, 2)]
    return (
        lax.ppermute(one, "frames", both_ways(first)),
        lax.ppermute(two, "frames", both_ways(second)),
    )


def swap_far(far, other):
    count = lax.axis_size("frames")
    near = [(i, i + 2) for i in range(count - 2) if i % 4 < 2]
    over = [(i, i + 2) for i in range(count - 2) if i % 4 >= 2]
    far = lax.ppermute(far, "frames", both_ways(near))
    other = lax.ppermute(other, "frames", both_ways(over)) if over else jnp.zeros_like(other)
    return far, other


def lookup(offsets, spatial):
    rank = lax.axis_index("frames")
    first = rank * FR_DEV
    frames = offsets.shape[0]
    around = ((REACH, REACH), (0, 0))
    shifts = lax.dynamic_slice_in_dim(jnp.pad(offsets, around), first, WINDOW, 0)
    blocks = lax.dynamic_slice_in_dim(
        jnp.pad(spatial, around + ((0, 0), (0, 0))), first, WINDOW, 0
    )
    ends = jnp.stack([first, rank, jnp.full_like(rank, frames)]).astype(jnp.int32)
    return jnp.concatenate([shifts.reshape(-1), blocks.reshape(-1), ends])


def call(kernel, name, scalars, arrays, outs, scratch, flops, space=pltpu.VMEM):
    arrays = [pltpu.with_memory_space_constraint(array, space) for array in arrays]
    return pl.pallas_call(
        kernel,
        out_shape=outs,
        in_specs=[pl.BlockSpec(memory_space=pltpu.SMEM)] * len(scalars)
        + [pl.BlockSpec(memory_space=space)] * len(arrays),
        out_specs=tuple(pl.BlockSpec(memory_space=pltpu.VMEM) for _ in outs),
        scratch_shapes=scratch,
        compiler_params=pltpu.CompilerParams(vmem_limit_bytes=16 << 20),
        cost_estimate=pl.CostEstimate(flops=flops, bytes_accessed=0, transcendentals=0),
        name=name,
    )(*scalars, *arrays)


def local(queries, keys, values, grad_out, offsets, spatial):
    width = queries.shape[1]
    heads = width // HD - MOVED

    def low(*shape):
        return pltpu.VMEM(shape, jnp.bfloat16)

    def full(*shape):
        return pltpu.VMEM(shape, jnp.float32)

    unit = 2 * FR_DEV * NSEL * TOK_FRAME * TOK_FRAME * HD
    rest = width - SPLIT
    y_send, k_send, v_send = call(
        pack_kernel, "pack", (), (queries, grad_out, keys, values),
        (low(2, ROWS, SPLIT), low(ROWS, rest), low(ROWS, rest)),
        [pltpu.SemaphoreType.DMA((4,))], unit, pltpu.HBM,
    )
    f_one, f_two = swap(y_send, y_send)
    k_one, k_two = swap(k_send, k_send)
    table = lookup(offsets, spatial)
    query, grad, key, value, bias, moved_bias = call(
        stage_kernel, "stage", (table,), (queries, grad_out, keys, values),
        (low(ROWS, width),) * 4
        + (full(FR_DEV, SLOTS, TOK_FRAME), full(WINDOW, FR_DEV, TOK_FRAME, TOK_FRAME)),
        [pltpu.SemaphoreType.DMA((4,))], unit, pltpu.HBM,
    )
    grid = (WINDOW, FR_DEV, MOVED, TOK_FRAME, TOK_FRAME)
    side = SIDE
    note = full(2 * NOTES, TOK_FRAME)
    masked, grad_probs, mine, n_one, n_two, s_far, s_other = call(
        stats_kernel, "stats", (table,), (query, grad, key, value, moved_bias, f_one, f_two),
        (full(*grid), full(*grid), full(3, 3 * side, TOK_FRAME))
        + (note, note) + (full(3, side, TOK_FRAME),) * 2,
        [full(FR_DEV, 3, 3 * side, TOK_FRAME)], 2 * MOVED * unit,
    )
    s_far, s_other = swap_far(s_far, s_other)
    v_send, mine = lax.optimization_barrier((v_send, mine))
    v_one, v_two = swap(v_send, v_send)
    k_one, k_two, s_far, s_other = lax.optimization_barrier((k_one, k_two, s_far, s_other))
    windows = low(DEPTH, 3 * ROWS, HD)
    accums = full(DEPTH, 3 * ROWS, HD)
    pairs = low(heads, FR_DEV, SLOTS, TOK_FRAME)
    chosen, prob_low, gv_own, gv_one, gv_two = call(
        values_kernel, "values_part", (table,),
        (query, grad, key, bias, k_one, k_two, n_one, n_two),
        (low(heads, FR_DEV, SLOTS, HD), pairs, full(ROWS, rest))
        + (low(ROWS + NOTES, rest),) * 2,
        [windows, accums], 2 * heads * unit,
    )
    rv_one, rv_two = swap(gv_one, gv_two)
    score_low, gk_own, gk_one, gk_two = call(
        keys_kernel, "keys_part", (table,), (query, grad, value, prob_low, v_one, v_two),
        (pairs, full(ROWS, rest), low(ROWS, rest), low(ROWS, rest)),
        [windows, low(DEPTH, FR_DEV, SLOTS, HD), accums], 2 * heads * unit,
    )
    rk_one, rk_two = swap(gk_one, gk_two)
    gk_own, masked = lax.optimization_barrier((gk_own, masked))
    y_prob, y_score, logs, deltas, gq_one, gq_two = call(
        back_kernel, "back", (table,),
        (key, masked, grad_probs, mine, rv_one, rv_two, s_far, s_other),
        (low(*grid), low(*grid), full(3 * side, TOK_FRAME), full(3 * side, TOK_FRAME))
        + (low(ROWS, SPLIT),) * 2,
        [full(2, ROWS, SPLIT), full(2, 2 * NOTES, TOK_FRAME)], MOVED * unit,
    )
    rq_one, rq_two = swap(gq_one, gq_two)
    gq_near, gk_near, gv_near = call(
        home_kernel, "home", (table,),
        (query, grad, key, f_one, f_two, masked, grad_probs, y_prob, y_score, logs, deltas),
        (full(ROWS, SPLIT), low(ROWS, SPLIT), low(ROWS, SPLIT)),
        [full(ROWS, SPLIT), full(ROWS, SPLIT)], 3 * MOVED * unit,
    )
    gq_rest, gv_rest, gk_own = call(
        rest_kernel, "rest", (),
        (query, grad, chosen, prob_low, score_low, gv_own, gk_own, rv_one, rv_two),
        (low(ROWS, rest), low(ROWS, rest), full(ROWS, rest)), [], 2 * heads * unit,
    )

    def joined(own, one, two):
        total = own + one.astype(jnp.float32) + two.astype(jnp.float32)
        return total.astype(jnp.bfloat16)

    grad_queries = jnp.concatenate([joined(gq_near, rq_one, rq_two), gq_rest], 1)
    grad_keys = jnp.concatenate([gk_near, joined(gk_own, rk_one, rk_two)], 1)
    grad_values = jnp.concatenate([gv_near, gv_rest], 1)
    return grad_queries, grad_keys, grad_values


def solution(mesh):
    rows = P(("clips", "frames"), "heads")
    return jax.shard_map(
        local,
        mesh=mesh,
        in_specs=(rows, rows, rows, rows, P("clips", None), P("clips", None, None, None)),
        out_specs=(rows, rows, rows),
        check_vma=False,
    )
```

```python
import math

import jax
import jax.numpy as jnp
from jax import lax
from jax.experimental import pallas as pl
from jax.experimental.pallas import tpu as pltpu
from jax.sharding import PartitionSpec as P

HD = 128
TOK_FRAME = 192
FR_DEV = 2
REACH = 2
NSEL = 3
SB = 4
DEPTH = 3
MOVED = 2
SPLIT = MOVED * HD
ROWS = FR_DEV * TOK_FRAME
WINDOW = FR_DEV + 2 * REACH
SLOTS = NSEL * TOK_FRAME
BLOCK = TOK_FRAME // SB
SCALE = HD ** (-0.5)
SCALE2 = SCALE * math.log2(math.e)
NEG = -(2.0**100)
NT = (((1,), (1,)), ((), ()))
NN = (((1,), (0,)), ((), ()))
TN = (((0,), (0,)), ((), ()))
MASKS = WINDOW * NSEL
FIRST = MASKS + WINDOW * NSEL * SB * SB
RANK = FIRST + 1
COUNT = FIRST + 2
NOTES = 32
SIDE = FR_DEV * MOVED
FAR = (0, 1, 4, 5)


def dot(lhs, rhs, dims):
    return lax.dot_general(lhs, rhs, dims, preferred_element_type=jnp.float32)


def column_of(head):
    return slice(head * HD, (head + 1) * HD)


def rows_of(frame):
    return slice(frame * TOK_FRAME, (frame + 1) * TOK_FRAME)


def side_of(table, side):
    return jnp.where(table[RANK] % 2 == 1, side, 2 - side)


def inside(table, place):
    target = table[FIRST] + place
    return (target >= 0) & (target < table[COUNT])


def spot_of(table, frame, slot):
    place = frame + table[(REACH + frame) * NSEL + slot]
    side = (place >= 0).astype(jnp.int32) + (place >= FR_DEV).astype(jnp.int32)
    return side_of(table, side) * FR_DEV + (place + FR_DEV) % FR_DEV


def span(table, frame, slot):
    spot = spot_of(table, frame, slot)
    return pl.ds(pl.multiple_of(spot * TOK_FRAME, TOK_FRAME), TOK_FRAME)


def pair_of(table, query, key):
    index = side_of(table, query // FR_DEV) * FR_DEV + query % FR_DEV
    place = index - REACH
    active = jnp.zeros((), jnp.int32)
    slot = jnp.zeros((), jnp.int32)
    for each in range(NSEL):
        hit = (table[index * NSEL + each] + place == key).astype(jnp.int32)
        active += hit
        slot += hit * each
    active = (active > 0) & inside(table, place)
    return active, MASKS + (index * NSEL + slot) * SB * SB


def write_bias(table, start, seen, bias, row):
    q_block = lax.broadcasted_iota(jnp.int32, (8, TOK_FRAME), 1) // BLOCK
    for k_block in range(SB):
        value = jnp.zeros((8, TOK_FRAME), jnp.float32)
        for block in range(SB):
            keep = (table[start + block * SB + k_block] > 0) & seen
            value = jnp.where(q_block == block, jnp.where(keep, 0.0, NEG), value)
        for step in range(0, BLOCK, 8):
            bias[pl.ds(row + k_block * BLOCK + step, 8), :] = value


def copy_all(pairs, sems):
    moves = [pltpu.make_async_copy(a, b, sems.at[i]) for i, (a, b) in enumerate(pairs)]
    for move in moves:
        move.start()
    return moves


def pack_kernel(queries, grad_out, keys, values, both, k_send, v_send, sems):
    moves = copy_all(
        [
            (queries.at[:, :SPLIT], both.at[0]),
            (grad_out.at[:, :SPLIT], both.at[1]),
            (keys.at[:, SPLIT:], k_send),
            (values.at[:, SPLIT:], v_send),
        ],
        sems,
    )
    for move in moves:
        move.wait()


def stage_kernel(table, *refs):
    arrays, copies, bias, moved_bias, sems = refs[:4], refs[4:8], refs[8], refs[9], refs[10]
    moves = copy_all(list(zip(arrays, copies)), sems)
    for frame in range(FR_DEV):
        for slot in range(NSEL):
            at = (REACH + frame) * NSEL + slot
            seen = inside(table, frame + table[at])
            write_bias(table, MASKS + at * SB * SB, seen, bias.at[frame], slot * TOK_FRAME)
    for query in range(WINDOW):
        for key in range(FR_DEV):
            active, start = pair_of(table, query, key)

            @pl.when(active)
            def _():
                write_bias(table, start, active, moved_bias.at[query, key], 0)

    for move in moves:
        move.wait()


def fill_window(window, one, own, two, column, far_column):
    window[0:ROWS] = one[:, far_column]
    window[ROWS : 2 * ROWS] = own[:, column]
    window[2 * ROWS : 3 * ROWS] = two[:, far_column]


def pick(table, frame, window, chosen):
    for slot in range(NSEL):
        chosen[rows_of(slot)] = window[span(table, frame, slot), :]


def spread(table, frame, accum, parts):
    for slot in range(1, NSEL):
        accum[span(table, frame, slot), :] += parts[rows_of(slot - 1)]


def values_kernel(
    table, queries, grad_out, k_own, bias, k_one, k_two, n_one, n_two,
    chosen_out, prob_out, own_out, one_out, two_out,
    windows, accums,
):
    for head in range(one_out.shape[1] // HD):
        column = column_of(MOVED + head)
        far_column = column_of(head)
        window = windows.at[head % DEPTH]
        accum = accums.at[head % DEPTH]
        fill_window(window, k_one, k_own, k_two, column, far_column)
        accum[...] = jnp.zeros_like(accum)
        for frame in range(FR_DEV):
            chosen = chosen_out.at[head, frame]
            pick(table, frame, window, chosen)
            scores = dot(chosen[...], queries[rows_of(frame), column], NT)
            masked = scores * SCALE2 + bias[frame]
            raised = jnp.exp2(masked - jnp.max(masked, 0, keepdims=True))
            inverse = 1.0 / jnp.sum(raised, 0, keepdims=True)
            prob_low = (raised * inverse).astype(jnp.bfloat16)
            prob_out[head, frame] = prob_low
            far = dot(prob_low[TOK_FRAME:], grad_out[rows_of(frame), column], NN)
            spread(table, frame, accum, far)
        one_out[:ROWS, far_column] = accum[0:ROWS].astype(one_out.dtype)
        own_out[:, far_column] = accum[ROWS : 2 * ROWS]
        two_out[:ROWS, far_column] = accum[2 * ROWS : 3 * ROWS].astype(two_out.dtype)
    write_notes(n_one, one_out)
    write_notes(n_two, two_out)


def keys_kernel(
    table, queries, grad_out, v_own, prob_in, v_one, v_two,
    score_out, own_out, one_out, two_out,
    windows, choices, accums,
):
    for head in range(one_out.shape[1] // HD):
        column = column_of(MOVED + head)
        far_column = column_of(head)
        window = windows.at[head % DEPTH]
        accum = accums.at[head % DEPTH]
        fill_window(window, v_one, v_own, v_two, column, far_column)
        accum[...] = jnp.zeros_like(accum)
        for frame in range(FR_DEV):
            chosen = choices.at[head % DEPTH, frame]
            pick(table, frame, window, chosen)
            grad_prob = dot(chosen[...], grad_out[rows_of(frame), column], NT)
            prob = prob_in[head, frame].astype(jnp.float32)
            delta = jnp.sum(prob * grad_prob, 0, keepdims=True)
            score_low = (prob * (grad_prob - delta)).astype(jnp.bfloat16)
            score_out[head, frame] = score_low
            far = dot(score_low[TOK_FRAME:], queries[rows_of(frame), column], NN)
            spread(table, frame, accum, far)
        one_out[:, far_column] = (accum[0:ROWS] * SCALE).astype(one_out.dtype)
        own_out[:, far_column] = accum[ROWS : 2 * ROWS]
        two_out[:, far_column] = (accum[2 * ROWS : 3 * ROWS] * SCALE).astype(two_out.dtype)


def rest_kernel(
    queries, grad_out, chosen_in, prob_in, score_in, gv_own, gk_own, rv_one, rv_two,
    query_out, value_out, key_out,
):
    for head in range(query_out.shape[1] // HD):
        column = column_of(MOVED + head)
        far_column = column_of(head)
        for frame in range(FR_DEV):
            rows = rows_of(frame)
            score_low = score_in[head, frame]
            grad_query = dot(score_low, chosen_in[head, frame], TN)
            query_out[rows, far_column] = (grad_query * SCALE).astype(query_out.dtype)
            near = dot(score_low[:TOK_FRAME], queries[rows, column], NN)
            key_out[rows, far_column] = (gk_own[rows, far_column] + near) * SCALE
            near = dot(prob_in[head, frame, :TOK_FRAME], grad_out[rows, column], NN)
            total = gv_own[rows, far_column] + near
            total += rv_one[rows, far_column].astype(jnp.float32)
            total += rv_two[rows, far_column].astype(jnp.float32)
            value_out[rows, far_column] = total.astype(value_out.dtype)


def pair_stats(table, window, key, index, query, grad, keys, values, bias, outs):
    masked_out, grad_prob_out, parts = outs
    active, _ = pair_of(table, window, key)

    @pl.when(active)
    def _():
        for head in range(MOVED):
            column = column_of(head)
            row = slice(index * MOVED + head, index * MOVED + head + 1)
            rows = rows_of(key)
            masked = dot(keys[rows, column], query(head), NT) * SCALE2 + bias[window, key]
            highest = rounded(jnp.max(masked, 0, keepdims=True))
            raised = jnp.exp2(masked - highest)
            grad_prob = dot(values[rows, column], grad(head), NT)
            masked_out[index, key, head] = masked
            grad_prob_out[index, key, head] = grad_prob
            parts[key, 0, row] = highest
            parts[key, 1, row] = jnp.sum(raised, 0, keepdims=True)
            parts[key, 2, row] = jnp.sum(raised * grad_prob, 0, keepdims=True)

    @pl.when(jnp.logical_not(active))
    def _():
        rows = slice(index * MOVED, (index + 1) * MOVED)
        parts[key, 0, rows] = jnp.full((MOVED, TOK_FRAME), NEG, jnp.float32)
        parts[key, 1, rows] = jnp.zeros((MOVED, TOK_FRAME), jnp.float32)
        parts[key, 2, rows] = jnp.zeros((MOVED, TOK_FRAME), jnp.float32)


def own_stats_kernel(
    table, queries, grad_out, keys, values, bias,
    masked_out, grad_prob_out, stats_out,
    parts,
):
    for index in range(FR_DEV):
        for key in range(FR_DEV):
            rows = rows_of(index)
            pair_stats(
                table, FR_DEV + index, key, index,
                lambda head: queries[rows, column_of(head)],
                lambda head: grad_out[rows, column_of(head)],
                keys, values, bias, (masked_out, grad_prob_out, parts),
            )
    for index, each in enumerate(joined_stats([parts[key] for key in range(FR_DEV)])):
        stats_out[index] = each


def stats_kernel(
    table, keys, values, bias, own, f_one, f_two,
    masked_out, grad_prob_out, mine_out, one_out, two_out, far_out, other_out,
    parts,
):
    for index, window in enumerate(FAR):
        sent = f_one if window < FR_DEV else f_two
        for key in range(FR_DEV):
            rows = rows_of(window % FR_DEV)
            pair_stats(
                table, window, key, index,
                lambda head: sent[0, rows, column_of(head)],
                lambda head: sent[1, rows, column_of(head)],
                keys, values, bias, (masked_out, grad_prob_out, parts),
            )
    far = joined_stats([parts[key] for key in range(FR_DEV)])
    rank = table[RANK] % 4
    swapped = (rank == 1) | (rank == 2)
    for index in range(3):
        mine_out[index, :SIDE] = far[index][:SIDE]
        mine_out[index, SIDE : 2 * SIDE] = own[index]
        mine_out[index, 2 * SIDE :] = far[index][SIDE:]
        far_out[index] = jnp.where(swapped, far[index][SIDE:], far[index][:SIDE])
        other_out[index] = jnp.where(swapped, far[index][:SIDE], far[index][SIDE:])
    for out, start in ((one_out, 0), (two_out, SIDE)):
        rows = slice(start, start + 2 * SIDE)
        out[...] = jnp.zeros_like(out)
        notes = (mine_out[0, rows], *halves(mine_out[1, rows]), *halves(mine_out[2, rows]))
        for index, note in enumerate(notes):
            out[index * 2 * SIDE : (index + 1) * 2 * SIDE] = note


def rounded(array):
    return array.astype(jnp.bfloat16).astype(jnp.float32)


def halves(array):
    high = rounded(array)
    return high, array - high


def write_notes(notes, message):
    for half in range(2):
        message[ROWS:, half * TOK_FRAME : (half + 1) * TOK_FRAME] = notes[
            half * NOTES : (half + 1) * NOTES
        ].astype(message.dtype)


def read_notes(message, notes):
    for half in range(2):
        notes[half * NOTES : (half + 1) * NOTES] = message[
            ROWS:, half * TOK_FRAME : (half + 1) * TOK_FRAME
        ].astype(notes.dtype)
    parts = [notes[i * 2 * SIDE : (i + 1) * 2 * SIDE] for i in range(5)]
    return parts[0], parts[1] + parts[2], parts[3] + parts[4]


def joined_stats(sources):
    tops = [jnp.where(each[1] > 0, each[0], NEG) for each in sources]
    highest = tops[0]
    for top in tops[1:]:
        highest = jnp.maximum(highest, top)
    weights = [jnp.exp2(top - highest) for top in tops]
    total = sum(weight * each[1] for weight, each in zip(weights, sources))
    moment = sum(weight * each[2] for weight, each in zip(weights, sources))
    return highest, total, moment


def finish_pair(window, index, key, head, masked, grad_probs, logs, deltas):
    row = slice(window * MOVED + head, window * MOVED + head + 1)
    prob = jnp.exp2(masked[index, key, head] - logs[row])
    score_low = (prob * (grad_probs[index, key, head] - deltas[row])).astype(jnp.bfloat16)
    return prob.astype(jnp.bfloat16), score_low


def back_kernel(
    table, keys, masked, grad_probs, mine, r_one, r_two, s_far, s_other,
    prob_out, score_out, logs, deltas, one_out, two_out,
    accums, notes,
):
    side = SIDE
    rank = table[RANK] % 4
    swapped = (rank == 1) | (rank == 2)
    far = [jnp.where(swapped, s_other[i], s_far[i]) for i in range(3)]
    other = [jnp.where(swapped, s_far[i], s_other[i]) for i in range(3)]
    s_one = read_notes(r_one, notes.at[0])
    s_two = read_notes(r_two, notes.at[1])
    s_mine = [mine[i] for i in range(3)]

    def part(stats, start):
        return [each[start : start + side] for each in stats]

    groups = (
        (part(s_mine, 0), part(s_one, side), far),
        (part(s_mine, side), part(s_one, 0), part(s_two, side)),
        (part(s_mine, 2 * side), part(s_two, 0), other),
    )
    for index, sources in enumerate(groups):
        highest, total, moment = joined_stats(sources)
        rows = slice(index * side, (index + 1) * side)
        total = jnp.where(total > 0, total, 1.0)
        logs[rows] = highest + jnp.log2(total)
        deltas[rows] = moment / total
    accums[...] = jnp.zeros_like(accums)
    for index, window in enumerate(FAR):
        for key in range(FR_DEV):
            active, _ = pair_of(table, window, key)

            @pl.when(active)
            def _():
                for head in range(MOVED):
                    prob_low, score_low = finish_pair(
                        window, index, key, head, masked, grad_probs, logs, deltas
                    )
                    prob_out[index, key, head] = prob_low
                    score_out[index, key, head] = score_low
                    accums[index // FR_DEV, rows_of(index % FR_DEV), column_of(head)] += dot(
                        score_low, keys[rows_of(key), column_of(head)], TN
                    )

    one_out[...] = (accums[0] * SCALE).astype(one_out.dtype)
    two_out[...] = (accums[1] * SCALE).astype(two_out.dtype)


def home_kernel(
    table, queries, grad_out, keys, f_one, f_two, masked, grad_probs, prob_in, score_in,
    logs, deltas,
    query_out, key_out, value_out,
    key_accum, value_accum,
):
    query_out[...] = jnp.zeros_like(query_out)
    key_accum[...] = jnp.zeros_like(key_accum)
    value_accum[...] = jnp.zeros_like(value_accum)
    for window in range(WINDOW):
        rows = rows_of(window % FR_DEV)
        near = window // FR_DEV == 1
        sent = f_one if window < FR_DEV else f_two
        for key in range(FR_DEV):
            active, _ = pair_of(table, window, key)

            @pl.when(active)
            def _():
                for head in range(MOVED):
                    column = column_of(head)
                    if near:
                        query = queries[rows, column]
                        grad = grad_out[rows, column]
                        prob_low, score_low = finish_pair(
                            window, window - FR_DEV, key, head, masked, grad_probs, logs, deltas
                        )
                        query_out[rows, column] += dot(
                            score_low, keys[rows_of(key), column], TN
                        )
                    else:
                        query = sent[0, rows, column]
                        grad = sent[1, rows, column]
                        prob_low = prob_in[FAR.index(window), key, head]
                        score_low = score_in[FAR.index(window), key, head]
                    key_accum[rows_of(key), column] += dot(score_low, query, NN)
                    value_accum[rows_of(key), column] += dot(prob_low, grad, NN)

    query_out[...] = query_out[...] * SCALE
    key_out[...] = (key_accum[...] * SCALE).astype(key_out.dtype)
    value_out[...] = value_accum[...].astype(value_out.dtype)


def both_ways(pairs):
    return [pair for i, j in pairs for pair in ((i, j), (j, i))]


def swap(one, two):
    count = lax.axis_size("frames")
    first = [(i, i + 1) for i in range(0, count - 1, 2)]
    second = [(i, i + 1) for i in range(1, count - 1, 2)]
    return (
        lax.ppermute(one, "frames", both_ways(first)),
        lax.ppermute(two, "frames", both_ways(second)),
    )


def swap_far(far, other):
    count = lax.axis_size("frames")
    near = [(i, i + 2) for i in range(count - 2) if i % 4 < 2]
    over = [(i, i + 2) for i in range(count - 2) if i % 4 >= 2]
    far = lax.ppermute(far, "frames", both_ways(near))
    other = lax.ppermute(other, "frames", both_ways(over)) if over else jnp.zeros_like(other)
    return far, other


def lookup(offsets, spatial):
    rank = lax.axis_index("frames")
    first = rank * FR_DEV
    frames = offsets.shape[0]
    around = ((REACH, REACH), (0, 0))
    shifts = lax.dynamic_slice_in_dim(jnp.pad(offsets, around), first, WINDOW, 0)
    blocks = lax.dynamic_slice_in_dim(
        jnp.pad(spatial, around + ((0, 0), (0, 0))), first, WINDOW, 0
    )
    ends = jnp.stack([first, rank, jnp.full_like(rank, frames)]).astype(jnp.int32)
    return jnp.concatenate([shifts.reshape(-1), blocks.reshape(-1), ends])


def call(kernel, name, scalars, arrays, outs, scratch, flops, space=pltpu.VMEM):
    arrays = [pltpu.with_memory_space_constraint(array, space) for array in arrays]
    return pl.pallas_call(
        kernel,
        out_shape=outs,
        in_specs=[pl.BlockSpec(memory_space=pltpu.SMEM)] * len(scalars)
        + [pl.BlockSpec(memory_space=space)] * len(arrays),
        out_specs=tuple(pl.BlockSpec(memory_space=pltpu.VMEM) for _ in outs),
        scratch_shapes=scratch,
        compiler_params=pltpu.CompilerParams(vmem_limit_bytes=16 << 20),
        cost_estimate=pl.CostEstimate(flops=flops, bytes_accessed=0, transcendentals=0),
        name=name,
    )(*scalars, *arrays)


def local(queries, keys, values, grad_out, offsets, spatial):
    width = queries.shape[1]
    heads = width // HD - MOVED

    def low(*shape):
        return pltpu.VMEM(shape, jnp.bfloat16)

    def full(*shape):
        return pltpu.VMEM(shape, jnp.float32)

    unit = 2 * FR_DEV * NSEL * TOK_FRAME * TOK_FRAME * HD
    rest = width - SPLIT
    y_send, k_send, v_send = call(
        pack_kernel, "pack", (), (queries, grad_out, keys, values),
        (low(2, ROWS, SPLIT), low(ROWS, rest), low(ROWS, rest)),
        [pltpu.SemaphoreType.DMA((4,))], unit, pltpu.HBM,
    )
    f_one, f_two = swap(y_send, y_send)
    k_one, k_two = swap(k_send, k_send)
    table = lookup(offsets, spatial)
    query, grad, key, value, bias, moved_bias = call(
        stage_kernel, "stage", (table,), (queries, grad_out, keys, values),
        (low(ROWS, width),) * 4
        + (full(FR_DEV, SLOTS, TOK_FRAME), full(WINDOW, FR_DEV, TOK_FRAME, TOK_FRAME)),
        [pltpu.SemaphoreType.DMA((4,))], unit, pltpu.HBM,
    )
    near_grid = (FR_DEV, FR_DEV, MOVED, TOK_FRAME, TOK_FRAME)
    far_grid = (len(FAR), FR_DEV, MOVED, TOK_FRAME, TOK_FRAME)
    near_masked, near_grads, own_stats = call(
        own_stats_kernel, "own_stats", (table,), (query, grad, key, value, moved_bias),
        (full(*near_grid), full(*near_grid), full(3, SIDE, TOK_FRAME)),
        [full(FR_DEV, 3, SIDE, TOK_FRAME)], MOVED * unit,
    )
    v_send, f_one, f_two, own_stats = lax.optimization_barrier(
        (v_send, f_one, f_two, own_stats)
    )
    v_one, v_two = swap(v_send, v_send)
    note = full(2 * NOTES, TOK_FRAME)
    masked, grad_probs, mine, n_one, n_two, s_far, s_other = call(
        stats_kernel, "stats", (table,), (key, value, moved_bias, own_stats, f_one, f_two),
        (full(*far_grid), full(*far_grid), full(3, 3 * SIDE, TOK_FRAME), note, note)
        + (full(3, SIDE, TOK_FRAME),) * 2,
        [full(FR_DEV, 3, 2 * SIDE, TOK_FRAME)], 2 * MOVED * unit,
    )
    s_far, s_other = swap_far(s_far, s_other)
    windows = low(DEPTH, 3 * ROWS, HD)
    accums = full(DEPTH, 3 * ROWS, HD)
    pairs = low(heads, FR_DEV, SLOTS, TOK_FRAME)
    chosen, prob_low, gv_own, gv_one, gv_two = call(
        values_kernel, "values_part", (table,),
        (query, grad, key, bias, k_one, k_two, n_one, n_two),
        (low(heads, FR_DEV, SLOTS, HD), pairs, full(ROWS, rest))
        + (low(ROWS + NOTES, rest),) * 2,
        [windows, accums], 2 * heads * unit,
    )
    rv_one, rv_two = swap(gv_one, gv_two)
    score_low, gk_own, gk_one, gk_two = call(
        keys_kernel, "keys_part", (table,), (query, grad, value, prob_low, v_one, v_two),
        (pairs, full(ROWS, rest), low(ROWS, rest), low(ROWS, rest)),
        [windows, low(DEPTH, FR_DEV, SLOTS, HD), accums], 2 * heads * unit,
    )
    gk_one, gk_two, s_far, s_other = lax.optimization_barrier((gk_one, gk_two, s_far, s_other))
    rk_one, rk_two = swap(gk_one, gk_two)
    gk_own, masked = lax.optimization_barrier((gk_own, masked))
    y_prob, y_score, logs, deltas, gq_one, gq_two = call(
        back_kernel, "back", (table,),
        (key, masked, grad_probs, mine, rv_one, rv_two, s_far, s_other),
        (low(*far_grid), low(*far_grid)) + (full(3 * SIDE, TOK_FRAME),) * 2
        + (low(ROWS, SPLIT),) * 2,
        [full(2, ROWS, SPLIT), full(2, 2 * NOTES, TOK_FRAME)], MOVED * unit,
    )
    rq_one, rq_two = swap(gq_one, gq_two)
    gq_near, gk_near, gv_near = call(
        home_kernel, "home", (table,),
        (query, grad, key, f_one, f_two, near_masked, near_grads, y_prob, y_score, logs, deltas),
        (full(ROWS, SPLIT), low(ROWS, SPLIT), low(ROWS, SPLIT)),
        [full(ROWS, SPLIT), full(ROWS, SPLIT)], 3 * MOVED * unit,
    )
    gq_rest, gv_rest, gk_own = call(
        rest_kernel, "rest", (),
        (query, grad, chosen, prob_low, score_low, gv_own, gk_own, rv_one, rv_two),
        (low(ROWS, rest), low(ROWS, rest), full(ROWS, rest)), [], 2 * heads * unit,
    )

    def joined(own, one, two):
        total = own + one.astype(jnp.float32) + two.astype(jnp.float32)
        return total.astype(jnp.bfloat16)

    grad_keys = jnp.concatenate([gk_near, joined(gk_own, rk_one, rk_two)], 1)
    grad_keys, gq_near = lax.optimization_barrier((grad_keys, gq_near))
    grad_queries = jnp.concatenate([joined(gq_near, rq_one, rq_two), gq_rest], 1)
    grad_values = jnp.concatenate([gv_near, gv_rest], 1)
    return grad_queries, grad_keys, grad_values


def solution(mesh):
    rows = P(("clips", "frames"), "heads")
    return jax.shard_map(
        local,
        mesh=mesh,
        in_specs=(rows, rows, rows, rows, P("clips", None), P("clips", None, None, None)),
        out_specs=(rows, rows, rows),
        check_vma=False,
    )
```

```python
import math

import jax
import jax.numpy as jnp
from jax import lax
from jax.experimental import pallas as pl
from jax.experimental.pallas import tpu as pltpu
from jax.sharding import PartitionSpec as P

HD = 128
TOK_FRAME = 192
FR_DEV = 2
REACH = 2
NSEL = 3
SB = 4
DEPTH = 3
MOVED = 2
SPLIT = MOVED * HD
ROWS = FR_DEV * TOK_FRAME
WINDOW = FR_DEV + 2 * REACH
SLOTS = NSEL * TOK_FRAME
BLOCK = TOK_FRAME // SB
SCALE = HD ** (-0.5)
SCALE2 = SCALE * math.log2(math.e)
NEG = -(2.0**100)
NT = (((1,), (1,)), ((), ()))
NN = (((1,), (0,)), ((), ()))
TN = (((0,), (0,)), ((), ()))
MASKS = WINDOW * NSEL
FIRST = MASKS + WINDOW * NSEL * SB * SB
RANK = FIRST + 1
COUNT = FIRST + 2
NOTES = 32
SIDE = FR_DEV * MOVED
FAR = (0, 1, 4, 5)


def dot(lhs, rhs, dims):
    return lax.dot_general(lhs, rhs, dims, preferred_element_type=jnp.float32)


def column_of(head):
    return slice(head * HD, (head + 1) * HD)


def rows_of(frame):
    return slice(frame * TOK_FRAME, (frame + 1) * TOK_FRAME)


def side_of(table, side):
    return jnp.where(table[RANK] % 2 == 1, side, 2 - side)


def inside(table, place):
    target = table[FIRST] + place
    return (target >= 0) & (target < table[COUNT])


def spot_of(table, frame, slot):
    place = frame + table[(REACH + frame) * NSEL + slot]
    side = (place >= 0).astype(jnp.int32) + (place >= FR_DEV).astype(jnp.int32)
    return side_of(table, side) * FR_DEV + (place + FR_DEV) % FR_DEV


def span(table, frame, slot):
    spot = spot_of(table, frame, slot)
    return pl.ds(pl.multiple_of(spot * TOK_FRAME, TOK_FRAME), TOK_FRAME)


def pair_of(table, query, key):
    index = side_of(table, query // FR_DEV) * FR_DEV + query % FR_DEV
    place = index - REACH
    active = jnp.zeros((), jnp.int32)
    slot = jnp.zeros((), jnp.int32)
    for each in range(NSEL):
        hit = (table[index * NSEL + each] + place == key).astype(jnp.int32)
        active += hit
        slot += hit * each
    active = (active > 0) & inside(table, place)
    return active, MASKS + (index * NSEL + slot) * SB * SB


def write_bias(table, start, seen, bias, row):
    q_block = lax.broadcasted_iota(jnp.int32, (8, TOK_FRAME), 1) // BLOCK
    for k_block in range(SB):
        value = jnp.zeros((8, TOK_FRAME), jnp.float32)
        for block in range(SB):
            keep = (table[start + block * SB + k_block] > 0) & seen
            value = jnp.where(q_block == block, jnp.where(keep, 0.0, NEG), value)
        for step in range(0, BLOCK, 8):
            bias[pl.ds(row + k_block * BLOCK + step, 8), :] = value


def copy_all(pairs, sems):
    moves = [pltpu.make_async_copy(a, b, sems.at[i]) for i, (a, b) in enumerate(pairs)]
    for move in moves:
        move.start()
    return moves


def pack_kernel(queries, grad_out, keys, values, both, k_send, v_send, sems):
    moves = copy_all(
        [
            (queries.at[:, :SPLIT], both.at[0]),
            (grad_out.at[:, :SPLIT], both.at[1]),
            (keys.at[:, SPLIT:], k_send),
            (values.at[:, SPLIT:], v_send),
        ],
        sems,
    )
    for move in moves:
        move.wait()


def stage_kernel(table, *refs):
    arrays, copies, bias, moved_bias, sems = refs[:4], refs[4:8], refs[8], refs[9], refs[10]
    moves = copy_all(list(zip(arrays, copies)), sems)
    for frame in range(FR_DEV):
        for slot in range(NSEL):
            at = (REACH + frame) * NSEL + slot
            seen = inside(table, frame + table[at])
            write_bias(table, MASKS + at * SB * SB, seen, bias.at[frame], slot * TOK_FRAME)
    for query in range(WINDOW):
        for key in range(FR_DEV):
            active, start = pair_of(table, query, key)

            @pl.when(active)
            def _():
                write_bias(table, start, active, moved_bias.at[query, key], 0)

    for move in moves:
        move.wait()


def fill_window(window, one, own, two, column, far_column):
    window[0:ROWS] = one[:, far_column]
    window[ROWS : 2 * ROWS] = own[:, column]
    window[2 * ROWS : 3 * ROWS] = two[:, far_column]


def pick(table, frame, window, chosen):
    for slot in range(NSEL):
        chosen[rows_of(slot)] = window[span(table, frame, slot), :]


def spread(table, frame, accum, parts):
    for slot in range(1, NSEL):
        accum[span(table, frame, slot), :] += parts[rows_of(slot - 1)]


def values_kernel(
    table, queries, grad_out, k_own, bias, k_one, k_two, n_one, n_two,
    chosen_out, prob_out, own_out, one_out, two_out,
    windows, accums,
):
    for head in range(one_out.shape[1] // HD):
        column = column_of(MOVED + head)
        far_column = column_of(head)
        window = windows.at[head % DEPTH]
        accum = accums.at[head % DEPTH]
        fill_window(window, k_one, k_own, k_two, column, far_column)
        accum[...] = jnp.zeros_like(accum)
        for frame in range(FR_DEV):
            chosen = chosen_out.at[head, frame]
            pick(table, frame, window, chosen)
            scores = dot(chosen[...], queries[rows_of(frame), column], NT)
            masked = scores * SCALE2 + bias[frame]
            raised = jnp.exp2(masked - jnp.max(masked, 0, keepdims=True))
            inverse = 1.0 / jnp.sum(raised, 0, keepdims=True)
            prob_low = (raised * inverse).astype(jnp.bfloat16)
            prob_out[head, frame] = prob_low
            far = dot(prob_low[TOK_FRAME:], grad_out[rows_of(frame), column], NN)
            spread(table, frame, accum, far)
        one_out[:ROWS, far_column] = accum[0:ROWS].astype(one_out.dtype)
        own_out[:, far_column] = accum[ROWS : 2 * ROWS]
        two_out[:ROWS, far_column] = accum[2 * ROWS : 3 * ROWS].astype(two_out.dtype)
    write_notes(n_one, one_out)
    write_notes(n_two, two_out)


def keys_kernel(
    table, queries, grad_out, v_own, prob_in, v_one, v_two,
    score_out, own_out, one_out, two_out,
    windows, choices, accums,
):
    for head in range(one_out.shape[1] // HD):
        column = column_of(MOVED + head)
        far_column = column_of(head)
        window = windows.at[head % DEPTH]
        accum = accums.at[head % DEPTH]
        fill_window(window, v_one, v_own, v_two, column, far_column)
        accum[...] = jnp.zeros_like(accum)
        for frame in range(FR_DEV):
            chosen = choices.at[head % DEPTH, frame]
            pick(table, frame, window, chosen)
            grad_prob = dot(chosen[...], grad_out[rows_of(frame), column], NT)
            prob = prob_in[head, frame].astype(jnp.float32)
            delta = jnp.sum(prob * grad_prob, 0, keepdims=True)
            score_low = (prob * (grad_prob - delta)).astype(jnp.bfloat16)
            score_out[head, frame] = score_low
            far = dot(score_low[TOK_FRAME:], queries[rows_of(frame), column], NN)
            spread(table, frame, accum, far)
        one_out[:, far_column] = (accum[0:ROWS] * SCALE).astype(one_out.dtype)
        own_out[:, far_column] = accum[ROWS : 2 * ROWS]
        two_out[:, far_column] = (accum[2 * ROWS : 3 * ROWS] * SCALE).astype(two_out.dtype)


def rest_kernel(
    queries, grad_out, chosen_in, prob_in, score_in, gv_own, gk_own,
    query_out, value_out, key_out,
):
    for head in range(query_out.shape[1] // HD):
        column = column_of(MOVED + head)
        far_column = column_of(head)
        for frame in range(FR_DEV):
            rows = rows_of(frame)
            score_low = score_in[head, frame]
            grad_query = dot(score_low, chosen_in[head, frame], TN)
            query_out[rows, far_column] = (grad_query * SCALE).astype(query_out.dtype)
            near = dot(score_low[:TOK_FRAME], queries[rows, column], NN)
            key_out[rows, far_column] = (gk_own[rows, far_column] + near) * SCALE
            near = dot(prob_in[head, frame, :TOK_FRAME], grad_out[rows, column], NN)
            value_out[rows, far_column] = gv_own[rows, far_column] + near


def joined(own, one, two):
    total = own[...] + one[...].astype(jnp.float32) + two[...].astype(jnp.float32)
    return total.astype(jnp.bfloat16)


def last_kernel(
    gq_rest, gk_near, gq_near, rq_one, rq_two, gk_own, rk_one, rk_two,
    query_out, key_out,
    query_done, key_done, sems,
):
    moves = copy_all(
        [(gq_rest, query_out.at[:, SPLIT:]), (gk_near, key_out.at[:, :SPLIT])], sems
    )
    key_done[...] = joined(gk_own, rk_one, rk_two)
    moves += copy_all([(key_done, key_out.at[:, SPLIT:])], sems.at[2:3])
    query_done[...] = joined(gq_near, rq_one, rq_two)
    moves += copy_all([(query_done, query_out.at[:, :SPLIT])], sems.at[3:4])
    for move in moves:
        move.wait()


def pair_stats(table, window, key, index, query, grad, keys, values, bias, outs):
    masked_out, grad_prob_out, parts = outs
    active, _ = pair_of(table, window, key)

    @pl.when(active)
    def _():
        for head in range(MOVED):
            column = column_of(head)
            row = slice(index * MOVED + head, index * MOVED + head + 1)
            rows = rows_of(key)
            masked = dot(keys[rows, column], query(head), NT) * SCALE2 + bias[window, key]
            highest = rounded(jnp.max(masked, 0, keepdims=True))
            raised = jnp.exp2(masked - highest)
            grad_prob = dot(values[rows, column], grad(head), NT)
            masked_out[index, key, head] = masked
            grad_prob_out[index, key, head] = grad_prob
            parts[key, 0, row] = highest
            parts[key, 1, row] = jnp.sum(raised, 0, keepdims=True)
            parts[key, 2, row] = jnp.sum(raised * grad_prob, 0, keepdims=True)

    @pl.when(jnp.logical_not(active))
    def _():
        rows = slice(index * MOVED, (index + 1) * MOVED)
        parts[key, 0, rows] = jnp.full((MOVED, TOK_FRAME), NEG, jnp.float32)
        parts[key, 1, rows] = jnp.zeros((MOVED, TOK_FRAME), jnp.float32)
        parts[key, 2, rows] = jnp.zeros((MOVED, TOK_FRAME), jnp.float32)


def own_stats_kernel(
    table, queries, grad_out, keys, values, bias,
    masked_out, grad_prob_out, stats_out,
    parts,
):
    for index in range(FR_DEV):
        for key in range(FR_DEV):
            rows = rows_of(index)
            pair_stats(
                table, FR_DEV + index, key, index,
                lambda head: queries[rows, column_of(head)],
                lambda head: grad_out[rows, column_of(head)],
                keys, values, bias, (masked_out, grad_prob_out, parts),
            )
    for index, each in enumerate(joined_stats([parts[key] for key in range(FR_DEV)])):
        stats_out[index] = each


def stats_kernel(
    table, keys, values, bias, own, f_one, f_two,
    masked_out, grad_prob_out, mine_out, one_out, two_out, far_out, other_out,
    parts,
):
    for index, window in enumerate(FAR):
        sent = f_one if window < FR_DEV else f_two
        for key in range(FR_DEV):
            rows = rows_of(window % FR_DEV)
            pair_stats(
                table, window, key, index,
                lambda head: sent[0, rows, column_of(head)],
                lambda head: sent[1, rows, column_of(head)],
                keys, values, bias, (masked_out, grad_prob_out, parts),
            )
    far = joined_stats([parts[key] for key in range(FR_DEV)])
    rank = table[RANK] % 4
    swapped = (rank == 1) | (rank == 2)
    for index in range(3):
        mine_out[index, :SIDE] = far[index][:SIDE]
        mine_out[index, SIDE : 2 * SIDE] = own[index]
        mine_out[index, 2 * SIDE :] = far[index][SIDE:]
        far_out[index] = jnp.where(swapped, far[index][SIDE:], far[index][:SIDE])
        other_out[index] = jnp.where(swapped, far[index][:SIDE], far[index][SIDE:])
    for out, start in ((one_out, 0), (two_out, SIDE)):
        rows = slice(start, start + 2 * SIDE)
        out[...] = jnp.zeros_like(out)
        notes = (mine_out[0, rows], *halves(mine_out[1, rows]), *halves(mine_out[2, rows]))
        for index, note in enumerate(notes):
            out[index * 2 * SIDE : (index + 1) * 2 * SIDE] = note


def rounded(array):
    return array.astype(jnp.bfloat16).astype(jnp.float32)


def halves(array):
    high = rounded(array)
    return high, array - high


def write_notes(notes, message):
    for half in range(2):
        message[ROWS:, half * TOK_FRAME : (half + 1) * TOK_FRAME] = notes[
            half * NOTES : (half + 1) * NOTES
        ].astype(message.dtype)


def read_notes(message, notes):
    for half in range(2):
        notes[half * NOTES : (half + 1) * NOTES] = message[
            ROWS:, half * TOK_FRAME : (half + 1) * TOK_FRAME
        ].astype(notes.dtype)
    parts = [notes[i * 2 * SIDE : (i + 1) * 2 * SIDE] for i in range(5)]
    return parts[0], parts[1] + parts[2], parts[3] + parts[4]


def joined_stats(sources):
    tops = [jnp.where(each[1] > 0, each[0], NEG) for each in sources]
    highest = tops[0]
    for top in tops[1:]:
        highest = jnp.maximum(highest, top)
    weights = [jnp.exp2(top - highest) for top in tops]
    total = sum(weight * each[1] for weight, each in zip(weights, sources))
    moment = sum(weight * each[2] for weight, each in zip(weights, sources))
    return highest, total, moment


def finish_pair(window, index, key, head, masked, grad_probs, logs, deltas):
    row = slice(window * MOVED + head, window * MOVED + head + 1)
    prob = jnp.exp2(masked[index, key, head] - logs[row])
    score_low = (prob * (grad_probs[index, key, head] - deltas[row])).astype(jnp.bfloat16)
    return prob.astype(jnp.bfloat16), score_low


def back_kernel(
    table, keys, masked, grad_probs, mine, r_one, r_two, s_far, s_other,
    prob_out, score_out, logs, deltas, one_out, two_out,
    accums, notes,
):
    side = SIDE
    rank = table[RANK] % 4
    swapped = (rank == 1) | (rank == 2)
    far = [jnp.where(swapped, s_other[i], s_far[i]) for i in range(3)]
    other = [jnp.where(swapped, s_far[i], s_other[i]) for i in range(3)]
    s_one = read_notes(r_one, notes.at[0])
    s_two = read_notes(r_two, notes.at[1])
    s_mine = [mine[i] for i in range(3)]

    def part(stats, start):
        return [each[start : start + side] for each in stats]

    groups = (
        (part(s_mine, 0), part(s_one, side), far),
        (part(s_mine, side), part(s_one, 0), part(s_two, side)),
        (part(s_mine, 2 * side), part(s_two, 0), other),
    )
    for index, sources in enumerate(groups):
        highest, total, moment = joined_stats(sources)
        rows = slice(index * side, (index + 1) * side)
        total = jnp.where(total > 0, total, 1.0)
        logs[rows] = highest + jnp.log2(total)
        deltas[rows] = moment / total
    accums[...] = jnp.zeros_like(accums)
    for index, window in enumerate(FAR):
        for key in range(FR_DEV):
            active, _ = pair_of(table, window, key)

            @pl.when(active)
            def _():
                for head in range(MOVED):
                    prob_low, score_low = finish_pair(
                        window, index, key, head, masked, grad_probs, logs, deltas
                    )
                    prob_out[index, key, head] = prob_low
                    score_out[index, key, head] = score_low
                    accums[index // FR_DEV, rows_of(index % FR_DEV), column_of(head)] += dot(
                        score_low, keys[rows_of(key), column_of(head)], TN
                    )

    one_out[...] = (accums[0] * SCALE).astype(one_out.dtype)
    two_out[...] = (accums[1] * SCALE).astype(two_out.dtype)


def home_kernel(
    table, queries, grad_out, keys, f_one, f_two, masked, grad_probs, prob_in, score_in,
    logs, deltas,
    query_out, key_out, value_out,
    key_accum, value_accum,
):
    query_out[...] = jnp.zeros_like(query_out)
    key_accum[...] = jnp.zeros_like(key_accum)
    value_accum[...] = jnp.zeros_like(value_accum)
    for window in range(WINDOW):
        rows = rows_of(window % FR_DEV)
        near = window // FR_DEV == 1
        sent = f_one if window < FR_DEV else f_two
        for key in range(FR_DEV):
            active, _ = pair_of(table, window, key)

            @pl.when(active)
            def _():
                for head in range(MOVED):
                    column = column_of(head)
                    if near:
                        query = queries[rows, column]
                        grad = grad_out[rows, column]
                        prob_low, score_low = finish_pair(
                            window, window - FR_DEV, key, head, masked, grad_probs, logs, deltas
                        )
                        query_out[rows, column] += dot(
                            score_low, keys[rows_of(key), column], TN
                        )
                    else:
                        query = sent[0, rows, column]
                        grad = sent[1, rows, column]
                        prob_low = prob_in[FAR.index(window), key, head]
                        score_low = score_in[FAR.index(window), key, head]
                    key_accum[rows_of(key), column] += dot(score_low, query, NN)
                    value_accum[rows_of(key), column] += dot(prob_low, grad, NN)

    query_out[...] = query_out[...] * SCALE
    key_out[...] = (key_accum[...] * SCALE).astype(key_out.dtype)
    value_out[...] = value_accum[...].astype(value_out.dtype)


def both_ways(pairs):
    return [pair for i, j in pairs for pair in ((i, j), (j, i))]


def swap(one, two):
    count = lax.axis_size("frames")
    first = [(i, i + 1) for i in range(0, count - 1, 2)]
    second = [(i, i + 1) for i in range(1, count - 1, 2)]
    return (
        lax.ppermute(one, "frames", both_ways(first)),
        lax.ppermute(two, "frames", both_ways(second)),
    )


def swap_far(far, other):
    count = lax.axis_size("frames")
    near = [(i, i + 2) for i in range(count - 2) if i % 4 < 2]
    over = [(i, i + 2) for i in range(count - 2) if i % 4 >= 2]
    far = lax.ppermute(far, "frames", both_ways(near))
    other = lax.ppermute(other, "frames", both_ways(over)) if over else jnp.zeros_like(other)
    return far, other


def lookup(offsets, spatial):
    rank = lax.axis_index("frames")
    first = rank * FR_DEV
    frames = offsets.shape[0]
    around = ((REACH, REACH), (0, 0))
    shifts = lax.dynamic_slice_in_dim(jnp.pad(offsets, around), first, WINDOW, 0)
    blocks = lax.dynamic_slice_in_dim(
        jnp.pad(spatial, around + ((0, 0), (0, 0))), first, WINDOW, 0
    )
    ends = jnp.stack([first, rank, jnp.full_like(rank, frames)]).astype(jnp.int32)
    return jnp.concatenate([shifts.reshape(-1), blocks.reshape(-1), ends])


def call(kernel, name, scalars, arrays, outs, scratch, flops, space=pltpu.VMEM, out_space=pltpu.VMEM):
    arrays = [pltpu.with_memory_space_constraint(array, space) for array in arrays]
    return pl.pallas_call(
        kernel,
        out_shape=outs,
        in_specs=[pl.BlockSpec(memory_space=pltpu.SMEM)] * len(scalars)
        + [pl.BlockSpec(memory_space=space)] * len(arrays),
        out_specs=tuple(pl.BlockSpec(memory_space=out_space) for _ in outs),
        scratch_shapes=scratch,
        compiler_params=pltpu.CompilerParams(vmem_limit_bytes=16 << 20),
        cost_estimate=pl.CostEstimate(flops=flops, bytes_accessed=0, transcendentals=0),
        name=name,
    )(*scalars, *arrays)


def local(queries, keys, values, grad_out, offsets, spatial):
    width = queries.shape[1]
    heads = width // HD - MOVED

    def low(*shape):
        return pltpu.VMEM(shape, jnp.bfloat16)

    def full(*shape):
        return pltpu.VMEM(shape, jnp.float32)

    unit = 2 * FR_DEV * NSEL * TOK_FRAME * TOK_FRAME * HD
    rest = width - SPLIT
    y_send, k_send, v_send = call(
        pack_kernel, "pack", (), (queries, grad_out, keys, values),
        (low(2, ROWS, SPLIT), low(ROWS, rest), low(ROWS, rest)),
        [pltpu.SemaphoreType.DMA((4,))], unit, pltpu.HBM,
    )
    f_one, f_two = swap(y_send, y_send)
    k_one, k_two = swap(k_send, k_send)
    table = lookup(offsets, spatial)
    query, grad, key, value, bias, moved_bias = call(
        stage_kernel, "stage", (table,), (queries, grad_out, keys, values),
        (low(ROWS, width),) * 4
        + (full(FR_DEV, SLOTS, TOK_FRAME), full(WINDOW, FR_DEV, TOK_FRAME, TOK_FRAME)),
        [pltpu.SemaphoreType.DMA((4,))], unit, pltpu.HBM,
    )
    near_grid = (FR_DEV, FR_DEV, MOVED, TOK_FRAME, TOK_FRAME)
    far_grid = (len(FAR), FR_DEV, MOVED, TOK_FRAME, TOK_FRAME)
    near_masked, near_grads, own_stats = call(
        own_stats_kernel, "own_stats", (table,), (query, grad, key, value, moved_bias),
        (full(*near_grid), full(*near_grid), full(3, SIDE, TOK_FRAME)),
        [full(FR_DEV, 3, SIDE, TOK_FRAME)], MOVED * unit,
    )
    f_one, f_two, own_stats = lax.optimization_barrier((f_one, f_two, own_stats))
    note = full(2 * NOTES, TOK_FRAME)
    masked, grad_probs, mine, n_one, n_two, s_far, s_other = call(
        stats_kernel, "stats", (table,), (key, value, moved_bias, own_stats, f_one, f_two),
        (full(*far_grid), full(*far_grid), full(3, 3 * SIDE, TOK_FRAME), note, note)
        + (full(3, SIDE, TOK_FRAME),) * 2,
        [full(FR_DEV, 3, 2 * SIDE, TOK_FRAME)], 2 * MOVED * unit,
    )
    s_far, s_other = swap_far(s_far, s_other)
    v_send, mine = lax.optimization_barrier((v_send, mine))
    v_one, v_two = swap(v_send, v_send)
    k_one, k_two, s_far, s_other = lax.optimization_barrier((k_one, k_two, s_far, s_other))
    windows = low(DEPTH, 3 * ROWS, HD)
    accums = full(DEPTH, 3 * ROWS, HD)
    pairs = low(heads, FR_DEV, SLOTS, TOK_FRAME)
    chosen, prob_low, gv_own, gv_one, gv_two = call(
        values_kernel, "values_part", (table,),
        (query, grad, key, bias, k_one, k_two, n_one, n_two),
        (low(heads, FR_DEV, SLOTS, HD), pairs, full(ROWS, rest))
        + (low(ROWS + NOTES, rest),) * 2,
        [windows, accums], 2 * heads * unit,
    )
    rv_one, rv_two = swap(gv_one, gv_two)
    score_low, gk_own, gk_one, gk_two = call(
        keys_kernel, "keys_part", (table,), (query, grad, value, prob_low, v_one, v_two),
        (pairs, full(ROWS, rest), low(ROWS, rest), low(ROWS, rest)),
        [windows, low(DEPTH, FR_DEV, SLOTS, HD), accums], 2 * heads * unit,
    )
    rk_one, rk_two = swap(gk_one, gk_two)
    gq_rest, gv_own, gk_own = call(
        rest_kernel, "rest", (),
        (query, grad, chosen, prob_low, score_low, gv_own, gk_own),
        (low(ROWS, rest), full(ROWS, rest), full(ROWS, rest)), [], heads * unit,
    )
    rv_one, rv_two, gv_own = lax.optimization_barrier((rv_one, rv_two, gv_own))
    y_prob, y_score, logs, deltas, gq_one, gq_two = call(
        back_kernel, "back", (table,),
        (key, masked, grad_probs, mine, rv_one, rv_two, s_far, s_other),
        (low(*far_grid), low(*far_grid)) + (full(3 * SIDE, TOK_FRAME),) * 2
        + (low(ROWS, SPLIT),) * 2,
        [full(2, ROWS, SPLIT), full(2, 2 * NOTES, TOK_FRAME)], MOVED * unit,
    )
    rq_one, rq_two = swap(gq_one, gq_two)
    gq_near, gk_near, gv_near = call(
        home_kernel, "home", (table,),
        (query, grad, key, f_one, f_two, near_masked, near_grads, y_prob, y_score, logs, deltas),
        (full(ROWS, SPLIT), low(ROWS, SPLIT), low(ROWS, SPLIT)),
        [full(ROWS, SPLIT), full(ROWS, SPLIT)], 3 * MOVED * unit,
    )
    grad_values = jnp.concatenate([gv_near, joined(gv_own, rv_one[:ROWS], rv_two[:ROWS])], 1)
    grad_queries, grad_keys = call(
        last_kernel, "last", (),
        (gq_rest, gk_near, gq_near, rq_one, rq_two, gk_own, rk_one, rk_two),
        (pltpu.HBM((ROWS, width), jnp.bfloat16),) * 2,
        [low(ROWS, SPLIT), low(ROWS, rest), pltpu.SemaphoreType.DMA((4,))],
        unit, pltpu.VMEM, pltpu.HBM,
    )
    return grad_queries, grad_keys, grad_values


def solution(mesh):
    rows = P(("clips", "frames"), "heads")
    return jax.shard_map(
        local,
        mesh=mesh,
        in_specs=(rows, rows, rows, rows, P("clips", None), P("clips", None, None, None)),
        out_specs=(rows, rows, rows),
        check_vma=False,
    )
```

```python
import math

import jax
import jax.numpy as jnp
from jax import lax
from jax.experimental import pallas as pl
from jax.experimental.pallas import tpu as pltpu
from jax.sharding import PartitionSpec as P

HD = 128
TOK_FRAME = 192
FR_DEV = 2
REACH = 2
NSEL = 3
SB = 4
DEPTH = 3
MOVED = 2
SPLIT = MOVED * HD
ROWS = FR_DEV * TOK_FRAME
WINDOW = FR_DEV + 2 * REACH
SLOTS = NSEL * TOK_FRAME
BLOCK = TOK_FRAME // SB
SCALE = HD ** (-0.5)
SCALE2 = SCALE * math.log2(math.e)
NEG = -(2.0**100)
NT = (((1,), (1,)), ((), ()))
NN = (((1,), (0,)), ((), ()))
TN = (((0,), (0,)), ((), ()))
MASKS = WINDOW * NSEL
FIRST = MASKS + WINDOW * NSEL * SB * SB
RANK = FIRST + 1
COUNT = FIRST + 2
NOTES = 32
SIDE = FR_DEV * MOVED
FAR = (0, 1, 4, 5)


def dot(lhs, rhs, dims):
    return lax.dot_general(lhs, rhs, dims, preferred_element_type=jnp.float32)


def column_of(head):
    return slice(head * HD, (head + 1) * HD)


def rows_of(frame):
    return slice(frame * TOK_FRAME, (frame + 1) * TOK_FRAME)


def side_of(table, side):
    return jnp.where(table[RANK] % 2 == 1, side, 2 - side)


def inside(table, place):
    target = table[FIRST] + place
    return (target >= 0) & (target < table[COUNT])


def spot_of(table, frame, slot):
    place = frame + table[(REACH + frame) * NSEL + slot]
    side = (place >= 0).astype(jnp.int32) + (place >= FR_DEV).astype(jnp.int32)
    return side_of(table, side) * FR_DEV + (place + FR_DEV) % FR_DEV


def span(table, frame, slot):
    spot = spot_of(table, frame, slot)
    return pl.ds(pl.multiple_of(spot * TOK_FRAME, TOK_FRAME), TOK_FRAME)


def pair_of(table, query, key):
    index = side_of(table, query // FR_DEV) * FR_DEV + query % FR_DEV
    place = index - REACH
    active = jnp.zeros((), jnp.int32)
    slot = jnp.zeros((), jnp.int32)
    for each in range(NSEL):
        hit = (table[index * NSEL + each] + place == key).astype(jnp.int32)
        active += hit
        slot += hit * each
    active = (active > 0) & inside(table, place)
    return active, MASKS + (index * NSEL + slot) * SB * SB


def write_bias(table, start, seen, bias, row):
    q_block = lax.broadcasted_iota(jnp.int32, (8, TOK_FRAME), 1) // BLOCK
    for k_block in range(SB):
        value = jnp.zeros((8, TOK_FRAME), jnp.float32)
        for block in range(SB):
            keep = (table[start + block * SB + k_block] > 0) & seen
            value = jnp.where(q_block == block, jnp.where(keep, 0.0, NEG), value)
        for step in range(0, BLOCK, 8):
            bias[pl.ds(row + k_block * BLOCK + step, 8), :] = value


def copy_all(pairs, sems):
    moves = [pltpu.make_async_copy(a, b, sems.at[i]) for i, (a, b) in enumerate(pairs)]
    for move in moves:
        move.start()
    return moves


def pack_kernel(queries, grad_out, keys, values, both, k_send, v_send, sems):
    moves = copy_all(
        [
            (queries.at[:, :SPLIT], both.at[0]),
            (grad_out.at[:, :SPLIT], both.at[1]),
            (keys.at[:, SPLIT:], k_send),
            (values.at[:, SPLIT:], v_send),
        ],
        sems,
    )
    for move in moves:
        move.wait()


def stage_kernel(table, *refs):
    arrays, copies, bias, moved_bias, sems = refs[:4], refs[4:8], refs[8], refs[9], refs[10]
    moves = copy_all(list(zip(arrays, copies)), sems)
    for frame in range(FR_DEV):
        for slot in range(NSEL):
            at = (REACH + frame) * NSEL + slot
            seen = inside(table, frame + table[at])
            write_bias(table, MASKS + at * SB * SB, seen, bias.at[frame], slot * TOK_FRAME)
    for query in range(WINDOW):
        for key in range(FR_DEV):
            active, start = pair_of(table, query, key)

            @pl.when(active)
            def _():
                write_bias(table, start, active, moved_bias.at[query, key], 0)

    for move in moves:
        move.wait()


def fill_window(window, one, own, two, column, far_column):
    window[0:ROWS] = one[:, far_column]
    window[ROWS : 2 * ROWS] = own[:, column]
    window[2 * ROWS : 3 * ROWS] = two[:, far_column]


def pick(table, frame, window, chosen):
    for slot in range(NSEL):
        chosen[rows_of(slot)] = window[span(table, frame, slot), :]


def spread(table, frame, accum, parts):
    for slot in range(1, NSEL):
        accum[span(table, frame, slot), :] += parts[rows_of(slot - 1)]


def values_kernel(
    table, queries, grad_out, k_own, bias, k_one, k_two, n_one, n_two,
    chosen_out, prob_out, own_out, one_out, two_out,
    windows, accums,
):
    for head in range(one_out.shape[1] // HD):
        column = column_of(MOVED + head)
        far_column = column_of(head)
        window = windows.at[head % DEPTH]
        accum = accums.at[head % DEPTH]
        fill_window(window, k_one, k_own, k_two, column, far_column)
        accum[...] = jnp.zeros_like(accum)
        for frame in range(FR_DEV):
            chosen = chosen_out.at[head, frame]
            pick(table, frame, window, chosen)
            scores = dot(chosen[...], queries[rows_of(frame), column], NT)
            masked = scores * SCALE2 + bias[frame]
            raised = jnp.exp2(masked - jnp.max(masked, 0, keepdims=True))
            inverse = 1.0 / jnp.sum(raised, 0, keepdims=True)
            prob_low = (raised * inverse).astype(jnp.bfloat16)
            prob_out[head, frame] = prob_low
            far = dot(prob_low[TOK_FRAME:], grad_out[rows_of(frame), column], NN)
            spread(table, frame, accum, far)
        one_out[:ROWS, far_column] = accum[0:ROWS].astype(one_out.dtype)
        own_out[:, far_column] = accum[ROWS : 2 * ROWS]
        two_out[:ROWS, far_column] = accum[2 * ROWS : 3 * ROWS].astype(two_out.dtype)
    write_notes(n_one, one_out)
    write_notes(n_two, two_out)


def keys_kernel(
    table, queries, grad_out, v_own, prob_in, v_one, v_two,
    score_out, own_out, one_out, two_out,
    windows, choices, accums,
):
    for head in range(one_out.shape[1] // HD):
        column = column_of(MOVED + head)
        far_column = column_of(head)
        window = windows.at[head % DEPTH]
        accum = accums.at[head % DEPTH]
        fill_window(window, v_one, v_own, v_two, column, far_column)
        accum[...] = jnp.zeros_like(accum)
        for frame in range(FR_DEV):
            chosen = choices.at[head % DEPTH, frame]
            pick(table, frame, window, chosen)
            grad_prob = dot(chosen[...], grad_out[rows_of(frame), column], NT)
            prob = prob_in[head, frame].astype(jnp.float32)
            delta = jnp.sum(prob * grad_prob, 0, keepdims=True)
            score_low = (prob * (grad_prob - delta)).astype(jnp.bfloat16)
            score_out[head, frame] = score_low
            far = dot(score_low[TOK_FRAME:], queries[rows_of(frame), column], NN)
            spread(table, frame, accum, far)
        one_out[:, far_column] = (accum[0:ROWS] * SCALE).astype(one_out.dtype)
        own_out[:, far_column] = accum[ROWS : 2 * ROWS]
        two_out[:, far_column] = (accum[2 * ROWS : 3 * ROWS] * SCALE).astype(two_out.dtype)


def rest_kernel(
    queries, grad_out, chosen_in, prob_in, score_in, gv_own, gk_own,
    query_out, value_out, key_out,
):
    for head in range(query_out.shape[1] // HD):
        column = column_of(MOVED + head)
        far_column = column_of(head)
        for frame in range(FR_DEV):
            rows = rows_of(frame)
            score_low = score_in[head, frame]
            grad_query = dot(score_low, chosen_in[head, frame], TN)
            query_out[rows, far_column] = (grad_query * SCALE).astype(query_out.dtype)
            near = dot(score_low[:TOK_FRAME], queries[rows, column], NN)
            key_out[rows, far_column] = (gk_own[rows, far_column] + near) * SCALE
            near = dot(prob_in[head, frame, :TOK_FRAME], grad_out[rows, column], NN)
            value_out[rows, far_column] = gv_own[rows, far_column] + near


def joined(own, one, two):
    total = own[...] + one[...].astype(jnp.float32) + two[...].astype(jnp.float32)
    return total.astype(jnp.bfloat16)


def last_kernel(
    gq_rest, gk_near, gq_near, rq_one, rq_two, gk_own, rk_one, rk_two,
    query_out, key_out,
    query_done, key_done, sems,
):
    moves = copy_all(
        [(gq_rest, query_out.at[:, SPLIT:]), (gk_near, key_out.at[:, :SPLIT])], sems
    )
    key_done[...] = joined(gk_own, rk_one, rk_two)
    moves += copy_all([(key_done, key_out.at[:, SPLIT:])], sems.at[2:3])
    query_done[...] = joined(gq_near, rq_one, rq_two)
    moves += copy_all([(query_done, query_out.at[:, :SPLIT])], sems.at[3:4])
    for move in moves:
        move.wait()


def pair_stats(table, window, key, index, query, grad, keys, values, bias, outs):
    masked_out, grad_prob_out, parts = outs
    active, _ = pair_of(table, window, key)

    @pl.when(active)
    def _():
        for head in range(MOVED):
            column = column_of(head)
            row = slice(index * MOVED + head, index * MOVED + head + 1)
            rows = rows_of(key)
            masked = dot(keys[rows, column], query(head), NT) * SCALE2 + bias[window, key]
            highest = rounded(jnp.max(masked, 0, keepdims=True))
            raised = jnp.exp2(masked - highest)
            grad_prob = dot(values[rows, column], grad(head), NT)
            masked_out[index, key, head] = masked
            grad_prob_out[index, key, head] = grad_prob
            parts[key, 0, row] = highest
            parts[key, 1, row] = jnp.sum(raised, 0, keepdims=True)
            parts[key, 2, row] = jnp.sum(raised * grad_prob, 0, keepdims=True)

    @pl.when(jnp.logical_not(active))
    def _():
        rows = slice(index * MOVED, (index + 1) * MOVED)
        parts[key, 0, rows] = jnp.full((MOVED, TOK_FRAME), NEG, jnp.float32)
        parts[key, 1, rows] = jnp.zeros((MOVED, TOK_FRAME), jnp.float32)
        parts[key, 2, rows] = jnp.zeros((MOVED, TOK_FRAME), jnp.float32)


def own_stats_kernel(
    table, queries, grad_out, keys, values, bias,
    masked_out, grad_prob_out, stats_out,
    parts,
):
    for index in range(FR_DEV):
        for key in range(FR_DEV):
            rows = rows_of(index)
            pair_stats(
                table, FR_DEV + index, key, index,
                lambda head: queries[rows, column_of(head)],
                lambda head: grad_out[rows, column_of(head)],
                keys, values, bias, (masked_out, grad_prob_out, parts),
            )
    for index, each in enumerate(joined_stats([parts[key] for key in range(FR_DEV)])):
        stats_out[index] = each


def stats_kernel(
    table, keys, values, bias, own, f_one, f_two,
    masked_out, grad_prob_out, mine_out, one_out, two_out, far_out, other_out,
    parts,
):
    for index, window in enumerate(FAR):
        sent = f_one if window < FR_DEV else f_two
        for key in range(FR_DEV):
            rows = rows_of(window % FR_DEV)
            pair_stats(
                table, window, key, index,
                lambda head: sent[0, rows, column_of(head)],
                lambda head: sent[1, rows, column_of(head)],
                keys, values, bias, (masked_out, grad_prob_out, parts),
            )
    far = joined_stats([parts[key] for key in range(FR_DEV)])
    rank = table[RANK] % 4
    swapped = (rank == 1) | (rank == 2)
    for index in range(3):
        mine_out[index, :SIDE] = far[index][:SIDE]
        mine_out[index, SIDE : 2 * SIDE] = own[index]
        mine_out[index, 2 * SIDE :] = far[index][SIDE:]
        far_out[index] = jnp.where(swapped, far[index][SIDE:], far[index][:SIDE])
        other_out[index] = jnp.where(swapped, far[index][:SIDE], far[index][SIDE:])
    for out, start in ((one_out, 0), (two_out, SIDE)):
        rows = slice(start, start + 2 * SIDE)
        out[...] = jnp.zeros_like(out)
        notes = (mine_out[0, rows], *halves(mine_out[1, rows]), *halves(mine_out[2, rows]))
        for index, note in enumerate(notes):
            out[index * 2 * SIDE : (index + 1) * 2 * SIDE] = note


def rounded(array):
    return array.astype(jnp.bfloat16).astype(jnp.float32)


def halves(array):
    high = rounded(array)
    return high, array - high


def write_notes(notes, message):
    for half in range(2):
        message[ROWS:, half * TOK_FRAME : (half + 1) * TOK_FRAME] = notes[
            half * NOTES : (half + 1) * NOTES
        ].astype(message.dtype)


def read_notes(message, notes):
    for half in range(2):
        notes[half * NOTES : (half + 1) * NOTES] = message[
            ROWS:, half * TOK_FRAME : (half + 1) * TOK_FRAME
        ].astype(notes.dtype)
    parts = [notes[i * 2 * SIDE : (i + 1) * 2 * SIDE] for i in range(5)]
    return parts[0], parts[1] + parts[2], parts[3] + parts[4]


def joined_stats(sources):
    tops = [jnp.where(each[1] > 0, each[0], NEG) for each in sources]
    highest = tops[0]
    for top in tops[1:]:
        highest = jnp.maximum(highest, top)
    weights = [jnp.exp2(top - highest) for top in tops]
    total = sum(weight * each[1] for weight, each in zip(weights, sources))
    moment = sum(weight * each[2] for weight, each in zip(weights, sources))
    return highest, total, moment


def finish_pair(window, index, key, head, masked, grad_probs, logs, deltas):
    row = slice(window * MOVED + head, window * MOVED + head + 1)
    prob = jnp.exp2(masked[index, key, head] - logs[row])
    score_low = (prob * (grad_probs[index, key, head] - deltas[row])).astype(jnp.bfloat16)
    return prob.astype(jnp.bfloat16), score_low


def back_kernel(
    table, keys, masked, grad_probs, mine, r_one, r_two, s_far, s_other,
    prob_out, score_out, logs, deltas, one_out, two_out,
    accums, notes,
):
    side = SIDE
    rank = table[RANK] % 4
    swapped = (rank == 1) | (rank == 2)
    far = [jnp.where(swapped, s_other[i], s_far[i]) for i in range(3)]
    other = [jnp.where(swapped, s_far[i], s_other[i]) for i in range(3)]
    s_one = read_notes(r_one, notes.at[0])
    s_two = read_notes(r_two, notes.at[1])
    s_mine = [mine[i] for i in range(3)]

    def part(stats, start):
        return [each[start : start + side] for each in stats]

    groups = (
        (part(s_mine, 0), part(s_one, side), far),
        (part(s_mine, side), part(s_one, 0), part(s_two, side)),
        (part(s_mine, 2 * side), part(s_two, 0), other),
    )
    for index, sources in enumerate(groups):
        highest, total, moment = joined_stats(sources)
        rows = slice(index * side, (index + 1) * side)
        total = jnp.where(total > 0, total, 1.0)
        logs[rows] = highest + jnp.log2(total)
        deltas[rows] = moment / total
    accums[...] = jnp.zeros_like(accums)
    for index, window in enumerate(FAR):
        for key in range(FR_DEV):
            active, _ = pair_of(table, window, key)

            @pl.when(active)
            def _():
                for head in range(MOVED):
                    prob_low, score_low = finish_pair(
                        window, index, key, head, masked, grad_probs, logs, deltas
                    )
                    prob_out[index, key, head] = prob_low
                    score_out[index, key, head] = score_low
                    accums[index // FR_DEV, rows_of(index % FR_DEV), column_of(head)] += dot(
                        score_low, keys[rows_of(key), column_of(head)], TN
                    )

    one_out[...] = (accums[0] * SCALE).astype(one_out.dtype)
    two_out[...] = (accums[1] * SCALE).astype(two_out.dtype)


def home_kernel(
    table, queries, grad_out, keys, f_one, f_two, masked, grad_probs, prob_in, score_in,
    logs, deltas,
    query_out, key_out, value_out,
    key_accum, value_accum,
):
    query_out[...] = jnp.zeros_like(query_out)
    key_accum[...] = jnp.zeros_like(key_accum)
    value_accum[...] = jnp.zeros_like(value_accum)
    for window in range(WINDOW):
        rows = rows_of(window % FR_DEV)
        near = window // FR_DEV == 1
        sent = f_one if window < FR_DEV else f_two
        for key in range(FR_DEV):
            active, _ = pair_of(table, window, key)

            @pl.when(active)
            def _():
                for head in range(MOVED):
                    column = column_of(head)
                    if near:
                        query = queries[rows, column]
                        grad = grad_out[rows, column]
                        prob_low, score_low = finish_pair(
                            window, window - FR_DEV, key, head, masked, grad_probs, logs, deltas
                        )
                        query_out[rows, column] += dot(
                            score_low, keys[rows_of(key), column], TN
                        )
                    else:
                        query = sent[0, rows, column]
                        grad = sent[1, rows, column]
                        prob_low = prob_in[FAR.index(window), key, head]
                        score_low = score_in[FAR.index(window), key, head]
                    key_accum[rows_of(key), column] += dot(score_low, query, NN)
                    value_accum[rows_of(key), column] += dot(prob_low, grad, NN)

    query_out[...] = query_out[...] * SCALE
    key_out[...] = (key_accum[...] * SCALE).astype(key_out.dtype)
    value_out[...] = value_accum[...].astype(value_out.dtype)


def both_ways(pairs):
    return [pair for i, j in pairs for pair in ((i, j), (j, i))]


def swap(one, two):
    count = lax.axis_size("frames")
    first = [(i, i + 1) for i in range(0, count - 1, 2)]
    second = [(i, i + 1) for i in range(1, count - 1, 2)]
    return (
        lax.ppermute(one, "frames", both_ways(first)),
        lax.ppermute(two, "frames", both_ways(second)),
    )


def swap_far(far, other):
    count = lax.axis_size("frames")
    near = [(i, i + 2) for i in range(count - 2) if i % 4 < 2]
    over = [(i, i + 2) for i in range(count - 2) if i % 4 >= 2]
    far = lax.ppermute(far, "frames", both_ways(near))
    other = lax.ppermute(other, "frames", both_ways(over)) if over else jnp.zeros_like(other)
    return far, other


def lookup(offsets, spatial):
    rank = lax.axis_index("frames")
    first = rank * FR_DEV
    frames = offsets.shape[0]
    around = ((REACH, REACH), (0, 0))
    shifts = lax.dynamic_slice_in_dim(jnp.pad(offsets, around), first, WINDOW, 0)
    blocks = lax.dynamic_slice_in_dim(
        jnp.pad(spatial, around + ((0, 0), (0, 0))), first, WINDOW, 0
    )
    ends = jnp.stack([first, rank, jnp.full_like(rank, frames)]).astype(jnp.int32)
    return jnp.concatenate([shifts.reshape(-1), blocks.reshape(-1), ends])


def call(kernel, name, scalars, arrays, outs, scratch, flops, space=pltpu.VMEM, out_space=pltpu.VMEM):
    arrays = [pltpu.with_memory_space_constraint(array, space) for array in arrays]
    return pl.pallas_call(
        kernel,
        out_shape=outs,
        in_specs=[pl.BlockSpec(memory_space=pltpu.SMEM)] * len(scalars)
        + [pl.BlockSpec(memory_space=space)] * len(arrays),
        out_specs=tuple(pl.BlockSpec(memory_space=out_space) for _ in outs),
        scratch_shapes=scratch,
        compiler_params=pltpu.CompilerParams(vmem_limit_bytes=16 << 20),
        cost_estimate=pl.CostEstimate(flops=flops, bytes_accessed=0, transcendentals=0),
        name=name,
    )(*scalars, *arrays)


def local(queries, keys, values, grad_out, offsets, spatial):
    width = queries.shape[1]
    heads = width // HD - MOVED

    def low(*shape):
        return pltpu.VMEM(shape, jnp.bfloat16)

    def full(*shape):
        return pltpu.VMEM(shape, jnp.float32)

    unit = 2 * FR_DEV * NSEL * TOK_FRAME * TOK_FRAME * HD
    rest = width - SPLIT
    y_send, k_send, v_send = call(
        pack_kernel, "pack", (), (queries, grad_out, keys, values),
        (low(2, ROWS, SPLIT), low(ROWS, rest), low(ROWS, rest)),
        [pltpu.SemaphoreType.DMA((4,))], unit, pltpu.HBM,
    )
    f_one, f_two = swap(y_send, y_send)
    k_one, k_two = swap(k_send, k_send)
    table = lookup(offsets, spatial)
    query, grad, key, value, bias, moved_bias = call(
        stage_kernel, "stage", (table,), (queries, grad_out, keys, values),
        (low(ROWS, width),) * 4
        + (full(FR_DEV, SLOTS, TOK_FRAME), full(WINDOW, FR_DEV, TOK_FRAME, TOK_FRAME)),
        [pltpu.SemaphoreType.DMA((4,))], unit, pltpu.HBM,
    )
    near_grid = (FR_DEV, FR_DEV, MOVED, TOK_FRAME, TOK_FRAME)
    far_grid = (len(FAR), FR_DEV, MOVED, TOK_FRAME, TOK_FRAME)
    near_masked, near_grads, own_stats = call(
        own_stats_kernel, "own_stats", (table,), (query, grad, key, value, moved_bias),
        (full(*near_grid), full(*near_grid), full(3, SIDE, TOK_FRAME)),
        [full(FR_DEV, 3, SIDE, TOK_FRAME)], MOVED * unit,
    )
    f_two, f_one, own_stats = lax.optimization_barrier((f_two, f_one, own_stats))
    note = full(2 * NOTES, TOK_FRAME)
    masked, grad_probs, mine, n_one, n_two, s_far, s_other = call(
        stats_kernel, "stats", (table,), (key, value, moved_bias, own_stats, f_one, f_two),
        (full(*far_grid), full(*far_grid), full(3, 3 * SIDE, TOK_FRAME), note, note)
        + (full(3, SIDE, TOK_FRAME),) * 2,
        [full(FR_DEV, 3, 2 * SIDE, TOK_FRAME)], 2 * MOVED * unit,
    )
    s_far, s_other = swap_far(s_far, s_other)
    v_send, mine = lax.optimization_barrier((v_send, mine))
    v_one, v_two = swap(v_send, v_send)
    k_two, k_one, s_far, s_other = lax.optimization_barrier((k_two, k_one, s_far, s_other))
    windows = low(DEPTH, 3 * ROWS, HD)
    accums = full(DEPTH, 3 * ROWS, HD)
    pairs = low(heads, FR_DEV, SLOTS, TOK_FRAME)
    chosen, prob_low, gv_own, gv_one, gv_two = call(
        values_kernel, "values_part", (table,),
        (query, grad, key, bias, k_one, k_two, n_one, n_two),
        (low(heads, FR_DEV, SLOTS, HD), pairs, full(ROWS, rest))
        + (low(ROWS + NOTES, rest),) * 2,
        [windows, accums], 2 * heads * unit,
    )
    rv_one, rv_two = swap(gv_one, gv_two)
    score_low, gk_own, gk_one, gk_two = call(
        keys_kernel, "keys_part", (table,), (query, grad, value, prob_low, v_one, v_two),
        (pairs, full(ROWS, rest), low(ROWS, rest), low(ROWS, rest)),
        [windows, low(DEPTH, FR_DEV, SLOTS, HD), accums], 2 * heads * unit,
    )
    rk_one, rk_two = swap(gk_one, gk_two)
    gq_rest, gv_own, gk_own = call(
        rest_kernel, "rest", (),
        (query, grad, chosen, prob_low, score_low, gv_own, gk_own),
        (low(ROWS, rest), full(ROWS, rest), full(ROWS, rest)), [], heads * unit,
    )
    rv_one, rv_two, gv_own = lax.optimization_barrier((rv_one, rv_two, gv_own))
    y_prob, y_score, logs, deltas, gq_one, gq_two = call(
        back_kernel, "back", (table,),
        (key, masked, grad_probs, mine, rv_one, rv_two, s_far, s_other),
        (low(*far_grid), low(*far_grid)) + (full(3 * SIDE, TOK_FRAME),) * 2
        + (low(ROWS, SPLIT),) * 2,
        [full(2, ROWS, SPLIT), full(2, 2 * NOTES, TOK_FRAME)], MOVED * unit,
    )
    rq_one, rq_two = swap(gq_one, gq_two)
    gq_near, gk_near, gv_near = call(
        home_kernel, "home", (table,),
        (query, grad, key, f_one, f_two, near_masked, near_grads, y_prob, y_score, logs, deltas),
        (full(ROWS, SPLIT), low(ROWS, SPLIT), low(ROWS, SPLIT)),
        [full(ROWS, SPLIT), full(ROWS, SPLIT)], 3 * MOVED * unit,
    )
    grad_values = jnp.concatenate([gv_near, joined(gv_own, rv_one[:ROWS], rv_two[:ROWS])], 1)
    grad_queries, grad_keys = call(
        last_kernel, "last", (),
        (gq_rest, gk_near, gq_near, rq_one, rq_two, gk_own, rk_one, rk_two),
        (pltpu.HBM((ROWS, width), jnp.bfloat16),) * 2,
        [low(ROWS, SPLIT), low(ROWS, rest), pltpu.SemaphoreType.DMA((4,))],
        unit, pltpu.VMEM, pltpu.HBM,
    )
    return grad_queries, grad_keys, grad_values


def solution(mesh):
    rows = P(("clips", "frames"), "heads")
    return jax.shard_map(
        local,
        mesh=mesh,
        in_specs=(rows, rows, rows, rows, P("clips", None), P("clips", None, None, None)),
        out_specs=(rows, rows, rows),
        check_vma=False,
    )
```

```python
import math

import jax
import jax.numpy as jnp
from jax import lax
from jax.experimental import pallas as pl
from jax.experimental.pallas import tpu as pltpu
from jax.sharding import PartitionSpec as P

HD = 128
TOK_FRAME = 192
FR_DEV = 2
REACH = 2
NSEL = 3
SB = 4
DEPTH = 3
MOVED = 2
SPLIT = MOVED * HD
ROWS = FR_DEV * TOK_FRAME
WINDOW = FR_DEV + 2 * REACH
SLOTS = NSEL * TOK_FRAME
BLOCK = TOK_FRAME // SB
SCALE = HD ** (-0.5)
SCALE2 = SCALE * math.log2(math.e)
NEG = -(2.0**100)
NT = (((1,), (1,)), ((), ()))
NN = (((1,), (0,)), ((), ()))
TN = (((0,), (0,)), ((), ()))
MASKS = WINDOW * NSEL
FIRST = MASKS + WINDOW * NSEL * SB * SB
RANK = FIRST + 1
COUNT = FIRST + 2
NOTES = 32
SIDE = FR_DEV * MOVED
FAR = (0, 1, 4, 5)


def dot(lhs, rhs, dims):
    return lax.dot_general(lhs, rhs, dims, preferred_element_type=jnp.float32)


def column_of(head):
    return slice(head * HD, (head + 1) * HD)


def rows_of(frame):
    return slice(frame * TOK_FRAME, (frame + 1) * TOK_FRAME)


def side_of(table, side):
    return jnp.where(table[RANK] % 2 == 1, side, 2 - side)


def inside(table, place):
    target = table[FIRST] + place
    return (target >= 0) & (target < table[COUNT])


def spot_of(table, frame, slot):
    place = frame + table[(REACH + frame) * NSEL + slot]
    side = (place >= 0).astype(jnp.int32) + (place >= FR_DEV).astype(jnp.int32)
    return side_of(table, side) * FR_DEV + (place + FR_DEV) % FR_DEV


def span(table, frame, slot):
    spot = spot_of(table, frame, slot)
    return pl.ds(pl.multiple_of(spot * TOK_FRAME, TOK_FRAME), TOK_FRAME)


def pair_of(table, query, key):
    index = side_of(table, query // FR_DEV) * FR_DEV + query % FR_DEV
    place = index - REACH
    active = jnp.zeros((), jnp.int32)
    slot = jnp.zeros((), jnp.int32)
    for each in range(NSEL):
        hit = (table[index * NSEL + each] + place == key).astype(jnp.int32)
        active += hit
        slot += hit * each
    active = (active > 0) & inside(table, place)
    return active, MASKS + (index * NSEL + slot) * SB * SB


def write_bias(table, start, seen, bias, row):
    q_block = lax.broadcasted_iota(jnp.int32, (8, TOK_FRAME), 1) // BLOCK
    for k_block in range(SB):
        value = jnp.zeros((8, TOK_FRAME), jnp.float32)
        for block in range(SB):
            keep = (table[start + block * SB + k_block] > 0) & seen
            value = jnp.where(q_block == block, jnp.where(keep, 0.0, NEG), value)
        for step in range(0, BLOCK, 8):
            bias[pl.ds(row + k_block * BLOCK + step, 8), :] = value


def copy_all(pairs, sems):
    moves = [pltpu.make_async_copy(a, b, sems.at[i]) for i, (a, b) in enumerate(pairs)]
    for move in moves:
        move.start()
    return moves


def pack_queries_kernel(queries, grad_out, both, sems):
    pairs = [(queries.at[:, :SPLIT], both.at[0]), (grad_out.at[:, :SPLIT], both.at[1])]
    for move in copy_all(pairs, sems):
        move.wait()


def pack_keys_kernel(keys, values, k_send, v_send, sems):
    pairs = [(keys.at[:, SPLIT:], k_send), (values.at[:, SPLIT:], v_send)]
    for move in copy_all(pairs, sems):
        move.wait()


def stage_kernel(table, *refs):
    arrays, copies, bias, moved_bias, sems = refs[:4], refs[4:8], refs[8], refs[9], refs[10]
    moves = copy_all(list(zip(arrays, copies)), sems)
    for frame in range(FR_DEV):
        for slot in range(NSEL):
            at = (REACH + frame) * NSEL + slot
            seen = inside(table, frame + table[at])
            write_bias(table, MASKS + at * SB * SB, seen, bias.at[frame], slot * TOK_FRAME)
    for query in range(WINDOW):
        for key in range(FR_DEV):
            active, start = pair_of(table, query, key)

            @pl.when(active)
            def _():
                write_bias(table, start, active, moved_bias.at[query, key], 0)

    for move in moves:
        move.wait()


def fill_window(window, one, own, two, column, far_column):
    window[0:ROWS] = one[:, far_column]
    window[ROWS : 2 * ROWS] = own[:, column]
    window[2 * ROWS : 3 * ROWS] = two[:, far_column]


def pick(table, frame, window, chosen):
    for slot in range(NSEL):
        chosen[rows_of(slot)] = window[span(table, frame, slot), :]


def spread(table, frame, accum, parts):
    for slot in range(1, NSEL):
        accum[span(table, frame, slot), :] += parts[rows_of(slot - 1)]


def own_scores_kernel(queries, k_own, bias, masked_out):
    for head in range(masked_out.shape[0]):
        column = column_of(MOVED + head)
        for frame in range(FR_DEV):
            rows = rows_of(frame)
            scores = dot(k_own[rows, column], queries[rows, column], NT)
            masked_out[head, frame] = scores * SCALE2 + bias[frame, :TOK_FRAME]


def values_kernel(
    table, queries, grad_out, k_own, bias, near_masked, k_one, k_two, n_one, n_two,
    chosen_out, prob_out, own_out, one_out, two_out,
    windows, accums,
):
    for head in range(one_out.shape[1] // HD):
        column = column_of(MOVED + head)
        far_column = column_of(head)
        window = windows.at[head % DEPTH]
        accum = accums.at[head % DEPTH]
        fill_window(window, k_one, k_own, k_two, column, far_column)
        accum[...] = jnp.zeros_like(accum)
        for frame in range(FR_DEV):
            rows = rows_of(frame)
            chosen = chosen_out.at[head, frame]
            chosen[:TOK_FRAME] = k_own[rows, column]
            for slot in range(1, NSEL):
                chosen[rows_of(slot)] = window[span(table, frame, slot), :]
            scores = dot(chosen[TOK_FRAME:], queries[rows, column], NT)
            masked = (near_masked[head, frame], scores * SCALE2 + bias[frame, TOK_FRAME:])
            highest = jnp.maximum(*(jnp.max(each, 0, keepdims=True) for each in masked))
            near, far = (jnp.exp2(each - highest) for each in masked)
            total = jnp.sum(near, 0, keepdims=True) + jnp.sum(far, 0, keepdims=True)
            inverse = 1.0 / total
            far_low = (far * inverse).astype(jnp.bfloat16)
            prob_out[head, frame, :TOK_FRAME] = (near * inverse).astype(jnp.bfloat16)
            prob_out[head, frame, TOK_FRAME:] = far_low
            spread(table, frame, accum, dot(far_low, grad_out[rows, column], NN))
        one_out[:ROWS, far_column] = accum[0:ROWS].astype(one_out.dtype)
        own_out[:, far_column] = accum[ROWS : 2 * ROWS]
        two_out[:ROWS, far_column] = accum[2 * ROWS : 3 * ROWS].astype(two_out.dtype)
    write_notes(n_one, one_out)
    write_notes(n_two, two_out)


def keys_kernel(
    table, queries, grad_out, v_own, prob_in, v_one, v_two,
    score_out, own_out, one_out, two_out,
    windows, choices, accums,
):
    for head in range(one_out.shape[1] // HD):
        column = column_of(MOVED + head)
        far_column = column_of(head)
        window = windows.at[head % DEPTH]
        accum = accums.at[head % DEPTH]
        fill_window(window, v_one, v_own, v_two, column, far_column)
        accum[...] = jnp.zeros_like(accum)
        for frame in range(FR_DEV):
            chosen = choices.at[head % DEPTH, frame]
            pick(table, frame, window, chosen)
            grad_prob = dot(chosen[...], grad_out[rows_of(frame), column], NT)
            prob = prob_in[head, frame].astype(jnp.float32)
            delta = jnp.sum(prob * grad_prob, 0, keepdims=True)
            score_low = (prob * (grad_prob - delta)).astype(jnp.bfloat16)
            score_out[head, frame] = score_low
            far = dot(score_low[TOK_FRAME:], queries[rows_of(frame), column], NN)
            spread(table, frame, accum, far)
        one_out[:, far_column] = (accum[0:ROWS] * SCALE).astype(one_out.dtype)
        own_out[:, far_column] = accum[ROWS : 2 * ROWS]
        two_out[:, far_column] = (accum[2 * ROWS : 3 * ROWS] * SCALE).astype(two_out.dtype)


def rest_kernel(
    queries, grad_out, chosen_in, prob_in, score_in, gv_own, gk_own,
    query_out, value_out, key_out,
):
    for head in range(query_out.shape[1] // HD):
        column = column_of(MOVED + head)
        far_column = column_of(head)
        for frame in range(FR_DEV):
            rows = rows_of(frame)
            score_low = score_in[head, frame]
            grad_query = dot(score_low, chosen_in[head, frame], TN)
            query_out[rows, far_column] = (grad_query * SCALE).astype(query_out.dtype)
            near = dot(score_low[:TOK_FRAME], queries[rows, column], NN)
            key_out[rows, far_column] = (gk_own[rows, far_column] + near) * SCALE
            near = dot(prob_in[head, frame, :TOK_FRAME], grad_out[rows, column], NN)
            value_out[rows, far_column] = gv_own[rows, far_column] + near


def joined(own, one, two):
    total = own[...] + one[...].astype(jnp.float32) + two[...].astype(jnp.float32)
    return total.astype(jnp.bfloat16)


def last_kernel(
    gq_rest, gk_near, gq_near, rq_one, rq_two, gk_own, rk_one, rk_two,
    query_out, key_out,
    query_done, key_done, sems,
):
    moves = copy_all(
        [(gq_rest, query_out.at[:, SPLIT:]), (gk_near, key_out.at[:, :SPLIT])], sems
    )
    key_done[...] = joined(gk_own, rk_one, rk_two)
    moves += copy_all([(key_done, key_out.at[:, SPLIT:])], sems.at[2:3])
    query_done[...] = joined(gq_near, rq_one, rq_two)
    moves += copy_all([(query_done, query_out.at[:, :SPLIT])], sems.at[3:4])
    for move in moves:
        move.wait()


def pair_stats(table, window, key, index, query, grad, keys, values, bias, outs):
    masked_out, grad_prob_out, parts = outs
    active, _ = pair_of(table, window, key)

    @pl.when(active)
    def _():
        for head in range(MOVED):
            column = column_of(head)
            row = slice(index * MOVED + head, index * MOVED + head + 1)
            rows = rows_of(key)
            masked = dot(keys[rows, column], query(head), NT) * SCALE2 + bias[window, key]
            highest = rounded(jnp.max(masked, 0, keepdims=True))
            raised = jnp.exp2(masked - highest)
            grad_prob = dot(values[rows, column], grad(head), NT)
            masked_out[index, key, head] = masked
            grad_prob_out[index, key, head] = grad_prob
            parts[key, 0, row] = highest
            parts[key, 1, row] = jnp.sum(raised, 0, keepdims=True)
            parts[key, 2, row] = jnp.sum(raised * grad_prob, 0, keepdims=True)

    @pl.when(jnp.logical_not(active))
    def _():
        rows = slice(index * MOVED, (index + 1) * MOVED)
        parts[key, 0, rows] = jnp.full((MOVED, TOK_FRAME), NEG, jnp.float32)
        parts[key, 1, rows] = jnp.zeros((MOVED, TOK_FRAME), jnp.float32)
        parts[key, 2, rows] = jnp.zeros((MOVED, TOK_FRAME), jnp.float32)


def own_stats_kernel(
    table, queries, grad_out, keys, values, bias,
    masked_out, grad_prob_out, stats_out,
    parts,
):
    for index in range(FR_DEV):
        for key in range(FR_DEV):
            rows = rows_of(index)
            pair_stats(
                table, FR_DEV + index, key, index,
                lambda head: queries[rows, column_of(head)],
                lambda head: grad_out[rows, column_of(head)],
                keys, values, bias, (masked_out, grad_prob_out, parts),
            )
    for index, each in enumerate(joined_stats([parts[key] for key in range(FR_DEV)])):
        stats_out[index] = each


def stats_kernel(
    table, keys, values, bias, own, f_one, f_two,
    masked_out, grad_prob_out, mine_out, one_out, two_out, far_out, other_out,
    parts,
):
    for index, window in enumerate(FAR):
        sent = f_one if window < FR_DEV else f_two
        for key in range(FR_DEV):
            rows = rows_of(window % FR_DEV)
            pair_stats(
                table, window, key, index,
                lambda head: sent[0, rows, column_of(head)],
                lambda head: sent[1, rows, column_of(head)],
                keys, values, bias, (masked_out, grad_prob_out, parts),
            )
    far = joined_stats([parts[key] for key in range(FR_DEV)])
    rank = table[RANK] % 4
    swapped = (rank == 1) | (rank == 2)
    for index in range(3):
        mine_out[index, :SIDE] = far[index][:SIDE]
        mine_out[index, SIDE : 2 * SIDE] = own[index]
        mine_out[index, 2 * SIDE :] = far[index][SIDE:]
        far_out[index] = jnp.where(swapped, far[index][SIDE:], far[index][:SIDE])
        other_out[index] = jnp.where(swapped, far[index][:SIDE], far[index][SIDE:])
    for out, start in ((one_out, 0), (two_out, SIDE)):
        rows = slice(start, start + 2 * SIDE)
        out[...] = jnp.zeros_like(out)
        notes = (mine_out[0, rows], *halves(mine_out[1, rows]), *halves(mine_out[2, rows]))
        for index, note in enumerate(notes):
            out[index * 2 * SIDE : (index + 1) * 2 * SIDE] = note


def rounded(array):
    return array.astype(jnp.bfloat16).astype(jnp.float32)


def halves(array):
    high = rounded(array)
    return high, array - high


def write_notes(notes, message):
    for half in range(2):
        message[ROWS:, half * TOK_FRAME : (half + 1) * TOK_FRAME] = notes[
            half * NOTES : (half + 1) * NOTES
        ].astype(message.dtype)


def read_notes(message, notes):
    for half in range(2):
        notes[half * NOTES : (half + 1) * NOTES] = message[
            ROWS:, half * TOK_FRAME : (half + 1) * TOK_FRAME
        ].astype(notes.dtype)
    parts = [notes[i * 2 * SIDE : (i + 1) * 2 * SIDE] for i in range(5)]
    return parts[0], parts[1] + parts[2], parts[3] + parts[4]


def joined_stats(sources):
    tops = [jnp.where(each[1] > 0, each[0], NEG) for each in sources]
    highest = tops[0]
    for top in tops[1:]:
        highest = jnp.maximum(highest, top)
    weights = [jnp.exp2(top - highest) for top in tops]
    total = sum(weight * each[1] for weight, each in zip(weights, sources))
    moment = sum(weight * each[2] for weight, each in zip(weights, sources))
    return highest, total, moment


def finish_pair(window, index, key, head, masked, grad_probs, logs, deltas):
    row = slice(window * MOVED + head, window * MOVED + head + 1)
    prob = jnp.exp2(masked[index, key, head] - logs[row])
    score_low = (prob * (grad_probs[index, key, head] - deltas[row])).astype(jnp.bfloat16)
    return prob.astype(jnp.bfloat16), score_low


def back_kernel(
    table, keys, masked, grad_probs, mine, r_one, r_two, s_far, s_other,
    prob_out, score_out, logs, deltas, one_out, two_out,
    accums, notes,
):
    side = SIDE
    rank = table[RANK] % 4
    swapped = (rank == 1) | (rank == 2)
    far = [jnp.where(swapped, s_other[i], s_far[i]) for i in range(3)]
    other = [jnp.where(swapped, s_far[i], s_other[i]) for i in range(3)]
    s_one = read_notes(r_one, notes.at[0])
    s_two = read_notes(r_two, notes.at[1])
    s_mine = [mine[i] for i in range(3)]

    def part(stats, start):
        return [each[start : start + side] for each in stats]

    groups = (
        (part(s_mine, 0), part(s_one, side), far),
        (part(s_mine, side), part(s_one, 0), part(s_two, side)),
        (part(s_mine, 2 * side), part(s_two, 0), other),
    )
    for index, sources in enumerate(groups):
        highest, total, moment = joined_stats(sources)
        rows = slice(index * side, (index + 1) * side)
        total = jnp.where(total > 0, total, 1.0)
        logs[rows] = highest + jnp.log2(total)
        deltas[rows] = moment / total
    accums[...] = jnp.zeros_like(accums)
    for index, window in enumerate(FAR):
        for key in range(FR_DEV):
            active, _ = pair_of(table, window, key)

            @pl.when(active)
            def _():
                for head in range(MOVED):
                    prob_low, score_low = finish_pair(
                        window, index, key, head, masked, grad_probs, logs, deltas
                    )
                    prob_out[index, key, head] = prob_low
                    score_out[index, key, head] = score_low
                    accums[index // FR_DEV, rows_of(index % FR_DEV), column_of(head)] += dot(
                        score_low, keys[rows_of(key), column_of(head)], TN
                    )

    one_out[...] = (accums[0] * SCALE).astype(one_out.dtype)
    two_out[...] = (accums[1] * SCALE).astype(two_out.dtype)


def home_kernel(
    table, queries, grad_out, keys, f_one, f_two, masked, grad_probs, prob_in, score_in,
    logs, deltas,
    query_out, key_out, value_out,
    key_accum, value_accum,
):
    query_out[...] = jnp.zeros_like(query_out)
    key_accum[...] = jnp.zeros_like(key_accum)
    value_accum[...] = jnp.zeros_like(value_accum)
    for window in range(WINDOW):
        rows = rows_of(window % FR_DEV)
        near = window // FR_DEV == 1
        sent = f_one if window < FR_DEV else f_two
        for key in range(FR_DEV):
            active, _ = pair_of(table, window, key)

            @pl.when(active)
            def _():
                for head in range(MOVED):
                    column = column_of(head)
                    if near:
                        query = queries[rows, column]
                        grad = grad_out[rows, column]
                        prob_low, score_low = finish_pair(
                            window, window - FR_DEV, key, head, masked, grad_probs, logs, deltas
                        )
                        query_out[rows, column] += dot(
                            score_low, keys[rows_of(key), column], TN
                        )
                    else:
                        query = sent[0, rows, column]
                        grad = sent[1, rows, column]
                        prob_low = prob_in[FAR.index(window), key, head]
                        score_low = score_in[FAR.index(window), key, head]
                    key_accum[rows_of(key), column] += dot(score_low, query, NN)
                    value_accum[rows_of(key), column] += dot(prob_low, grad, NN)

    query_out[...] = query_out[...] * SCALE
    key_out[...] = (key_accum[...] * SCALE).astype(key_out.dtype)
    value_out[...] = value_accum[...].astype(value_out.dtype)


def both_ways(pairs):
    return [pair for i, j in pairs for pair in ((i, j), (j, i))]


def swap(one, two):
    count = lax.axis_size("frames")
    first = [(i, i + 1) for i in range(0, count - 1, 2)]
    second = [(i, i + 1) for i in range(1, count - 1, 2)]
    return (
        lax.ppermute(one, "frames", both_ways(first)),
        lax.ppermute(two, "frames", both_ways(second)),
    )


def swap_far(far, other):
    count = lax.axis_size("frames")
    near = [(i, i + 2) for i in range(count - 2) if i % 4 < 2]
    over = [(i, i + 2) for i in range(count - 2) if i % 4 >= 2]
    far = lax.ppermute(far, "frames", both_ways(near))
    other = lax.ppermute(other, "frames", both_ways(over)) if over else jnp.zeros_like(other)
    return far, other


def lookup(offsets, spatial):
    rank = lax.axis_index("frames")
    first = rank * FR_DEV
    frames = offsets.shape[0]
    around = ((REACH, REACH), (0, 0))
    shifts = lax.dynamic_slice_in_dim(jnp.pad(offsets, around), first, WINDOW, 0)
    blocks = lax.dynamic_slice_in_dim(
        jnp.pad(spatial, around + ((0, 0), (0, 0))), first, WINDOW, 0
    )
    ends = jnp.stack([first, rank, jnp.full_like(rank, frames)]).astype(jnp.int32)
    return jnp.concatenate([shifts.reshape(-1), blocks.reshape(-1), ends])


def call(kernel, name, scalars, arrays, outs, scratch, flops, space=pltpu.VMEM, out_space=pltpu.VMEM):
    arrays = [pltpu.with_memory_space_constraint(array, space) for array in arrays]
    return pl.pallas_call(
        kernel,
        out_shape=outs,
        in_specs=[pl.BlockSpec(memory_space=pltpu.SMEM)] * len(scalars)
        + [pl.BlockSpec(memory_space=space)] * len(arrays),
        out_specs=tuple(pl.BlockSpec(memory_space=out_space) for _ in outs),
        scratch_shapes=scratch,
        compiler_params=pltpu.CompilerParams(vmem_limit_bytes=16 << 20),
        cost_estimate=pl.CostEstimate(flops=flops, bytes_accessed=0, transcendentals=0),
        name=name,
    )(*scalars, *arrays)


def local(queries, keys, values, grad_out, offsets, spatial):
    width = queries.shape[1]
    heads = width // HD - MOVED

    def low(*shape):
        return pltpu.VMEM(shape, jnp.bfloat16)

    def full(*shape):
        return pltpu.VMEM(shape, jnp.float32)

    unit = 2 * FR_DEV * NSEL * TOK_FRAME * TOK_FRAME * HD
    rest = width - SPLIT
    (y_send,) = call(
        pack_queries_kernel, "pack_queries", (), (queries, grad_out),
        (low(2, ROWS, SPLIT),), [pltpu.SemaphoreType.DMA((2,))], unit, pltpu.HBM,
    )
    k_send, v_send = call(
        pack_keys_kernel, "pack_keys", (), (keys, values),
        (low(ROWS, rest), low(ROWS, rest)), [pltpu.SemaphoreType.DMA((2,))], unit, pltpu.HBM,
    )
    f_one, f_two = swap(y_send, y_send)
    k_one, k_two = swap(k_send, k_send)
    table = lookup(offsets, spatial)
    query, grad, key, value, bias, moved_bias = call(
        stage_kernel, "stage", (table,), (queries, grad_out, keys, values),
        (low(ROWS, width),) * 4
        + (full(FR_DEV, SLOTS, TOK_FRAME), full(WINDOW, FR_DEV, TOK_FRAME, TOK_FRAME)),
        [pltpu.SemaphoreType.DMA((4,))], unit, pltpu.HBM,
    )
    near_grid = (FR_DEV, FR_DEV, MOVED, TOK_FRAME, TOK_FRAME)
    far_grid = (len(FAR), FR_DEV, MOVED, TOK_FRAME, TOK_FRAME)
    near_masked, near_grads, own_stats = call(
        own_stats_kernel, "own_stats", (table,), (query, grad, key, value, moved_bias),
        (full(*near_grid), full(*near_grid), full(3, SIDE, TOK_FRAME)),
        [full(FR_DEV, 3, SIDE, TOK_FRAME)], MOVED * unit,
    )
    (near_scores,) = call(
        own_scores_kernel, "own_scores", (), (query, key, bias),
        (full(heads, FR_DEV, TOK_FRAME, TOK_FRAME),), [], heads * unit // 3,
    )
    f_two, f_one, own_stats, near_scores = lax.optimization_barrier(
        (f_two, f_one, own_stats, near_scores)
    )
    note = full(2 * NOTES, TOK_FRAME)
    masked, grad_probs, mine, n_one, n_two, s_far, s_other = call(
        stats_kernel, "stats", (table,), (key, value, moved_bias, own_stats, f_one, f_two),
        (full(*far_grid), full(*far_grid), full(3, 3 * SIDE, TOK_FRAME), note, note)
        + (full(3, SIDE, TOK_FRAME),) * 2,
        [full(FR_DEV, 3, 2 * SIDE, TOK_FRAME)], 2 * MOVED * unit,
    )
    s_far, s_other = swap_far(s_far, s_other)
    v_send, mine = lax.optimization_barrier((v_send, mine))
    v_one, v_two = swap(v_send, v_send)
    k_two, k_one, s_far, s_other = lax.optimization_barrier((k_two, k_one, s_far, s_other))
    windows = low(DEPTH, 3 * ROWS, HD)
    accums = full(DEPTH, 3 * ROWS, HD)
    pairs = low(heads, FR_DEV, SLOTS, TOK_FRAME)
    chosen, prob_low, gv_own, gv_one, gv_two = call(
        values_kernel, "values_part", (table,),
        (query, grad, key, bias, near_scores, k_one, k_two, n_one, n_two),
        (low(heads, FR_DEV, SLOTS, HD), pairs, full(ROWS, rest))
        + (low(ROWS + NOTES, rest),) * 2,
        [windows, accums], 2 * heads * unit,
    )
    rv_one, rv_two = swap(gv_one, gv_two)
    score_low, gk_own, gk_one, gk_two = call(
        keys_kernel, "keys_part", (table,), (query, grad, value, prob_low, v_one, v_two),
        (pairs, full(ROWS, rest), low(ROWS, rest), low(ROWS, rest)),
        [windows, low(DEPTH, FR_DEV, SLOTS, HD), accums], 2 * heads * unit,
    )
    rk_one, rk_two = swap(gk_one, gk_two)
    y_prob, y_score, logs, deltas, gq_one, gq_two = call(
        back_kernel, "back", (table,),
        (key, masked, grad_probs, mine, rv_one, rv_two, s_far, s_other),
        (low(*far_grid), low(*far_grid)) + (full(3 * SIDE, TOK_FRAME),) * 2
        + (low(ROWS, SPLIT),) * 2,
        [full(2, ROWS, SPLIT), full(2, 2 * NOTES, TOK_FRAME)], MOVED * unit,
    )
    rq_one, rq_two = swap(gq_one, gq_two)
    score_low, logs = lax.optimization_barrier((score_low, logs))
    gq_rest, gv_own, gk_own = call(
        rest_kernel, "rest", (),
        (query, grad, chosen, prob_low, score_low, gv_own, gk_own),
        (low(ROWS, rest), full(ROWS, rest), full(ROWS, rest)), [], heads * unit,
    )
    gq_near, gk_near, gv_near = call(
        home_kernel, "home", (table,),
        (query, grad, key, f_one, f_two, near_masked, near_grads, y_prob, y_score, logs, deltas),
        (full(ROWS, SPLIT), low(ROWS, SPLIT), low(ROWS, SPLIT)),
        [full(ROWS, SPLIT), full(ROWS, SPLIT)], 3 * MOVED * unit,
    )
    grad_values = jnp.concatenate([gv_near, joined(gv_own, rv_one[:ROWS], rv_two[:ROWS])], 1)
    grad_queries, grad_keys = call(
        last_kernel, "last", (),
        (gq_rest, gk_near, gq_near, rq_one, rq_two, gk_own, rk_one, rk_two),
        (pltpu.HBM((ROWS, width), jnp.bfloat16),) * 2,
        [low(ROWS, SPLIT), low(ROWS, rest), pltpu.SemaphoreType.DMA((4,))],
        unit, pltpu.VMEM, pltpu.HBM,
    )
    return grad_queries, grad_keys, grad_values


def solution(mesh):
    rows = P(("clips", "frames"), "heads")
    return jax.shard_map(
        local,
        mesh=mesh,
        in_specs=(rows, rows, rows, rows, P("clips", None), P("clips", None, None, None)),
        out_specs=(rows, rows, rows),
        check_vma=False,
    )
```

```python
import functools
import math

import jax
import jax.numpy as jnp
from jax import lax
from jax.experimental import pallas as pl
from jax.experimental.pallas import tpu as pltpu
from jax.sharding import PartitionSpec as P

HD = 128
TOK_FRAME = 192
FR_DEV = 2
REACH = 2
NSEL = 3
SB = 4
DEPTH = 3
MOVED = 2
SPLIT = MOVED * HD
ROWS = FR_DEV * TOK_FRAME
WINDOW = FR_DEV + 2 * REACH
SLOTS = NSEL * TOK_FRAME
BLOCK = TOK_FRAME // SB
SCALE = HD ** (-0.5)
SCALE2 = SCALE * math.log2(math.e)
NEG = -(2.0**100)
NT = (((1,), (1,)), ((), ()))
NN = (((1,), (0,)), ((), ()))
TN = (((0,), (0,)), ((), ()))
MASKS = WINDOW * NSEL
FIRST = MASKS + WINDOW * NSEL * SB * SB
RANK = FIRST + 1
COUNT = FIRST + 2
NOTES = 32
SIDE = FR_DEV * MOVED
FAR = (0, 1, 4, 5)


def dot(lhs, rhs, dims):
    return lax.dot_general(lhs, rhs, dims, preferred_element_type=jnp.float32)


def column_of(head):
    return slice(head * HD, (head + 1) * HD)


def rows_of(frame):
    return slice(frame * TOK_FRAME, (frame + 1) * TOK_FRAME)


def side_of(table, side):
    return jnp.where(table[RANK] % 2 == 1, side, 2 - side)


def inside(table, place):
    target = table[FIRST] + place
    return (target >= 0) & (target < table[COUNT])


def spot_of(table, frame, slot):
    place = frame + table[(REACH + frame) * NSEL + slot]
    side = (place >= 0).astype(jnp.int32) + (place >= FR_DEV).astype(jnp.int32)
    return side_of(table, side) * FR_DEV + (place + FR_DEV) % FR_DEV


def span(table, frame, slot):
    spot = spot_of(table, frame, slot)
    return pl.ds(pl.multiple_of(spot * TOK_FRAME, TOK_FRAME), TOK_FRAME)


def pair_of(table, query, key):
    index = side_of(table, query // FR_DEV) * FR_DEV + query % FR_DEV
    place = index - REACH
    active = jnp.zeros((), jnp.int32)
    slot = jnp.zeros((), jnp.int32)
    for each in range(NSEL):
        hit = (table[index * NSEL + each] + place == key).astype(jnp.int32)
        active += hit
        slot += hit * each
    active = (active > 0) & inside(table, place)
    return active, MASKS + (index * NSEL + slot) * SB * SB


def write_bias(table, start, seen, bias, row):
    q_block = lax.broadcasted_iota(jnp.int32, (8, TOK_FRAME), 1) // BLOCK
    for k_block in range(SB):
        value = jnp.zeros((8, TOK_FRAME), jnp.float32)
        for block in range(SB):
            keep = (table[start + block * SB + k_block] > 0) & seen
            value = jnp.where(q_block == block, jnp.where(keep, 0.0, NEG), value)
        for step in range(0, BLOCK, 8):
            bias[pl.ds(row + k_block * BLOCK + step, 8), :] = value


def copy_all(pairs, sems):
    moves = [pltpu.make_async_copy(a, b, sems.at[i]) for i, (a, b) in enumerate(pairs)]
    for move in moves:
        move.start()
    return moves


def pack_queries_kernel(queries, grad_out, both, sems):
    pairs = [(queries.at[:, :SPLIT], both.at[0]), (grad_out.at[:, :SPLIT], both.at[1])]
    for move in copy_all(pairs, sems):
        move.wait()


def pack_keys_kernel(keys, values, k_send, v_send, sems):
    pairs = [(keys.at[:, SPLIT:], k_send), (values.at[:, SPLIT:], v_send)]
    for move in copy_all(pairs, sems):
        move.wait()


def stage_kernel(table, *refs):
    arrays, copies, bias, moved_bias, sems = refs[:4], refs[4:8], refs[8], refs[9], refs[10]
    moves = copy_all(list(zip(arrays, copies)), sems)
    for frame in range(FR_DEV):
        for slot in range(NSEL):
            at = (REACH + frame) * NSEL + slot
            seen = inside(table, frame + table[at])
            write_bias(table, MASKS + at * SB * SB, seen, bias.at[frame], slot * TOK_FRAME)
    for query in range(WINDOW):
        for key in range(FR_DEV):
            active, start = pair_of(table, query, key)

            @pl.when(active)
            def _():
                write_bias(table, start, active, moved_bias.at[query, key], 0)

    for move in moves:
        move.wait()


def fill_window(window, one, own, two, column, far_column):
    window[0:ROWS] = one[:, far_column]
    window[ROWS : 2 * ROWS] = own[:, column]
    window[2 * ROWS : 3 * ROWS] = two[:, far_column]


def pick(table, frame, window, chosen):
    for slot in range(NSEL):
        chosen[rows_of(slot)] = window[span(table, frame, slot), :]


def spread(table, frame, accum, parts):
    for slot in range(1, NSEL):
        accum[span(table, frame, slot), :] += parts[rows_of(slot - 1)]


def own_scores_kernel(queries, k_own, bias, masked_out):
    for head in range(masked_out.shape[0]):
        column = column_of(MOVED + head)
        for frame in range(FR_DEV):
            rows = rows_of(frame)
            scores = dot(k_own[rows, column], queries[rows, column], NT)
            masked_out[head, frame] = scores * SCALE2 + bias[frame, :TOK_FRAME]


def values_kernel(
    table, queries, grad_out, k_own, bias, near_masked, k_one, k_two, n_one, n_two,
    chosen_out, prob_out, own_out, one_out, two_out,
    windows, accums,
):
    for head in range(one_out.shape[1] // HD):
        column = column_of(MOVED + head)
        far_column = column_of(head)
        window = windows.at[head % DEPTH]
        accum = accums.at[head % DEPTH]
        fill_window(window, k_one, k_own, k_two, column, far_column)
        accum[...] = jnp.zeros_like(accum)
        for frame in range(FR_DEV):
            rows = rows_of(frame)
            chosen = chosen_out.at[head, frame]
            chosen[:TOK_FRAME] = k_own[rows, column]
            for slot in range(1, NSEL):
                chosen[rows_of(slot)] = window[span(table, frame, slot), :]
            scores = dot(chosen[TOK_FRAME:], queries[rows, column], NT)
            masked = (near_masked[head, frame], scores * SCALE2 + bias[frame, TOK_FRAME:])
            highest = jnp.maximum(*(jnp.max(each, 0, keepdims=True) for each in masked))
            near, far = (jnp.exp2(each - highest) for each in masked)
            total = jnp.sum(near, 0, keepdims=True) + jnp.sum(far, 0, keepdims=True)
            inverse = 1.0 / total
            far_low = (far * inverse).astype(jnp.bfloat16)
            prob_out[head, frame, :TOK_FRAME] = (near * inverse).astype(jnp.bfloat16)
            prob_out[head, frame, TOK_FRAME:] = far_low
            spread(table, frame, accum, dot(far_low, grad_out[rows, column], NN))
        one_out[:ROWS, far_column] = accum[0:ROWS].astype(one_out.dtype)
        own_out[:, far_column] = accum[ROWS : 2 * ROWS]
        two_out[:ROWS, far_column] = accum[2 * ROWS : 3 * ROWS].astype(two_out.dtype)
    write_notes(n_one, one_out)
    write_notes(n_two, two_out)


def keys_kernel(
    table, queries, grad_out, v_own, prob_in, v_one, v_two,
    score_out, own_out, one_out, two_out,
    windows, choices, accums,
):
    for head in range(one_out.shape[1] // HD):
        column = column_of(MOVED + head)
        far_column = column_of(head)
        window = windows.at[head % DEPTH]
        accum = accums.at[head % DEPTH]
        fill_window(window, v_one, v_own, v_two, column, far_column)
        accum[...] = jnp.zeros_like(accum)
        for frame in range(FR_DEV):
            chosen = choices.at[head % DEPTH, frame]
            pick(table, frame, window, chosen)
            grad_prob = dot(chosen[...], grad_out[rows_of(frame), column], NT)
            prob = prob_in[head, frame].astype(jnp.float32)
            delta = jnp.sum(prob * grad_prob, 0, keepdims=True)
            score_low = (prob * (grad_prob - delta)).astype(jnp.bfloat16)
            score_out[head, frame] = score_low
            far = dot(score_low[TOK_FRAME:], queries[rows_of(frame), column], NN)
            spread(table, frame, accum, far)
        one_out[:, far_column] = (accum[0:ROWS] * SCALE).astype(one_out.dtype)
        own_out[:, far_column] = accum[ROWS : 2 * ROWS]
        two_out[:, far_column] = (accum[2 * ROWS : 3 * ROWS] * SCALE).astype(two_out.dtype)


def rest_kernel(
    queries, grad_out, chosen_in, prob_in, score_in, gv_own, gk_own,
    query_out, value_out, key_out,
):
    for head in range(query_out.shape[1] // HD):
        column = column_of(MOVED + head)
        far_column = column_of(head)
        for frame in range(FR_DEV):
            rows = rows_of(frame)
            score_low = score_in[head, frame]
            grad_query = dot(score_low, chosen_in[head, frame], TN)
            query_out[rows, far_column] = (grad_query * SCALE).astype(query_out.dtype)
            near = dot(score_low[:TOK_FRAME], queries[rows, column], NN)
            key_out[rows, far_column] = (gk_own[rows, far_column] + near) * SCALE
            near = dot(prob_in[head, frame, :TOK_FRAME], grad_out[rows, column], NN)
            value_out[rows, far_column] = gv_own[rows, far_column] + near


def joined(own, one, two):
    total = own[...] + one[...].astype(jnp.float32) + two[...].astype(jnp.float32)
    return total.astype(jnp.bfloat16)


def finish_kernel(order, ready, own, one, two, out, done, sems):
    ready_at, done_at = order
    moves = copy_all([(ready, out.at[:, ready_at])], sems.at[0:1])
    done[...] = joined(own, one, two)
    moves += copy_all([(done, out.at[:, done_at])], sems.at[1:2])
    for move in moves:
        move.wait()


def pair_stats(table, window, key, index, query, grad, keys, values, bias, outs):
    masked_out, grad_prob_out, parts = outs
    active, _ = pair_of(table, window, key)

    @pl.when(active)
    def _():
        for head in range(MOVED):
            column = column_of(head)
            row = slice(index * MOVED + head, index * MOVED + head + 1)
            rows = rows_of(key)
            masked = dot(keys[rows, column], query(head), NT) * SCALE2 + bias[window, key]
            highest = rounded(jnp.max(masked, 0, keepdims=True))
            raised = jnp.exp2(masked - highest)
            grad_prob = dot(values[rows, column], grad(head), NT)
            masked_out[index, key, head] = masked
            grad_prob_out[index, key, head] = grad_prob
            parts[key, 0, row] = highest
            parts[key, 1, row] = jnp.sum(raised, 0, keepdims=True)
            parts[key, 2, row] = jnp.sum(raised * grad_prob, 0, keepdims=True)

    @pl.when(jnp.logical_not(active))
    def _():
        rows = slice(index * MOVED, (index + 1) * MOVED)
        parts[key, 0, rows] = jnp.full((MOVED, TOK_FRAME), NEG, jnp.float32)
        parts[key, 1, rows] = jnp.zeros((MOVED, TOK_FRAME), jnp.float32)
        parts[key, 2, rows] = jnp.zeros((MOVED, TOK_FRAME), jnp.float32)


def own_stats_kernel(
    table, queries, grad_out, keys, values, bias,
    masked_out, grad_prob_out, stats_out,
    parts,
):
    for index in range(FR_DEV):
        for key in range(FR_DEV):
            rows = rows_of(index)
            pair_stats(
                table, FR_DEV + index, key, index,
                lambda head: queries[rows, column_of(head)],
                lambda head: grad_out[rows, column_of(head)],
                keys, values, bias, (masked_out, grad_prob_out, parts),
            )
    for index, each in enumerate(joined_stats([parts[key] for key in range(FR_DEV)])):
        stats_out[index] = each


def stats_kernel(
    table, keys, values, bias, own, f_one, f_two,
    masked_out, grad_prob_out, mine_out, one_out, two_out, far_out, other_out,
    parts,
):
    for index, window in enumerate(FAR):
        sent = f_one if window < FR_DEV else f_two
        for key in range(FR_DEV):
            rows = rows_of(window % FR_DEV)
            pair_stats(
                table, window, key, index,
                lambda head: sent[0, rows, column_of(head)],
                lambda head: sent[1, rows, column_of(head)],
                keys, values, bias, (masked_out, grad_prob_out, parts),
            )
    far = joined_stats([parts[key] for key in range(FR_DEV)])
    rank = table[RANK] % 4
    swapped = (rank == 1) | (rank == 2)
    for index in range(3):
        mine_out[index, :SIDE] = far[index][:SIDE]
        mine_out[index, SIDE : 2 * SIDE] = own[index]
        mine_out[index, 2 * SIDE :] = far[index][SIDE:]
        far_out[index] = jnp.where(swapped, far[index][SIDE:], far[index][:SIDE])
        other_out[index] = jnp.where(swapped, far[index][:SIDE], far[index][SIDE:])
    for out, start in ((one_out, 0), (two_out, SIDE)):
        rows = slice(start, start + 2 * SIDE)
        out[...] = jnp.zeros_like(out)
        notes = (mine_out[0, rows], *halves(mine_out[1, rows]), *halves(mine_out[2, rows]))
        for index, note in enumerate(notes):
            out[index * 2 * SIDE : (index + 1) * 2 * SIDE] = note


def rounded(array):
    return array.astype(jnp.bfloat16).astype(jnp.float32)


def halves(array):
    high = rounded(array)
    return high, array - high


def write_notes(notes, message):
    for half in range(2):
        message[ROWS:, half * TOK_FRAME : (half + 1) * TOK_FRAME] = notes[
            half * NOTES : (half + 1) * NOTES
        ].astype(message.dtype)


def read_notes(message, notes):
    for half in range(2):
        notes[half * NOTES : (half + 1) * NOTES] = message[
            ROWS:, half * TOK_FRAME : (half + 1) * TOK_FRAME
        ].astype(notes.dtype)
    parts = [notes[i * 2 * SIDE : (i + 1) * 2 * SIDE] for i in range(5)]
    return parts[0], parts[1] + parts[2], parts[3] + parts[4]


def joined_stats(sources):
    tops = [jnp.where(each[1] > 0, each[0], NEG) for each in sources]
    highest = tops[0]
    for top in tops[1:]:
        highest = jnp.maximum(highest, top)
    weights = [jnp.exp2(top - highest) for top in tops]
    total = sum(weight * each[1] for weight, each in zip(weights, sources))
    moment = sum(weight * each[2] for weight, each in zip(weights, sources))
    return highest, total, moment


def finish_pair(window, index, key, head, masked, grad_probs, logs, deltas):
    row = slice(window * MOVED + head, window * MOVED + head + 1)
    prob = jnp.exp2(masked[index, key, head] - logs[row])
    score_low = (prob * (grad_probs[index, key, head] - deltas[row])).astype(jnp.bfloat16)
    return prob.astype(jnp.bfloat16), score_low


def back_kernel(
    table, keys, masked, grad_probs, mine, r_one, r_two, s_far, s_other,
    prob_out, score_out, logs, deltas, one_out, two_out,
    accums, notes,
):
    side = SIDE
    rank = table[RANK] % 4
    swapped = (rank == 1) | (rank == 2)
    far = [jnp.where(swapped, s_other[i], s_far[i]) for i in range(3)]
    other = [jnp.where(swapped, s_far[i], s_other[i]) for i in range(3)]
    s_one = read_notes(r_one, notes.at[0])
    s_two = read_notes(r_two, notes.at[1])
    s_mine = [mine[i] for i in range(3)]

    def part(stats, start):
        return [each[start : start + side] for each in stats]

    groups = (
        (part(s_mine, 0), part(s_one, side), far),
        (part(s_mine, side), part(s_one, 0), part(s_two, side)),
        (part(s_mine, 2 * side), part(s_two, 0), other),
    )
    for index, sources in enumerate(groups):
        highest, total, moment = joined_stats(sources)
        rows = slice(index * side, (index + 1) * side)
        total = jnp.where(total > 0, total, 1.0)
        logs[rows] = highest + jnp.log2(total)
        deltas[rows] = moment / total
    accums[...] = jnp.zeros_like(accums)
    for index, window in enumerate(FAR):
        for key in range(FR_DEV):
            active, _ = pair_of(table, window, key)

            @pl.when(active)
            def _():
                for head in range(MOVED):
                    prob_low, score_low = finish_pair(
                        window, index, key, head, masked, grad_probs, logs, deltas
                    )
                    prob_out[index, key, head] = prob_low
                    score_out[index, key, head] = score_low
                    accums[index // FR_DEV, rows_of(index % FR_DEV), column_of(head)] += dot(
                        score_low, keys[rows_of(key), column_of(head)], TN
                    )

    one_out[...] = (accums[0] * SCALE).astype(one_out.dtype)
    two_out[...] = (accums[1] * SCALE).astype(two_out.dtype)


def home_kernel(
    table, queries, grad_out, keys, f_one, f_two, masked, grad_probs, prob_in, score_in,
    logs, deltas,
    query_out, key_out, value_out,
    key_accum, value_accum,
):
    query_out[...] = jnp.zeros_like(query_out)
    key_accum[...] = jnp.zeros_like(key_accum)
    value_accum[...] = jnp.zeros_like(value_accum)
    for window in range(WINDOW):
        rows = rows_of(window % FR_DEV)
        near = window // FR_DEV == 1
        sent = f_one if window < FR_DEV else f_two
        for key in range(FR_DEV):
            active, _ = pair_of(table, window, key)

            @pl.when(active)
            def _():
                for head in range(MOVED):
                    column = column_of(head)
                    if near:
                        query = queries[rows, column]
                        grad = grad_out[rows, column]
                        prob_low, score_low = finish_pair(
                            window, window - FR_DEV, key, head, masked, grad_probs, logs, deltas
                        )
                        query_out[rows, column] += dot(
                            score_low, keys[rows_of(key), column], TN
                        )
                    else:
                        query = sent[0, rows, column]
                        grad = sent[1, rows, column]
                        prob_low = prob_in[FAR.index(window), key, head]
                        score_low = score_in[FAR.index(window), key, head]
                    key_accum[rows_of(key), column] += dot(score_low, query, NN)
                    value_accum[rows_of(key), column] += dot(prob_low, grad, NN)

    query_out[...] = query_out[...] * SCALE
    key_out[...] = (key_accum[...] * SCALE).astype(key_out.dtype)
    value_out[...] = value_accum[...].astype(value_out.dtype)


def both_ways(pairs):
    return [pair for i, j in pairs for pair in ((i, j), (j, i))]


def swap(one, two):
    count = lax.axis_size("frames")
    first = [(i, i + 1) for i in range(0, count - 1, 2)]
    second = [(i, i + 1) for i in range(1, count - 1, 2)]
    return (
        lax.ppermute(one, "frames", both_ways(first)),
        lax.ppermute(two, "frames", both_ways(second)),
    )


def swap_far(far, other):
    count = lax.axis_size("frames")
    near = [(i, i + 2) for i in range(count - 2) if i % 4 < 2]
    over = [(i, i + 2) for i in range(count - 2) if i % 4 >= 2]
    far = lax.ppermute(far, "frames", both_ways(near))
    other = lax.ppermute(other, "frames", both_ways(over)) if over else jnp.zeros_like(other)
    return far, other


def lookup(offsets, spatial):
    rank = lax.axis_index("frames")
    first = rank * FR_DEV
    frames = offsets.shape[0]
    around = ((REACH, REACH), (0, 0))
    shifts = lax.dynamic_slice_in_dim(jnp.pad(offsets, around), first, WINDOW, 0)
    blocks = lax.dynamic_slice_in_dim(
        jnp.pad(spatial, around + ((0, 0), (0, 0))), first, WINDOW, 0
    )
    ends = jnp.stack([first, rank, jnp.full_like(rank, frames)]).astype(jnp.int32)
    return jnp.concatenate([shifts.reshape(-1), blocks.reshape(-1), ends])


def call(kernel, name, scalars, arrays, outs, scratch, flops, space=pltpu.VMEM, out_space=pltpu.VMEM):
    arrays = [pltpu.with_memory_space_constraint(array, space) for array in arrays]
    return pl.pallas_call(
        kernel,
        out_shape=outs,
        in_specs=[pl.BlockSpec(memory_space=pltpu.SMEM)] * len(scalars)
        + [pl.BlockSpec(memory_space=space)] * len(arrays),
        out_specs=tuple(pl.BlockSpec(memory_space=out_space) for _ in outs),
        scratch_shapes=scratch,
        compiler_params=pltpu.CompilerParams(vmem_limit_bytes=16 << 20),
        cost_estimate=pl.CostEstimate(flops=flops, bytes_accessed=0, transcendentals=0),
        name=name,
    )(*scalars, *arrays)


def local(queries, keys, values, grad_out, offsets, spatial):
    width = queries.shape[1]
    heads = width // HD - MOVED

    def low(*shape):
        return pltpu.VMEM(shape, jnp.bfloat16)

    def full(*shape):
        return pltpu.VMEM(shape, jnp.float32)

    unit = 2 * FR_DEV * NSEL * TOK_FRAME * TOK_FRAME * HD
    rest = width - SPLIT
    (y_send,) = call(
        pack_queries_kernel, "pack_queries", (), (queries, grad_out),
        (low(2, ROWS, SPLIT),), [pltpu.SemaphoreType.DMA((2,))], unit, pltpu.HBM,
    )
    k_send, v_send = call(
        pack_keys_kernel, "pack_keys", (), (keys, values),
        (low(ROWS, rest), low(ROWS, rest)), [pltpu.SemaphoreType.DMA((2,))], unit, pltpu.HBM,
    )
    f_one, f_two = swap(y_send, y_send)
    k_one, k_two = swap(k_send, k_send)
    table = lookup(offsets, spatial)
    query, grad, key, value, bias, moved_bias = call(
        stage_kernel, "stage", (table,), (queries, grad_out, keys, values),
        (low(ROWS, width),) * 4
        + (full(FR_DEV, SLOTS, TOK_FRAME), full(WINDOW, FR_DEV, TOK_FRAME, TOK_FRAME)),
        [pltpu.SemaphoreType.DMA((4,))], unit, pltpu.HBM,
    )
    near_grid = (FR_DEV, FR_DEV, MOVED, TOK_FRAME, TOK_FRAME)
    far_grid = (len(FAR), FR_DEV, MOVED, TOK_FRAME, TOK_FRAME)
    near_masked, near_grads, own_stats = call(
        own_stats_kernel, "own_stats", (table,), (query, grad, key, value, moved_bias),
        (full(*near_grid), full(*near_grid), full(3, SIDE, TOK_FRAME)),
        [full(FR_DEV, 3, SIDE, TOK_FRAME)], MOVED * unit,
    )
    (near_scores,) = call(
        own_scores_kernel, "own_scores", (), (query, key, bias),
        (full(heads, FR_DEV, TOK_FRAME, TOK_FRAME),), [], heads * unit // 3,
    )
    f_two, f_one, own_stats, near_scores = lax.optimization_barrier(
        (f_two, f_one, own_stats, near_scores)
    )
    note = full(2 * NOTES, TOK_FRAME)
    masked, grad_probs, mine, n_one, n_two, s_far, s_other = call(
        stats_kernel, "stats", (table,), (key, value, moved_bias, own_stats, f_one, f_two),
        (full(*far_grid), full(*far_grid), full(3, 3 * SIDE, TOK_FRAME), note, note)
        + (full(3, SIDE, TOK_FRAME),) * 2,
        [full(FR_DEV, 3, 2 * SIDE, TOK_FRAME)], 2 * MOVED * unit,
    )
    s_far, s_other = swap_far(s_far, s_other)
    v_send, mine = lax.optimization_barrier((v_send, mine))
    v_one, v_two = swap(v_send, v_send)
    k_two, k_one, s_far, s_other = lax.optimization_barrier((k_two, k_one, s_far, s_other))
    windows = low(DEPTH, 3 * ROWS, HD)
    accums = full(DEPTH, 3 * ROWS, HD)
    pairs = low(heads, FR_DEV, SLOTS, TOK_FRAME)
    chosen, prob_low, gv_own, gv_one, gv_two = call(
        values_kernel, "values_part", (table,),
        (query, grad, key, bias, near_scores, k_one, k_two, n_one, n_two),
        (low(heads, FR_DEV, SLOTS, HD), pairs, full(ROWS, rest))
        + (low(ROWS + NOTES, rest),) * 2,
        [windows, accums], 2 * heads * unit,
    )
    rv_one, rv_two = swap(gv_one, gv_two)
    score_low, gk_own, gk_one, gk_two = call(
        keys_kernel, "keys_part", (table,), (query, grad, value, prob_low, v_one, v_two),
        (pairs, full(ROWS, rest), low(ROWS, rest), low(ROWS, rest)),
        [windows, low(DEPTH, FR_DEV, SLOTS, HD), accums], 2 * heads * unit,
    )
    rk_one, rk_two = swap(gk_one, gk_two)
    y_prob, y_score, logs, deltas, gq_one, gq_two = call(
        back_kernel, "back", (table,),
        (key, masked, grad_probs, mine, rv_one, rv_two, s_far, s_other),
        (low(*far_grid), low(*far_grid)) + (full(3 * SIDE, TOK_FRAME),) * 2
        + (low(ROWS, SPLIT),) * 2,
        [full(2, ROWS, SPLIT), full(2, 2 * NOTES, TOK_FRAME)], MOVED * unit,
    )
    rq_one, rq_two = swap(gq_one, gq_two)
    score_low, logs = lax.optimization_barrier((score_low, logs))
    gq_rest, gv_own, gk_own = call(
        rest_kernel, "rest", (),
        (query, grad, chosen, prob_low, score_low, gv_own, gk_own),
        (low(ROWS, rest), full(ROWS, rest), full(ROWS, rest)), [], heads * unit,
    )
    gq_near, gk_near, gv_near = call(
        home_kernel, "home", (table,),
        (query, grad, key, f_one, f_two, near_masked, near_grads, y_prob, y_score, logs, deltas),
        (full(ROWS, SPLIT), low(ROWS, SPLIT), low(ROWS, SPLIT)),
        [full(ROWS, SPLIT), full(ROWS, SPLIT)], 3 * MOVED * unit,
    )
    grad_values = jnp.concatenate([gv_near, joined(gv_own, rv_one[:ROWS], rv_two[:ROWS])], 1)
    moved, kept = slice(0, SPLIT), slice(SPLIT, width)
    result = (pltpu.HBM((ROWS, width), jnp.bfloat16),)
    (grad_keys,) = call(
        functools.partial(finish_kernel, (moved, kept)), "last_keys", (),
        (gk_near, gk_own, rk_one, rk_two), result,
        [low(ROWS, rest), pltpu.SemaphoreType.DMA((2,))], unit, pltpu.VMEM, pltpu.HBM,
    )
    grad_keys, gq_near = lax.optimization_barrier((grad_keys, gq_near))
    (grad_queries,) = call(
        functools.partial(finish_kernel, (kept, moved)), "last_queries", (),
        (gq_rest, gq_near, rq_one, rq_two), result,
        [low(ROWS, SPLIT), pltpu.SemaphoreType.DMA((2,))], unit, pltpu.VMEM, pltpu.HBM,
    )
    return grad_queries, grad_keys, grad_values


def solution(mesh):
    rows = P(("clips", "frames"), "heads")
    return jax.shard_map(
        local,
        mesh=mesh,
        in_specs=(rows, rows, rows, rows, P("clips", None), P("clips", None, None, None)),
        out_specs=(rows, rows, rows),
        check_vma=False,
    )
```

```python
import functools
import math

import jax
import jax.numpy as jnp
from jax import lax
from jax.experimental import pallas as pl
from jax.experimental.pallas import tpu as pltpu
from jax.sharding import PartitionSpec as P

HD = 128
TOK_FRAME = 192
FR_DEV = 2
REACH = 2
NSEL = 3
SB = 4
DEPTH = 3
MOVED = 2
SPLIT = MOVED * HD
ROWS = FR_DEV * TOK_FRAME
WINDOW = FR_DEV + 2 * REACH
SLOTS = NSEL * TOK_FRAME
BLOCK = TOK_FRAME // SB
SCALE = HD ** (-0.5)
SCALE2 = SCALE * math.log2(math.e)
NEG = -(2.0**100)
NT = (((1,), (1,)), ((), ()))
NN = (((1,), (0,)), ((), ()))
TN = (((0,), (0,)), ((), ()))
MASKS = WINDOW * NSEL
FIRST = MASKS + WINDOW * NSEL * SB * SB
RANK = FIRST + 1
COUNT = FIRST + 2
NOTES = 24
SIDE = FR_DEV * MOVED
FAR = (0, 1, 4, 5)


def dot(lhs, rhs, dims):
    return lax.dot_general(lhs, rhs, dims, preferred_element_type=jnp.float32)


def column_of(head):
    return slice(head * HD, (head + 1) * HD)


def rows_of(frame):
    return slice(frame * TOK_FRAME, (frame + 1) * TOK_FRAME)


def side_of(table, side):
    return jnp.where(table[RANK] % 2 == 1, side, 2 - side)


def inside(table, place):
    target = table[FIRST] + place
    return (target >= 0) & (target < table[COUNT])


def spot_of(table, frame, slot):
    place = frame + table[(REACH + frame) * NSEL + slot]
    side = (place >= 0).astype(jnp.int32) + (place >= FR_DEV).astype(jnp.int32)
    return side_of(table, side) * FR_DEV + (place + FR_DEV) % FR_DEV


def span(table, frame, slot):
    spot = spot_of(table, frame, slot)
    return pl.ds(pl.multiple_of(spot * TOK_FRAME, TOK_FRAME), TOK_FRAME)


def pair_of(table, query, key):
    index = side_of(table, query // FR_DEV) * FR_DEV + query % FR_DEV
    place = index - REACH
    active = jnp.zeros((), jnp.int32)
    slot = jnp.zeros((), jnp.int32)
    for each in range(NSEL):
        hit = (table[index * NSEL + each] + place == key).astype(jnp.int32)
        active += hit
        slot += hit * each
    active = (active > 0) & inside(table, place)
    return active, MASKS + (index * NSEL + slot) * SB * SB


def write_bias(table, start, seen, bias, row):
    q_block = lax.broadcasted_iota(jnp.int32, (8, TOK_FRAME), 1) // BLOCK
    for k_block in range(SB):
        value = jnp.zeros((8, TOK_FRAME), jnp.float32)
        for block in range(SB):
            keep = (table[start + block * SB + k_block] > 0) & seen
            value = jnp.where(q_block == block, jnp.where(keep, 0.0, NEG), value)
        for step in range(0, BLOCK, 8):
            bias[pl.ds(row + k_block * BLOCK + step, 8), :] = value


def copy_all(pairs, sems):
    moves = [pltpu.make_async_copy(a, b, sems.at[i]) for i, (a, b) in enumerate(pairs)]
    for move in moves:
        move.start()
    return moves


def pack_queries_kernel(queries, grad_out, both, sems):
    pairs = [(queries.at[:, :SPLIT], both.at[0]), (grad_out.at[:, :SPLIT], both.at[1])]
    for move in copy_all(pairs, sems):
        move.wait()


def pack_keys_kernel(keys, values, k_send, v_send, sems):
    pairs = [(keys.at[:, SPLIT:], k_send), (values.at[:, SPLIT:], v_send)]
    for move in copy_all(pairs, sems):
        move.wait()


def stage_kernel(table, *refs):
    arrays, copies, bias, moved_bias, sems = refs[:4], refs[4:8], refs[8], refs[9], refs[10]
    moves = copy_all(list(zip(arrays, copies)), sems)
    for frame in range(FR_DEV):
        for slot in range(NSEL):
            at = (REACH + frame) * NSEL + slot
            seen = inside(table, frame + table[at])
            write_bias(table, MASKS + at * SB * SB, seen, bias.at[frame], slot * TOK_FRAME)
    for query in range(WINDOW):
        for key in range(FR_DEV):
            active, start = pair_of(table, query, key)

            @pl.when(active)
            def _():
                write_bias(table, start, active, moved_bias.at[query, key], 0)

    for move in moves:
        move.wait()


def fill_window(window, one, own, two, column, far_column):
    window[0:ROWS] = one[:, far_column]
    window[ROWS : 2 * ROWS] = own[:, column]
    window[2 * ROWS : 3 * ROWS] = two[:, far_column]


def spread(table, frame, accum, parts):
    for slot in range(1, NSEL):
        accum[span(table, frame, slot), :] += parts[rows_of(slot - 1)]


def own_scores_kernel(queries, grad_out, k_own, v_own, bias, masked_out, grad_prob_out):
    for head in range(masked_out.shape[0]):
        column = column_of(MOVED + head)
        for frame in range(FR_DEV):
            rows = rows_of(frame)
            scores = dot(k_own[rows, column], queries[rows, column], NT)
            masked_out[head, frame] = scores * SCALE2 + bias[frame, :TOK_FRAME]
            grad_prob_out[head, frame] = dot(v_own[rows, column], grad_out[rows, column], NT)


def values_kernel(
    table, queries, grad_out, k_own, bias, near_masked, k_one, k_two, n_one, n_two,
    chosen_out, prob_out, own_out, one_out, two_out,
    windows, accums,
):
    for head in range(one_out.shape[1] // HD):
        column = column_of(MOVED + head)
        far_column = column_of(head)
        window = windows.at[head % DEPTH]
        accum = accums.at[head % DEPTH]
        fill_window(window, k_one, k_own, k_two, column, far_column)
        accum[...] = jnp.zeros_like(accum)
        for frame in range(FR_DEV):
            rows = rows_of(frame)
            chosen = chosen_out.at[head, frame]
            chosen[:TOK_FRAME] = k_own[rows, column]
            for slot in range(1, NSEL):
                chosen[rows_of(slot)] = window[span(table, frame, slot), :]
            scores = dot(chosen[TOK_FRAME:], queries[rows, column], NT)
            masked = (near_masked[head, frame], scores * SCALE2 + bias[frame, TOK_FRAME:])
            highest = jnp.maximum(*(jnp.max(each, 0, keepdims=True) for each in masked))
            near, far = (jnp.exp2(each - highest) for each in masked)
            total = jnp.sum(near, 0, keepdims=True) + jnp.sum(far, 0, keepdims=True)
            inverse = 1.0 / total
            far_low = (far * inverse).astype(jnp.bfloat16)
            prob_out[head, frame, :TOK_FRAME] = (near * inverse).astype(jnp.bfloat16)
            prob_out[head, frame, TOK_FRAME:] = far_low
            spread(table, frame, accum, dot(far_low, grad_out[rows, column], NN))
        one_out[:ROWS, far_column] = accum[0:ROWS].astype(one_out.dtype)
        own_out[:, far_column] = accum[ROWS : 2 * ROWS]
        two_out[:ROWS, far_column] = accum[2 * ROWS : 3 * ROWS].astype(two_out.dtype)
    write_notes(n_one, one_out)
    write_notes(n_two, two_out)


def keys_kernel(
    table, queries, grad_out, v_own, near_grads, prob_in, v_one, v_two,
    score_out, own_out, one_out, two_out,
    windows, choices, accums,
):
    for head in range(one_out.shape[1] // HD):
        column = column_of(MOVED + head)
        far_column = column_of(head)
        window = windows.at[head % DEPTH]
        accum = accums.at[head % DEPTH]
        fill_window(window, v_one, v_own, v_two, column, far_column)
        accum[...] = jnp.zeros_like(accum)
        for frame in range(FR_DEV):
            rows = rows_of(frame)
            chosen = choices.at[head % DEPTH, frame]
            for slot in range(1, NSEL):
                chosen[rows_of(slot - 1)] = window[span(table, frame, slot), :]
            near_grad = near_grads[head, frame]
            far_grad = dot(chosen[...], grad_out[rows, column], NT)
            near = prob_in[head, frame, :TOK_FRAME].astype(jnp.float32)
            far = prob_in[head, frame, TOK_FRAME:].astype(jnp.float32)
            delta = jnp.sum(near * near_grad, 0, keepdims=True)
            delta += jnp.sum(far * far_grad, 0, keepdims=True)
            far_low = (far * (far_grad - delta)).astype(jnp.bfloat16)
            score_out[head, frame, :TOK_FRAME] = (near * (near_grad - delta)).astype(jnp.bfloat16)
            score_out[head, frame, TOK_FRAME:] = far_low
            spread(table, frame, accum, dot(far_low, queries[rows, column], NN))
        one_out[:, far_column] = (accum[0:ROWS] * SCALE).astype(one_out.dtype)
        own_out[:, far_column] = accum[ROWS : 2 * ROWS]
        two_out[:, far_column] = (accum[2 * ROWS : 3 * ROWS] * SCALE).astype(two_out.dtype)


def rest_kernel(
    queries, grad_out, chosen_in, prob_in, score_in, gv_own, gk_own,
    query_out, value_out, key_out,
):
    for head in range(query_out.shape[1] // HD):
        column = column_of(MOVED + head)
        far_column = column_of(head)
        for frame in range(FR_DEV):
            rows = rows_of(frame)
            score_low = score_in[head, frame]
            grad_query = dot(score_low, chosen_in[head, frame], TN)
            query_out[rows, far_column] = (grad_query * SCALE).astype(query_out.dtype)
            near = dot(score_low[:TOK_FRAME], queries[rows, column], NN)
            key_out[rows, far_column] = (gk_own[rows, far_column] + near) * SCALE
            near = dot(prob_in[head, frame, :TOK_FRAME], grad_out[rows, column], NN)
            value_out[rows, far_column] = gv_own[rows, far_column] + near


def joined(own, one, two):
    total = own[...] + one[...].astype(jnp.float32) + two[...].astype(jnp.float32)
    return total.astype(jnp.bfloat16)


def finish_kernel(order, ready, own, one, two, out, done, sems):
    ready_at, done_at = order
    moves = copy_all([(ready, out.at[:, ready_at])], sems.at[0:1])
    done[...] = joined(own, one, two)
    moves += copy_all([(done, out.at[:, done_at])], sems.at[1:2])
    for move in moves:
        move.wait()


def pair_stats(table, window, key, index, query, grad, keys, values, bias, outs):
    masked_out, grad_prob_out, parts = outs
    active, _ = pair_of(table, window, key)

    @pl.when(active)
    def _():
        for head in range(MOVED):
            column = column_of(head)
            row = slice(index * MOVED + head, index * MOVED + head + 1)
            rows = rows_of(key)
            masked = dot(keys[rows, column], query(head), NT) * SCALE2 + bias[window, key]
            highest = rounded(jnp.max(masked, 0, keepdims=True))
            raised = jnp.exp2(masked - highest)
            grad_prob = dot(values[rows, column], grad(head), NT)
            masked_out[index, key, head] = masked
            grad_prob_out[index, key, head] = grad_prob
            parts[key, 0, row] = highest
            parts[key, 1, row] = jnp.sum(raised, 0, keepdims=True)
            parts[key, 2, row] = jnp.sum(raised * grad_prob, 0, keepdims=True)

    @pl.when(jnp.logical_not(active))
    def _():
        rows = slice(index * MOVED, (index + 1) * MOVED)
        parts[key, 0, rows] = jnp.full((MOVED, TOK_FRAME), NEG, jnp.float32)
        parts[key, 1, rows] = jnp.zeros((MOVED, TOK_FRAME), jnp.float32)
        parts[key, 2, rows] = jnp.zeros((MOVED, TOK_FRAME), jnp.float32)


def own_stats_kernel(
    table, queries, grad_out, keys, values, bias,
    masked_out, grad_prob_out, stats_out,
    parts,
):
    for index in range(FR_DEV):
        for key in range(FR_DEV):
            rows = rows_of(index)
            pair_stats(
                table, FR_DEV + index, key, index,
                lambda head: queries[rows, column_of(head)],
                lambda head: grad_out[rows, column_of(head)],
                keys, values, bias, (masked_out, grad_prob_out, parts),
            )
    for index, each in enumerate(joined_stats([parts[key] for key in range(FR_DEV)])):
        stats_out[index] = each


def stats_kernel(
    table, keys, values, bias, own, f_one, f_two,
    masked_out, grad_prob_out, mine_out, one_out, two_out, far_out, other_out,
    parts,
):
    for index, window in enumerate(FAR):
        sent = f_one if window < FR_DEV else f_two
        for key in range(FR_DEV):
            rows = rows_of(window % FR_DEV)
            pair_stats(
                table, window, key, index,
                lambda head: sent[0, rows, column_of(head)],
                lambda head: sent[1, rows, column_of(head)],
                keys, values, bias, (masked_out, grad_prob_out, parts),
            )
    far = joined_stats([parts[key] for key in range(FR_DEV)])
    rank = table[RANK] % 4
    swapped = (rank == 1) | (rank == 2)
    for index in range(3):
        mine_out[index, :SIDE] = far[index][:SIDE]
        mine_out[index, SIDE : 2 * SIDE] = own[index]
        mine_out[index, 2 * SIDE :] = far[index][SIDE:]
        far_out[index] = jnp.where(swapped, far[index][SIDE:], far[index][:SIDE])
        other_out[index] = jnp.where(swapped, far[index][:SIDE], far[index][SIDE:])
    for out, start in ((one_out, 0), (two_out, SIDE)):
        rows = slice(start, start + 2 * SIDE)
        out[...] = jnp.zeros_like(out)
        notes = (mine_out[0, rows], *halves(mine_out[1, rows]), *halves(mine_out[2, rows]))
        for index, note in enumerate(notes):
            out[index * 2 * SIDE : (index + 1) * 2 * SIDE] = note


def rounded(array):
    return array.astype(jnp.bfloat16).astype(jnp.float32)


def halves(array):
    high = rounded(array)
    return high, array - high


def write_notes(notes, message):
    for half in range(2):
        message[ROWS:, half * TOK_FRAME : (half + 1) * TOK_FRAME] = notes[
            half * NOTES : (half + 1) * NOTES
        ].astype(message.dtype)


def read_notes(message, notes):
    for half in range(2):
        notes[half * NOTES : (half + 1) * NOTES] = message[
            ROWS:, half * TOK_FRAME : (half + 1) * TOK_FRAME
        ].astype(notes.dtype)
    parts = [notes[i * 2 * SIDE : (i + 1) * 2 * SIDE] for i in range(5)]
    return parts[0], parts[1] + parts[2], parts[3] + parts[4]


def joined_stats(sources):
    tops = [jnp.where(each[1] > 0, each[0], NEG) for each in sources]
    highest = tops[0]
    for top in tops[1:]:
        highest = jnp.maximum(highest, top)
    weights = [jnp.exp2(top - highest) for top in tops]
    total = sum(weight * each[1] for weight, each in zip(weights, sources))
    moment = sum(weight * each[2] for weight, each in zip(weights, sources))
    return highest, total, moment


def finish_pair(window, index, key, head, masked, grad_probs, logs, deltas):
    row = slice(window * MOVED + head, window * MOVED + head + 1)
    prob = jnp.exp2(masked[index, key, head] - logs[row])
    score_low = (prob * (grad_probs[index, key, head] - deltas[row])).astype(jnp.bfloat16)
    return prob.astype(jnp.bfloat16), score_low


def back_kernel(
    table, keys, masked, grad_probs, mine, r_one, r_two, s_far, s_other,
    prob_out, score_out, logs, deltas, one_out, two_out,
    accums, notes,
):
    side = SIDE
    rank = table[RANK] % 4
    swapped = (rank == 1) | (rank == 2)
    far = [jnp.where(swapped, s_other[i], s_far[i]) for i in range(3)]
    other = [jnp.where(swapped, s_far[i], s_other[i]) for i in range(3)]
    s_one = read_notes(r_one, notes.at[0])
    s_two = read_notes(r_two, notes.at[1])
    s_mine = [mine[i] for i in range(3)]

    def part(stats, start):
        return [each[start : start + side] for each in stats]

    groups = (
        (part(s_mine, 0), part(s_one, side), far),
        (part(s_mine, side), part(s_one, 0), part(s_two, side)),
        (part(s_mine, 2 * side), part(s_two, 0), other),
    )
    for index, sources in enumerate(groups):
        highest, total, moment = joined_stats(sources)
        rows = slice(index * side, (index + 1) * side)
        total = jnp.where(total > 0, total, 1.0)
        logs[rows] = highest + jnp.log2(total)
        deltas[rows] = moment / total
    accums[...] = jnp.zeros_like(accums)
    for index, window in enumerate(FAR):
        for key in range(FR_DEV):
            active, _ = pair_of(table, window, key)

            @pl.when(active)
            def _():
                for head in range(MOVED):
                    prob_low, score_low = finish_pair(
                        window, index, key, head, masked, grad_probs, logs, deltas
                    )
                    prob_out[index, key, head] = prob_low
                    score_out[index, key, head] = score_low
                    accums[index // FR_DEV, rows_of(index % FR_DEV), column_of(head)] += dot(
                        score_low, keys[rows_of(key), column_of(head)], TN
                    )

    one_out[...] = (accums[0] * SCALE).astype(one_out.dtype)
    two_out[...] = (accums[1] * SCALE).astype(two_out.dtype)


def home_kernel(
    table, queries, grad_out, keys, f_one, f_two, masked, grad_probs, prob_in, score_in,
    logs, deltas,
    query_out, key_out, value_out,
    key_accum, value_accum,
):
    query_out[...] = jnp.zeros_like(query_out)
    key_accum[...] = jnp.zeros_like(key_accum)
    value_accum[...] = jnp.zeros_like(value_accum)
    for window in range(WINDOW):
        rows = rows_of(window % FR_DEV)
        near = window // FR_DEV == 1
        sent = f_one if window < FR_DEV else f_two
        for key in range(FR_DEV):
            active, _ = pair_of(table, window, key)

            @pl.when(active)
            def _():
                for head in range(MOVED):
                    column = column_of(head)
                    if near:
                        query = queries[rows, column]
                        grad = grad_out[rows, column]
                        prob_low, score_low = finish_pair(
                            window, window - FR_DEV, key, head, masked, grad_probs, logs, deltas
                        )
                        query_out[rows, column] += dot(
                            score_low, keys[rows_of(key), column], TN
                        )
                    else:
                        query = sent[0, rows, column]
                        grad = sent[1, rows, column]
                        prob_low = prob_in[FAR.index(window), key, head]
                        score_low = score_in[FAR.index(window), key, head]
                    key_accum[rows_of(key), column] += dot(score_low, query, NN)
                    value_accum[rows_of(key), column] += dot(prob_low, grad, NN)

    query_out[...] = query_out[...] * SCALE
    key_out[...] = (key_accum[...] * SCALE).astype(key_out.dtype)
    value_out[...] = value_accum[...].astype(value_out.dtype)


def both_ways(pairs):
    return [pair for i, j in pairs for pair in ((i, j), (j, i))]


def swap(one, two):
    count = lax.axis_size("frames")
    first = [(i, i + 1) for i in range(0, count - 1, 2)]
    second = [(i, i + 1) for i in range(1, count - 1, 2)]
    return (
        lax.ppermute(one, "frames", both_ways(first)),
        lax.ppermute(two, "frames", both_ways(second)),
    )


def swap_far(far, other):
    count = lax.axis_size("frames")
    near = [(i, i + 2) for i in range(count - 2) if i % 4 < 2]
    over = [(i, i + 2) for i in range(count - 2) if i % 4 >= 2]
    far = lax.ppermute(far, "frames", both_ways(near))
    other = lax.ppermute(other, "frames", both_ways(over)) if over else jnp.zeros_like(other)
    return far, other


def lookup(offsets, spatial):
    rank = lax.axis_index("frames")
    first = rank * FR_DEV
    frames = offsets.shape[0]
    around = ((REACH, REACH), (0, 0))
    shifts = lax.dynamic_slice_in_dim(jnp.pad(offsets, around), first, WINDOW, 0)
    blocks = lax.dynamic_slice_in_dim(
        jnp.pad(spatial, around + ((0, 0), (0, 0))), first, WINDOW, 0
    )
    ends = jnp.stack([first, rank, jnp.full_like(rank, frames)]).astype(jnp.int32)
    return jnp.concatenate([shifts.reshape(-1), blocks.reshape(-1), ends])


def call(kernel, name, scalars, arrays, outs, scratch, flops, space=pltpu.VMEM, out_space=pltpu.VMEM):
    arrays = [pltpu.with_memory_space_constraint(array, space) for array in arrays]
    return pl.pallas_call(
        kernel,
        out_shape=outs,
        in_specs=[pl.BlockSpec(memory_space=pltpu.SMEM)] * len(scalars)
        + [pl.BlockSpec(memory_space=space)] * len(arrays),
        out_specs=tuple(pl.BlockSpec(memory_space=out_space) for _ in outs),
        scratch_shapes=scratch,
        compiler_params=pltpu.CompilerParams(vmem_limit_bytes=16 << 20),
        cost_estimate=pl.CostEstimate(flops=flops, bytes_accessed=0, transcendentals=0),
        name=name,
    )(*scalars, *arrays)


def local(queries, keys, values, grad_out, offsets, spatial):
    width = queries.shape[1]
    heads = width // HD - MOVED

    def low(*shape):
        return pltpu.VMEM(shape, jnp.bfloat16)

    def full(*shape):
        return pltpu.VMEM(shape, jnp.float32)

    unit = 2 * FR_DEV * NSEL * TOK_FRAME * TOK_FRAME * HD
    rest = width - SPLIT
    (y_send,) = call(
        pack_queries_kernel, "pack_queries", (), (queries, grad_out),
        (low(2, ROWS, SPLIT),), [pltpu.SemaphoreType.DMA((2,))], unit, pltpu.HBM,
    )
    k_send, v_send = call(
        pack_keys_kernel, "pack_keys", (), (keys, values),
        (low(ROWS, rest), low(ROWS, rest)), [pltpu.SemaphoreType.DMA((2,))], unit, pltpu.HBM,
    )
    f_one, f_two = swap(y_send, y_send)
    k_one, k_two = swap(k_send, k_send)
    table = lookup(offsets, spatial)
    query, grad, key, value, bias, moved_bias = call(
        stage_kernel, "stage", (table,), (queries, grad_out, keys, values),
        (low(ROWS, width),) * 4
        + (full(FR_DEV, SLOTS, TOK_FRAME), full(WINDOW, FR_DEV, TOK_FRAME, TOK_FRAME)),
        [pltpu.SemaphoreType.DMA((4,))], unit, pltpu.HBM,
    )
    near_grid = (FR_DEV, FR_DEV, MOVED, TOK_FRAME, TOK_FRAME)
    far_grid = (len(FAR), FR_DEV, MOVED, TOK_FRAME, TOK_FRAME)
    near_masked, near_grads, own_stats = call(
        own_stats_kernel, "own_stats", (table,), (query, grad, key, value, moved_bias),
        (full(*near_grid), full(*near_grid), full(3, SIDE, TOK_FRAME)),
        [full(FR_DEV, 3, SIDE, TOK_FRAME)], MOVED * unit,
    )
    near_scores, rest_grads = call(
        own_scores_kernel, "own_scores", (), (query, grad, key, value, bias),
        (full(heads, FR_DEV, TOK_FRAME, TOK_FRAME),) * 2, [], heads * unit // 2,
    )
    f_two, f_one, own_stats, near_scores = lax.optimization_barrier(
        (f_two, f_one, own_stats, near_scores)
    )
    note = full(2 * NOTES, TOK_FRAME)
    masked, grad_probs, mine, n_one, n_two, s_far, s_other = call(
        stats_kernel, "stats", (table,), (key, value, moved_bias, own_stats, f_one, f_two),
        (full(*far_grid), full(*far_grid), full(3, 3 * SIDE, TOK_FRAME), note, note)
        + (full(3, SIDE, TOK_FRAME),) * 2,
        [full(FR_DEV, 3, 2 * SIDE, TOK_FRAME)], 2 * MOVED * unit,
    )
    s_far, s_other = swap_far(s_far, s_other)
    v_send, mine = lax.optimization_barrier((v_send, mine))
    v_one, v_two = swap(v_send, v_send)
    k_two, k_one, s_far, s_other = lax.optimization_barrier((k_two, k_one, s_far, s_other))
    windows = low(DEPTH, 3 * ROWS, HD)
    accums = full(DEPTH, 3 * ROWS, HD)
    pairs = low(heads, FR_DEV, SLOTS, TOK_FRAME)
    chosen, prob_low, gv_own, gv_one, gv_two = call(
        values_kernel, "values_part", (table,),
        (query, grad, key, bias, near_scores, k_one, k_two, n_one, n_two),
        (low(heads, FR_DEV, SLOTS, HD), pairs, full(ROWS, rest))
        + (low(ROWS + NOTES, rest),) * 2,
        [windows, accums], 2 * heads * unit,
    )
    rv_one, rv_two = swap(gv_one, gv_two)
    score_low, gk_own, gk_one, gk_two = call(
        keys_kernel, "keys_part", (table,),
        (query, grad, value, rest_grads, prob_low, v_one, v_two),
        (pairs, full(ROWS, rest), low(ROWS, rest), low(ROWS, rest)),
        [windows, low(DEPTH, FR_DEV, SLOTS - TOK_FRAME, HD), accums], 2 * heads * unit,
    )
    rk_one, rk_two = swap(gk_one, gk_two)
    y_prob, y_score, logs, deltas, gq_one, gq_two = call(
        back_kernel, "back", (table,),
        (key, masked, grad_probs, mine, rv_one, rv_two, s_far, s_other),
        (low(*far_grid), low(*far_grid)) + (full(3 * SIDE, TOK_FRAME),) * 2
        + (low(ROWS, SPLIT),) * 2,
        [full(2, ROWS, SPLIT), full(2, 2 * NOTES, TOK_FRAME)], MOVED * unit,
    )
    rq_one, rq_two = swap(gq_one, gq_two)
    score_low, logs = lax.optimization_barrier((score_low, logs))
    gq_rest, gv_own, gk_own = call(
        rest_kernel, "rest", (),
        (query, grad, chosen, prob_low, score_low, gv_own, gk_own),
        (low(ROWS, rest), full(ROWS, rest), full(ROWS, rest)), [], heads * unit,
    )
    gq_near, gk_near, gv_near = call(
        home_kernel, "home", (table,),
        (query, grad, key, f_one, f_two, near_masked, near_grads, y_prob, y_score, logs, deltas),
        (full(ROWS, SPLIT), low(ROWS, SPLIT), low(ROWS, SPLIT)),
        [full(ROWS, SPLIT), full(ROWS, SPLIT)], 3 * MOVED * unit,
    )
    grad_values = jnp.concatenate([gv_near, joined(gv_own, rv_one[:ROWS], rv_two[:ROWS])], 1)
    moved, kept = slice(0, SPLIT), slice(SPLIT, width)
    result = (pltpu.HBM((ROWS, width), jnp.bfloat16),)
    (grad_keys,) = call(
        functools.partial(finish_kernel, (moved, kept)), "last_keys", (),
        (gk_near, gk_own, rk_one, rk_two), result,
        [low(ROWS, rest), pltpu.SemaphoreType.DMA((2,))], unit, pltpu.VMEM, pltpu.HBM,
    )
    grad_keys, gq_near = lax.optimization_barrier((grad_keys, gq_near))
    (grad_queries,) = call(
        functools.partial(finish_kernel, (kept, moved)), "last_queries", (),
        (gq_rest, gq_near, rq_one, rq_two), result,
        [low(ROWS, SPLIT), pltpu.SemaphoreType.DMA((2,))], unit, pltpu.VMEM, pltpu.HBM,
    )
    return grad_queries, grad_keys, grad_values


def solution(mesh):
    rows = P(("clips", "frames"), "heads")
    return jax.shard_map(
        local,
        mesh=mesh,
        in_specs=(rows, rows, rows, rows, P("clips", None), P("clips", None, None, None)),
        out_specs=(rows, rows, rows),
        check_vma=False,
    )
```

```python
import functools
import math

import jax
import jax.numpy as jnp
from jax import lax
from jax.experimental import pallas as pl
from jax.experimental.pallas import tpu as pltpu
from jax.sharding import PartitionSpec as P

HD = 128
TOK_FRAME = 192
FR_DEV = 2
REACH = 2
NSEL = 3
SB = 4
DEPTH = 3
MOVED = 2
SPLIT = MOVED * HD
ROWS = FR_DEV * TOK_FRAME
WINDOW = FR_DEV + 2 * REACH
SLOTS = NSEL * TOK_FRAME
BLOCK = TOK_FRAME // SB
SCALE = HD ** (-0.5)
SCALE2 = SCALE * math.log2(math.e)
NEG = -(2.0**100)
NT = (((1,), (1,)), ((), ()))
NN = (((1,), (0,)), ((), ()))
TN = (((0,), (0,)), ((), ()))
MASKS = WINDOW * NSEL
FIRST = MASKS + WINDOW * NSEL * SB * SB
RANK = FIRST + 1
COUNT = FIRST + 2
NOTES = 24
SIDE = FR_DEV * MOVED
FAR = (0, 1, 4, 5)


def dot(lhs, rhs, dims):
    return lax.dot_general(lhs, rhs, dims, preferred_element_type=jnp.float32)


def column_of(head):
    return slice(head * HD, (head + 1) * HD)


def rows_of(frame):
    return slice(frame * TOK_FRAME, (frame + 1) * TOK_FRAME)


def side_of(table, side):
    return jnp.where(table[RANK] % 2 == 1, side, 2 - side)


def inside(table, place):
    target = table[FIRST] + place
    return (target >= 0) & (target < table[COUNT])


def spot_of(table, frame, slot):
    place = frame + table[(REACH + frame) * NSEL + slot]
    side = (place >= 0).astype(jnp.int32) + (place >= FR_DEV).astype(jnp.int32)
    return side_of(table, side) * FR_DEV + (place + FR_DEV) % FR_DEV


def span(table, frame, slot):
    spot = spot_of(table, frame, slot)
    return pl.ds(pl.multiple_of(spot * TOK_FRAME, TOK_FRAME), TOK_FRAME)


def pair_of(table, query, key):
    index = side_of(table, query // FR_DEV) * FR_DEV + query % FR_DEV
    place = index - REACH
    active = jnp.zeros((), jnp.int32)
    slot = jnp.zeros((), jnp.int32)
    for each in range(NSEL):
        hit = (table[index * NSEL + each] + place == key).astype(jnp.int32)
        active += hit
        slot += hit * each
    active = (active > 0) & inside(table, place)
    return active, MASKS + (index * NSEL + slot) * SB * SB


def write_bias(table, start, seen, bias, row):
    q_block = lax.broadcasted_iota(jnp.int32, (8, TOK_FRAME), 1) // BLOCK
    for k_block in range(SB):
        value = jnp.zeros((8, TOK_FRAME), jnp.float32)
        for block in range(SB):
            keep = (table[start + block * SB + k_block] > 0) & seen
            value = jnp.where(q_block == block, jnp.where(keep, 0.0, NEG), value)
        for step in range(0, BLOCK, 8):
            bias[pl.ds(row + k_block * BLOCK + step, 8), :] = value


def copy_all(pairs, sems):
    moves = [pltpu.make_async_copy(a, b, sems.at[i]) for i, (a, b) in enumerate(pairs)]
    for move in moves:
        move.start()
    return moves


def pack_queries_kernel(queries, grad_out, both, sems):
    pairs = [(queries.at[:, :SPLIT], both.at[0]), (grad_out.at[:, :SPLIT], both.at[1])]
    for move in copy_all(pairs, sems):
        move.wait()


def pack_keys_kernel(keys, values, k_send, v_send, sems):
    pairs = [(keys.at[:, SPLIT:], k_send), (values.at[:, SPLIT:], v_send)]
    for move in copy_all(pairs, sems):
        move.wait()


def stage_kernel(table, *refs):
    arrays, copies, bias, moved_bias, sems = refs[:4], refs[4:8], refs[8], refs[9], refs[10]
    moves = copy_all(list(zip(arrays, copies)), sems)
    for frame in range(FR_DEV):
        for slot in range(NSEL):
            at = (REACH + frame) * NSEL + slot
            seen = inside(table, frame + table[at])
            write_bias(table, MASKS + at * SB * SB, seen, bias.at[frame], slot * TOK_FRAME)
    for query in range(WINDOW):
        for key in range(FR_DEV):
            active, start = pair_of(table, query, key)

            @pl.when(active)
            def _():
                write_bias(table, start, active, moved_bias.at[query, key], 0)

    for move in moves:
        move.wait()


def fill_window(window, one, own, two, column, far_column):
    window[0:ROWS] = one[:, far_column]
    window[ROWS : 2 * ROWS] = own[:, column]
    window[2 * ROWS : 3 * ROWS] = two[:, far_column]


def spread(table, frame, accum, parts):
    for slot in range(1, NSEL):
        accum[span(table, frame, slot), :] += parts[rows_of(slot - 1)]


def own_scores_kernel(queries, grad_out, k_own, v_own, bias, masked_out, grad_prob_out):
    for head in range(masked_out.shape[0]):
        column = column_of(MOVED + head)
        for frame in range(FR_DEV):
            rows = rows_of(frame)
            scores = dot(k_own[rows, column], queries[rows, column], NT)
            masked_out[head, frame] = scores * SCALE2 + bias[frame, :TOK_FRAME]
            grad_prob_out[head, frame] = dot(v_own[rows, column], grad_out[rows, column], NT)


def values_kernel(
    table, queries, grad_out, k_own, bias, near_masked, k_one, k_two, n_one, n_two,
    chosen_out, prob_out, own_out, one_out, two_out,
    windows, accums,
):
    for head in range(one_out.shape[1] // HD):
        column = column_of(MOVED + head)
        far_column = column_of(head)
        window = windows.at[head % DEPTH]
        accum = accums.at[head % DEPTH]
        fill_window(window, k_one, k_own, k_two, column, far_column)
        accum[...] = jnp.zeros_like(accum)
        for frame in range(FR_DEV):
            rows = rows_of(frame)
            chosen = chosen_out.at[head, frame]
            chosen[:TOK_FRAME] = k_own[rows, column]
            for slot in range(1, NSEL):
                chosen[rows_of(slot)] = window[span(table, frame, slot), :]
            scores = dot(chosen[TOK_FRAME:], queries[rows, column], NT)
            masked = (near_masked[head, frame], scores * SCALE2 + bias[frame, TOK_FRAME:])
            highest = jnp.maximum(*(jnp.max(each, 0, keepdims=True) for each in masked))
            near, far = (jnp.exp2(each - highest) for each in masked)
            total = jnp.sum(near, 0, keepdims=True) + jnp.sum(far, 0, keepdims=True)
            inverse = 1.0 / total
            far_low = (far * inverse).astype(jnp.bfloat16)
            prob_out[head, frame, :TOK_FRAME] = (near * inverse).astype(jnp.bfloat16)
            prob_out[head, frame, TOK_FRAME:] = far_low
            spread(table, frame, accum, dot(far_low, grad_out[rows, column], NN))
        one_out[:ROWS, far_column] = accum[0:ROWS].astype(one_out.dtype)
        own_out[:, far_column] = accum[ROWS : 2 * ROWS]
        two_out[:ROWS, far_column] = accum[2 * ROWS : 3 * ROWS].astype(two_out.dtype)
    write_notes(n_one, one_out)
    write_notes(n_two, two_out)


def keys_kernel(
    table, queries, grad_out, v_own, near_grads, prob_in, v_one, v_two,
    score_out, own_out, one_out, two_out,
    windows, choices, accums,
):
    for head in range(one_out.shape[1] // HD):
        column = column_of(MOVED + head)
        far_column = column_of(head)
        window = windows.at[head % DEPTH]
        accum = accums.at[head % DEPTH]
        fill_window(window, v_one, v_own, v_two, column, far_column)
        accum[...] = jnp.zeros_like(accum)
        for frame in range(FR_DEV):
            rows = rows_of(frame)
            chosen = choices.at[head % DEPTH, frame]
            for slot in range(1, NSEL):
                chosen[rows_of(slot - 1)] = window[span(table, frame, slot), :]
            near_grad = near_grads[head, frame]
            far_grad = dot(chosen[...], grad_out[rows, column], NT)
            near = prob_in[head, frame, :TOK_FRAME].astype(jnp.float32)
            far = prob_in[head, frame, TOK_FRAME:].astype(jnp.float32)
            delta = jnp.sum(near * near_grad, 0, keepdims=True)
            delta += jnp.sum(far * far_grad, 0, keepdims=True)
            far_low = (far * (far_grad - delta)).astype(jnp.bfloat16)
            score_out[head, frame, :TOK_FRAME] = (near * (near_grad - delta)).astype(jnp.bfloat16)
            score_out[head, frame, TOK_FRAME:] = far_low
            spread(table, frame, accum, dot(far_low, queries[rows, column], NN))
        one_out[:, far_column] = (accum[0:ROWS] * SCALE).astype(one_out.dtype)
        own_out[:, far_column] = accum[ROWS : 2 * ROWS]
        two_out[:, far_column] = (accum[2 * ROWS : 3 * ROWS] * SCALE).astype(two_out.dtype)


def rest_kernel(
    queries, grad_out, chosen_in, prob_in, score_in, gv_own, gk_own,
    query_out, value_out, key_out,
):
    for head in range(query_out.shape[1] // HD):
        column = column_of(MOVED + head)
        far_column = column_of(head)
        for frame in range(FR_DEV):
            rows = rows_of(frame)
            score_low = score_in[head, frame]
            grad_query = dot(score_low, chosen_in[head, frame], TN)
            query_out[rows, far_column] = (grad_query * SCALE).astype(query_out.dtype)
            near = dot(score_low[:TOK_FRAME], queries[rows, column], NN)
            key_out[rows, far_column] = (gk_own[rows, far_column] + near) * SCALE
            near = dot(prob_in[head, frame, :TOK_FRAME], grad_out[rows, column], NN)
            value_out[rows, far_column] = gv_own[rows, far_column] + near


def joined(own, one, two):
    total = own[...] + one[...].astype(jnp.float32) + two[...].astype(jnp.float32)
    return total.astype(jnp.bfloat16)


def finish_kernel(order, ready, own, one, two, out, done, sems):
    ready_at, done_at = order
    moves = copy_all([(ready, out.at[:, ready_at])], sems.at[0:1])
    done[...] = joined(own, one, two)
    moves += copy_all([(done, out.at[:, done_at])], sems.at[1:2])
    for move in moves:
        move.wait()


def pair_stats(table, window, key, index, query, grad, keys, values, bias, outs):
    masked_out, grad_prob_out, parts = outs
    active, _ = pair_of(table, window, key)

    @pl.when(active)
    def _():
        for head in range(MOVED):
            column = column_of(head)
            row = slice(index * MOVED + head, index * MOVED + head + 1)
            rows = rows_of(key)
            masked = dot(keys[rows, column], query(head), NT) * SCALE2 + bias[window, key]
            highest = rounded(jnp.max(masked, 0, keepdims=True))
            raised = jnp.exp2(masked - highest)
            grad_prob = dot(values[rows, column], grad(head), NT)
            masked_out[index, key, head] = masked
            grad_prob_out[index, key, head] = grad_prob
            parts[key, 0, row] = highest
            parts[key, 1, row] = jnp.sum(raised, 0, keepdims=True)
            parts[key, 2, row] = jnp.sum(raised * grad_prob, 0, keepdims=True)

    @pl.when(jnp.logical_not(active))
    def _():
        rows = slice(index * MOVED, (index + 1) * MOVED)
        parts[key, 0, rows] = jnp.full((MOVED, TOK_FRAME), NEG, jnp.float32)
        parts[key, 1, rows] = jnp.zeros((MOVED, TOK_FRAME), jnp.float32)
        parts[key, 2, rows] = jnp.zeros((MOVED, TOK_FRAME), jnp.float32)


def own_stats_kernel(
    table, queries, grad_out, keys, values, bias,
    masked_out, grad_prob_out, stats_out,
    parts,
):
    for index in range(FR_DEV):
        for key in range(FR_DEV):
            rows = rows_of(index)
            pair_stats(
                table, FR_DEV + index, key, index,
                lambda head: queries[rows, column_of(head)],
                lambda head: grad_out[rows, column_of(head)],
                keys, values, bias, (masked_out, grad_prob_out, parts),
            )
    for index, each in enumerate(joined_stats([parts[key] for key in range(FR_DEV)])):
        stats_out[index] = each


def stats_kernel(
    table, keys, values, bias, own, f_one, f_two,
    masked_out, grad_prob_out, mine_out, one_out, two_out, far_out, other_out,
    parts,
):
    for index, window in enumerate(FAR):
        sent = f_one if window < FR_DEV else f_two
        for key in range(FR_DEV):
            rows = rows_of(window % FR_DEV)
            pair_stats(
                table, window, key, index,
                lambda head: sent[0, rows, column_of(head)],
                lambda head: sent[1, rows, column_of(head)],
                keys, values, bias, (masked_out, grad_prob_out, parts),
            )
    far = joined_stats([parts[key] for key in range(FR_DEV)])
    rank = table[RANK] % 4
    swapped = (rank == 1) | (rank == 2)
    for index in range(3):
        mine_out[index, :SIDE] = far[index][:SIDE]
        mine_out[index, SIDE : 2 * SIDE] = own[index]
        mine_out[index, 2 * SIDE :] = far[index][SIDE:]
        far_out[index] = jnp.where(swapped, far[index][SIDE:], far[index][:SIDE])
        other_out[index] = jnp.where(swapped, far[index][:SIDE], far[index][SIDE:])
    for out, start in ((one_out, 0), (two_out, SIDE)):
        rows = slice(start, start + 2 * SIDE)
        out[...] = jnp.zeros_like(out)
        notes = (mine_out[0, rows], *halves(mine_out[1, rows]), *halves(mine_out[2, rows]))
        for index, note in enumerate(notes):
            out[index * 2 * SIDE : (index + 1) * 2 * SIDE] = note


def rounded(array):
    return array.astype(jnp.bfloat16).astype(jnp.float32)


def halves(array):
    high = rounded(array)
    return high, array - high


def write_notes(notes, message):
    for half in range(2):
        message[ROWS:, half * TOK_FRAME : (half + 1) * TOK_FRAME] = notes[
            half * NOTES : (half + 1) * NOTES
        ].astype(message.dtype)


def read_notes(message, notes):
    for half in range(2):
        notes[half * NOTES : (half + 1) * NOTES] = message[
            ROWS:, half * TOK_FRAME : (half + 1) * TOK_FRAME
        ].astype(notes.dtype)
    parts = [notes[i * 2 * SIDE : (i + 1) * 2 * SIDE] for i in range(5)]
    return parts[0], parts[1] + parts[2], parts[3] + parts[4]


def joined_stats(sources):
    tops = [jnp.where(each[1] > 0, each[0], NEG) for each in sources]
    highest = tops[0]
    for top in tops[1:]:
        highest = jnp.maximum(highest, top)
    weights = [jnp.exp2(top - highest) for top in tops]
    total = sum(weight * each[1] for weight, each in zip(weights, sources))
    moment = sum(weight * each[2] for weight, each in zip(weights, sources))
    return highest, total, moment


def finish_pair(window, index, key, head, masked, grad_probs, logs, deltas):
    row = slice(window * MOVED + head, window * MOVED + head + 1)
    prob = jnp.exp2(masked[index, key, head] - logs[row])
    score_low = (prob * (grad_probs[index, key, head] - deltas[row])).astype(jnp.bfloat16)
    return prob.astype(jnp.bfloat16), score_low


def back_kernel(
    table, keys, masked, grad_probs, mine, r_one, r_two, s_far, s_other,
    prob_out, score_out, logs, deltas, one_out, two_out,
    accums, notes,
):
    side = SIDE
    rank = table[RANK] % 4
    swapped = (rank == 1) | (rank == 2)
    far = [jnp.where(swapped, s_other[i], s_far[i]) for i in range(3)]
    other = [jnp.where(swapped, s_far[i], s_other[i]) for i in range(3)]
    s_one = read_notes(r_one, notes.at[0])
    s_two = read_notes(r_two, notes.at[1])
    s_mine = [mine[i] for i in range(3)]

    def part(stats, start):
        return [each[start : start + side] for each in stats]

    groups = (
        (part(s_mine, 0), part(s_one, side), far),
        (part(s_mine, side), part(s_one, 0), part(s_two, side)),
        (part(s_mine, 2 * side), part(s_two, 0), other),
    )
    for index, sources in enumerate(groups):
        highest, total, moment = joined_stats(sources)
        rows = slice(index * side, (index + 1) * side)
        total = jnp.where(total > 0, total, 1.0)
        logs[rows] = highest + jnp.log2(total)
        deltas[rows] = moment / total
    accums[...] = jnp.zeros_like(accums)
    for index, window in enumerate(FAR):
        for key in range(FR_DEV):
            active, _ = pair_of(table, window, key)

            @pl.when(active)
            def _():
                for head in range(MOVED):
                    prob_low, score_low = finish_pair(
                        window, index, key, head, masked, grad_probs, logs, deltas
                    )
                    prob_out[index, key, head] = prob_low
                    score_out[index, key, head] = score_low
                    accums[index // FR_DEV, rows_of(index % FR_DEV), column_of(head)] += dot(
                        score_low, keys[rows_of(key), column_of(head)], TN
                    )

    one_out[...] = (accums[0] * SCALE).astype(one_out.dtype)
    two_out[...] = (accums[1] * SCALE).astype(two_out.dtype)


def home_kernel(
    table, queries, grad_out, keys, f_one, f_two, masked, grad_probs, prob_in, score_in,
    logs, deltas,
    query_out, key_out, value_out,
    key_accum, value_accum,
):
    query_out[...] = jnp.zeros_like(query_out)
    key_accum[...] = jnp.zeros_like(key_accum)
    value_accum[...] = jnp.zeros_like(value_accum)
    for window in range(WINDOW):
        rows = rows_of(window % FR_DEV)
        near = window // FR_DEV == 1
        sent = f_one if window < FR_DEV else f_two
        for key in range(FR_DEV):
            active, _ = pair_of(table, window, key)

            @pl.when(active)
            def _():
                for head in range(MOVED):
                    column = column_of(head)
                    if near:
                        query = queries[rows, column]
                        grad = grad_out[rows, column]
                        prob_low, score_low = finish_pair(
                            window, window - FR_DEV, key, head, masked, grad_probs, logs, deltas
                        )
                        query_out[rows, column] += dot(
                            score_low, keys[rows_of(key), column], TN
                        )
                    else:
                        query = sent[0, rows, column]
                        grad = sent[1, rows, column]
                        prob_low = prob_in[FAR.index(window), key, head]
                        score_low = score_in[FAR.index(window), key, head]
                    key_accum[rows_of(key), column] += dot(score_low, query, NN)
                    value_accum[rows_of(key), column] += dot(prob_low, grad, NN)

    query_out[...] = query_out[...] * SCALE
    key_out[...] = (key_accum[...] * SCALE).astype(key_out.dtype)
    value_out[...] = value_accum[...].astype(value_out.dtype)


def both_ways(pairs):
    return [pair for i, j in pairs for pair in ((i, j), (j, i))]


def swap(one, two):
    count = lax.axis_size("frames")
    first = [(i, i + 1) for i in range(0, count - 1, 2)]
    second = [(i, i + 1) for i in range(1, count - 1, 2)]
    return (
        lax.ppermute(one, "frames", both_ways(first)),
        lax.ppermute(two, "frames", both_ways(second)),
    )


def swap_far(far, other):
    count = lax.axis_size("frames")
    near = [(i, i + 2) for i in range(count - 2) if i % 4 < 2]
    over = [(i, i + 2) for i in range(count - 2) if i % 4 >= 2]
    far = lax.ppermute(far, "frames", both_ways(near))
    other = lax.ppermute(other, "frames", both_ways(over)) if over else jnp.zeros_like(other)
    return far, other


def lookup(offsets, spatial):
    rank = lax.axis_index("frames")
    first = rank * FR_DEV
    frames = offsets.shape[0]
    around = ((REACH, REACH), (0, 0))
    shifts = lax.dynamic_slice_in_dim(jnp.pad(offsets, around), first, WINDOW, 0)
    blocks = lax.dynamic_slice_in_dim(
        jnp.pad(spatial, around + ((0, 0), (0, 0))), first, WINDOW, 0
    )
    ends = jnp.stack([first, rank, jnp.full_like(rank, frames)]).astype(jnp.int32)
    return jnp.concatenate([shifts.reshape(-1), blocks.reshape(-1), ends])


def call(kernel, name, scalars, arrays, outs, scratch, flops, space=pltpu.VMEM, out_space=pltpu.VMEM):
    arrays = [pltpu.with_memory_space_constraint(array, space) for array in arrays]
    return pl.pallas_call(
        kernel,
        out_shape=outs,
        in_specs=[pl.BlockSpec(memory_space=pltpu.SMEM)] * len(scalars)
        + [pl.BlockSpec(memory_space=space)] * len(arrays),
        out_specs=tuple(pl.BlockSpec(memory_space=out_space) for _ in outs),
        scratch_shapes=scratch,
        compiler_params=pltpu.CompilerParams(vmem_limit_bytes=16 << 20),
        cost_estimate=pl.CostEstimate(flops=flops, bytes_accessed=0, transcendentals=0),
        name=name,
    )(*scalars, *arrays)


def local(queries, keys, values, grad_out, offsets, spatial):
    width = queries.shape[1]
    heads = width // HD - MOVED

    def low(*shape):
        return pltpu.VMEM(shape, jnp.bfloat16)

    def full(*shape):
        return pltpu.VMEM(shape, jnp.float32)

    unit = 2 * FR_DEV * NSEL * TOK_FRAME * TOK_FRAME * HD
    rest = width - SPLIT
    (y_send,) = call(
        pack_queries_kernel, "pack_queries", (), (queries, grad_out),
        (low(2, ROWS, SPLIT),), [pltpu.SemaphoreType.DMA((2,))], unit, pltpu.HBM,
    )
    k_send, v_send = call(
        pack_keys_kernel, "pack_keys", (), (keys, values),
        (low(ROWS, rest), low(ROWS, rest)), [pltpu.SemaphoreType.DMA((2,))], unit, pltpu.HBM,
    )
    f_one, f_two = swap(y_send, y_send)
    k_one, k_two = swap(k_send, k_send)
    table = lookup(offsets, spatial)
    query, grad, key, value, bias, moved_bias = call(
        stage_kernel, "stage", (table,), (queries, grad_out, keys, values),
        (low(ROWS, width),) * 4
        + (full(FR_DEV, SLOTS, TOK_FRAME), full(WINDOW, FR_DEV, TOK_FRAME, TOK_FRAME)),
        [pltpu.SemaphoreType.DMA((4,))], unit, pltpu.HBM,
    )
    near_grid = (FR_DEV, FR_DEV, MOVED, TOK_FRAME, TOK_FRAME)
    far_grid = (len(FAR), FR_DEV, MOVED, TOK_FRAME, TOK_FRAME)
    near_masked, near_grads, own_stats = call(
        own_stats_kernel, "own_stats", (table,), (query, grad, key, value, moved_bias),
        (full(*near_grid), full(*near_grid), full(3, SIDE, TOK_FRAME)),
        [full(FR_DEV, 3, SIDE, TOK_FRAME)], MOVED * unit,
    )
    near_scores, rest_grads = call(
        own_scores_kernel, "own_scores", (), (query, grad, key, value, bias),
        (full(heads, FR_DEV, TOK_FRAME, TOK_FRAME),) * 2, [], heads * unit // 2,
    )
    f_two, f_one, own_stats, near_scores = lax.optimization_barrier(
        (f_two, f_one, own_stats, near_scores)
    )
    note = full(2 * NOTES, TOK_FRAME)
    masked, grad_probs, mine, n_one, n_two, s_far, s_other = call(
        stats_kernel, "stats", (table,), (key, value, moved_bias, own_stats, f_one, f_two),
        (full(*far_grid), full(*far_grid), full(3, 3 * SIDE, TOK_FRAME), note, note)
        + (full(3, SIDE, TOK_FRAME),) * 2,
        [full(FR_DEV, 3, 2 * SIDE, TOK_FRAME)], 2 * MOVED * unit,
    )
    s_far, s_other = swap_far(s_far, s_other)
    v_send, mine = lax.optimization_barrier((v_send, mine))
    v_one, v_two = swap(v_send, v_send)
    k_two, k_one, s_far, s_other = lax.optimization_barrier((k_two, k_one, s_far, s_other))
    windows = low(DEPTH, 3 * ROWS, HD)
    accums = full(DEPTH, 3 * ROWS, HD)
    pairs = low(heads, FR_DEV, SLOTS, TOK_FRAME)
    chosen, prob_low, gv_own, gv_one, gv_two = call(
        values_kernel, "values_part", (table,),
        (query, grad, key, bias, near_scores, k_one, k_two, n_one, n_two),
        (low(heads, FR_DEV, SLOTS, HD), pairs, full(ROWS, rest))
        + (low(ROWS + NOTES, rest),) * 2,
        [windows, accums], 2 * heads * unit,
    )
    rv_one, rv_two = swap(gv_one, gv_two)
    score_low, gk_own, gk_one, gk_two = call(
        keys_kernel, "keys_part", (table,),
        (query, grad, value, rest_grads, prob_low, v_one, v_two),
        (pairs, full(ROWS, rest), low(ROWS, rest), low(ROWS, rest)),
        [windows, low(DEPTH, FR_DEV, SLOTS - TOK_FRAME, HD), accums], 2 * heads * unit,
    )
    rk_one, rk_two = swap(gk_one, gk_two)
    gq_rest, gv_own, gk_own = call(
        rest_kernel, "rest", (),
        (query, grad, chosen, prob_low, score_low, gv_own, gk_own),
        (low(ROWS, rest), full(ROWS, rest), full(ROWS, rest)), [], heads * unit,
    )
    rv_one, rv_two, gv_own = lax.optimization_barrier((rv_one, rv_two, gv_own))
    y_prob, y_score, logs, deltas, gq_one, gq_two = call(
        back_kernel, "back", (table,),
        (key, masked, grad_probs, mine, rv_one, rv_two, s_far, s_other),
        (low(*far_grid), low(*far_grid)) + (full(3 * SIDE, TOK_FRAME),) * 2
        + (low(ROWS, SPLIT),) * 2,
        [full(2, ROWS, SPLIT), full(2, 2 * NOTES, TOK_FRAME)], MOVED * unit,
    )
    rq_one, rq_two = swap(gq_one, gq_two)
    gq_near, gk_near, gv_near = call(
        home_kernel, "home", (table,),
        (query, grad, key, f_one, f_two, near_masked, near_grads, y_prob, y_score, logs, deltas),
        (full(ROWS, SPLIT), low(ROWS, SPLIT), low(ROWS, SPLIT)),
        [full(ROWS, SPLIT), full(ROWS, SPLIT)], 3 * MOVED * unit,
    )
    grad_values = jnp.concatenate([gv_near, joined(gv_own, rv_one[:ROWS], rv_two[:ROWS])], 1)
    moved, kept = slice(0, SPLIT), slice(SPLIT, width)
    result = (pltpu.HBM((ROWS, width), jnp.bfloat16),)
    (grad_keys,) = call(
        functools.partial(finish_kernel, (moved, kept)), "last_keys", (),
        (gk_near, gk_own, rk_one, rk_two), result,
        [low(ROWS, rest), pltpu.SemaphoreType.DMA((2,))], unit, pltpu.VMEM, pltpu.HBM,
    )
    grad_keys, gq_near = lax.optimization_barrier((grad_keys, gq_near))
    (grad_queries,) = call(
        functools.partial(finish_kernel, (kept, moved)), "last_queries", (),
        (gq_rest, gq_near, rq_one, rq_two), result,
        [low(ROWS, SPLIT), pltpu.SemaphoreType.DMA((2,))], unit, pltpu.VMEM, pltpu.HBM,
    )
    return grad_queries, grad_keys, grad_values


def solution(mesh):
    rows = P(("clips", "frames"), "heads")
    return jax.shard_map(
        local,
        mesh=mesh,
        in_specs=(rows, rows, rows, rows, P("clips", None), P("clips", None, None, None)),
        out_specs=(rows, rows, rows),
        check_vma=False,
    )
```
